32 devices in a mesh: lat: 4 (over x, core), lon: 8 (over z, y).
Axes of the slice: x: 2, y: 2, z: 4, core: 2. Of those that a mesh axis runs over, the one named last changes fastest.
Arguments:
- ensemble: float32 [48, 384, 4, 128], P('lat', 'lon'), may hold values from -6 to 6
- grad_increment: float32 [48, 384, 128], P('lat', 'lon'), may hold values from -6 to 6
- normalization: float32 [48, 384], P('lat', 'lon'), may hold values from 12 to 48
- lon_diffusion: float32 [48, 384], P('lat', 'lon'), may hold values from 1152 to 4608
- lat_diffusion: float32 [48, 384], P('lat', 'lon'), may hold values from 288 to 1152
- vert_diag: float32 [128], replicated, may hold values from 1 to 2
- vert_sub: float32 [127], replicated, may hold values from -0.8 to -0.3
Outputs:
- grad_alpha: float32 [48, 384, 4, 128], P('lat', 'lon')
The draws below stay inside these ranges and needn't reach their ends.
All inputs are finite; a program needn't handle non-finite values.
Results may differ from the reference program's by a relative error of at most 0.0003.
Values sent between devices are 32-bit elements; how exact they have to be, the bound alone decides.
No kernel may reach another device: no remote copies, remote signals or barrier semaphores. Data moves between devices by JAX's collectives and lax.ppermute only.
A program may use at most 64 MiB of HBM per device.

```python
import math
import jax
import jax.numpy as jnp
from jax import lax

LEV = 128
MEMB = 4
NLAT = 48
NLON = 384


def steps_of(stream_key, shape, shards, low, largest):
    def one(position, shards_of):
        heights = jax.random.uniform(jax.random.fold_in(jax.random.fold_in(stream_key, 6), position), (shards_of,), jnp.float32, low / len(shards), largest / len(shards))
        return jnp.repeat(jnp.exp(heights), shape[position] // shards_of).reshape((-1,) + (1,) * (len(shape) - position - 1))

    factor_of = one(*shards[0])
    for cut in shards[1:]:
        factor_of = factor_of * one(*cut)
    return factor_of


def bell_draw(key, dims, deviation, reach, split=(), kind=jnp.bfloat16):
    values = deviation * jax.random.normal(key, dims, jnp.float32)
    if split:
        values = values * steps_of(key, dims, split, -0.22, 0.18)
    return jnp.clip(values, -reach, reach).astype(kind)


def setup_inputs(seed: int = 0) -> dict:
    seeds = jax.random.split(jax.random.key(seed), 8)
    ensemble = bell_draw(seeds[0], (NLAT, NLON, MEMB, LEV), 1.0, 6.0, ((0, 4), (1, 8)), jnp.float32)
    grad_increment = bell_draw(seeds[1], (NLAT, NLON, LEV), 1.0, 6.0, ((0, 4), (1, 8)), jnp.float32)
    normalization = jnp.clip(jnp.exp(math.log(48.0) - 1.3862944 * jax.random.uniform(seeds[2], (NLAT, NLON), jnp.float32) ** steps_of(seeds[2], (NLAT, NLON), ((0, 4), (1, 8)), -0.2, 0.2)), 12.0, 48.0)
    lon_diffusion = jnp.clip(jnp.exp(math.log(4608.0) - 1.3862944 * jax.random.uniform(seeds[3], (NLAT, NLON), jnp.float32) ** steps_of(seeds[3], (NLAT, NLON), ((0, 4), (1, 8)), -0.2, 0.2)), 1152.0, 4608.0)
    lat_diffusion = jnp.clip(jnp.exp(math.log(1152.0) - 1.3862944 * jax.random.uniform(seeds[4], (NLAT, NLON), jnp.float32) ** steps_of(seeds[4], (NLAT, NLON), ((0, 4), (1, 8)), -0.2, 0.2)), 288.0, 1152.0)
    vert_diag = jnp.clip(jax.random.uniform(seeds[5], (LEV,), jnp.float32, 1.0, 2.0), 1.0, 2.0)
    vert_sub = jnp.clip(jax.random.uniform(seeds[6], (LEV - 1,), jnp.float32, -0.8, -0.3), -0.8, -0.3)
    return dict(ensemble=ensemble, grad_increment=grad_increment, normalization=normalization, lon_diffusion=lon_diffusion, lat_diffusion=lat_diffusion, vert_diag=vert_diag, vert_sub=vert_sub)


HIGHEST = lax.Precision.HIGHEST

def thomas_solve(diagonal, upper_band, rhs_vals):
    lower_band = jnp.concatenate([jnp.zeros_like(upper_band[:1]), upper_band[:-1]], axis=0)

    def forward(carry, item):
        ratio_prev, value_prev = carry
        diag_now, low_now, up_now, rhs_now = item
        pivot_val = diag_now - low_now * ratio_prev
        ratio_now = up_now / pivot_val
        value_now = (rhs_now - low_now[:, None] * value_prev) / pivot_val[:, None]
        return ((ratio_now, value_now), (ratio_now, value_now))
    start = (jnp.zeros_like(diagonal[0]), jnp.zeros_like(rhs_vals[0]))
    _, (ratio_all, value_all) = lax.scan(forward, start, (diagonal, lower_band, upper_band, rhs_vals))

    def backward(next_val, item):
        ratio_now, value_now = item
        result = value_now - ratio_now[:, None] * next_val
        return (result, result)
    _, solved = lax.scan(backward, jnp.zeros_like(rhs_vals[0]), (ratio_all, value_all), reverse=True)
    return solved

def longitude_solve(weighted, lon_diffusion):
    coeff_t = jnp.transpose(lon_diffusion)
    diagonal = 1.0 + jnp.roll(coeff_t, 1, axis=0) + coeff_t
    corner = -coeff_t[-1]
    gamma_val = -diagonal[0]
    diag_mod = jnp.concatenate([(diagonal[0] - gamma_val)[None], diagonal[1:-1], (diagonal[-1] - corner * corner / gamma_val)[None]], axis=0)
    upper_band = jnp.concatenate([-coeff_t[:-1], jnp.zeros_like(coeff_t[:1])], axis=0)
    rhs_t = jnp.transpose(weighted, (1, 0, 2))
    first_sol = thomas_solve(diag_mod, upper_band, rhs_t)
    middle = jnp.zeros((coeff_t.shape[0] - 2, coeff_t.shape[1], 1), coeff_t.dtype)
    update_vec = jnp.concatenate([gamma_val[None, :, None], middle, corner[None, :, None]], axis=0)
    second_sol = thomas_solve(diag_mod, upper_band, update_vec)
    factor_ratio = (corner / gamma_val)[:, None]
    dot_first = first_sol[0] + factor_ratio * first_sol[-1]
    dot_second = second_sol[0] + factor_ratio * second_sol[-1]
    solved = first_sol - second_sol * (dot_first / (1.0 + dot_second))[None]
    return jnp.transpose(solved, (1, 0, 2))

def latitude_solve(along_lon, lat_diffusion):
    lat_total = lat_diffusion.shape[0]
    row_ids = jnp.arange(lat_total).astype(lat_diffusion.dtype)
    latitude = -jnp.pi / 2 + (row_ids + 0.5) * jnp.pi / lat_total
    cosine = jnp.cos(latitude)
    edge_keep = (jnp.arange(lat_total) < lat_total - 1).astype(lat_diffusion.dtype)
    coeff = lat_diffusion * edge_keep[:, None]
    before = jnp.concatenate([jnp.zeros_like(coeff[:1]), coeff[:-1]], axis=0)
    diagonal = cosine[:, None] + before + coeff
    solved = thomas_solve(diagonal, -coeff, along_lon)
    return cosine[:, None, None] * solved

def vertical_inverse(vert_diag, vert_sub):
    factor = jnp.diag(vert_diag) + jnp.diag(vert_sub, -1)
    identity = jnp.eye(vert_diag.shape[0], dtype=vert_diag.dtype)
    return jax.scipy.linalg.cho_solve((factor, True), identity)

def reference(ensemble, grad_increment, normalization, lon_diffusion, lat_diffusion, vert_diag, vert_sub):
    lat_total, lon_total, members, levels = ensemble.shape
    weighted = normalization[:, :, None, None] * ensemble * grad_increment[:, :, None, :]
    weighted = weighted.reshape(lat_total, lon_total, members * levels)
    along_lon = longitude_solve(weighted, lon_diffusion)
    along_lat = latitude_solve(along_lon, lat_diffusion)
    along_lat = along_lat.reshape(lat_total, lon_total, members, levels)
    inverse = vertical_inverse(vert_diag, vert_sub)
    return jnp.einsum('abml,lk->abmk', along_lat, inverse, precision=HIGHEST)
```

```python
import functools
import math

import jax
import jax.numpy as jnp
from jax import lax
from jax.experimental import pallas as pl
from jax.experimental.pallas import tpu as pltpu
from jax.sharding import PartitionSpec as P

F32 = jnp.float32
LANES = 128
CHUNK = 16
PART = 64
VMEM_BYTES = 16 * 2**20


def call(kernel, outs, scratch=(), in_specs=None, out_specs=None, cost=None):
    specs = {k: v for k, v in (("in_specs", in_specs), ("out_specs", out_specs)) if v is not None}
    return pl.pallas_call(
        kernel,
        out_shape=outs,
        **specs,
        scratch_shapes=scratch,
        cost_estimate=cost,
        compiler_params=pltpu.CompilerParams(vmem_limit_bytes=VMEM_BYTES),
    )


def shape(*dims, dtype=F32):
    return jax.ShapeDtypeStruct(dims, dtype)


def lane_of(value, lane, rows):
    return jnp.broadcast_to(value[:, lane : lane + 1], (rows, LANES))


def split_rows(value):
    rest = value.shape[0] - 8
    fill = jnp.ones((8 - rest, value.shape[1]), F32)
    return value[:8], jnp.concatenate([value[8:], fill], axis=0)


def lon_sweep_kernel(ens_hbm, grad_hbm, norm_ref, diff_ref, part_ref, phi_ref, psi_ref, pay_ref, ens, grad, sem):
    rows, cells, _ = ens_hbm.shape
    cols = grad_hbm.shape[1]
    memb = cells // cols
    rest = rows - 8
    copies = []
    for c in range(cols // CHUNK):
        group = []
        for j in range(rows):
            g_rows, e_rows = pl.ds(c * CHUNK, CHUNK), pl.ds(c * CHUNK * memb, CHUNK * memb)
            group.append(pltpu.make_async_copy(grad_hbm.at[j, g_rows], grad.at[g_rows, j, :], sem.at[c, 0, j]))
            group.append(pltpu.make_async_copy(ens_hbm.at[j, e_rows], ens.at[e_rows, j, :], sem.at[c, 1, j]))
        copies.append(group)
    for group in copies:
        for copy in group:
            copy.start()
    step = split_rows(1.0 / diff_ref[...])
    norm = split_rows(norm_ref[...])
    zero, one = jnp.zeros((8, LANES), F32), jnp.ones((8, LANES), F32)
    u = [[zero] * memb for _ in range(2)]
    flux = [[zero] * memb for _ in range(2)]
    phi, phi_f, psi, psi_f = [one] * 2, [zero] * 2, [zero] * 2, [one] * 2
    for i in range(cols):
        if i % CHUNK == 0:
            for copy in copies[i // CHUNK]:
                copy.wait()
        for g in range(2):
            tile = slice(8 * g, 8 * g + 8)
            t = lane_of(step[g], i, 8)
            w = lane_of(norm[g], i, 8) * grad[i, tile, :]
            for m in range(memb):
                part_ref[i * memb + m, tile, :] = u[g][m]
                f = w * ens[i * memb + m, tile, :]
                flux[g][m] = flux[g][m] + (u[g][m] - f)
                u[g][m] = u[g][m] + t * flux[g][m]
            phi_ref[i, tile, :] = phi[g]
            psi_ref[i, tile, :] = psi[g]
            phi_f[g] = phi_f[g] + phi[g]
            psi_f[g] = psi_f[g] + psi[g]
            phi[g] = phi[g] + t * phi_f[g]
            psi[g] = psi[g] + t * psi_f[g]
    lanes = lax.broadcasted_iota(jnp.int32, (8, LANES), 1)
    half = memb * rows
    for g in range(2):
        b = 1.0 / psi[g]
        a, d = phi[g] * b, psi_f[g] * b
        first = 0 if g == 0 else 8 * memb
        size = 8 if g == 0 else rest
        for m in range(memb):
            pay_ref[first + m * size : first + (m + 1) * size, :] = (u[g][m] * b)[:size]
            pay_ref[half + first + m * size : half + first + (m + 1) * size, :] = (flux[g][m] - d * u[g][m])[:size]
        coef = jnp.where(lanes == 0, a, jnp.where(lanes == 1, b, d))
        for k in range(8 // size):
            row = 2 * half + 8 * g + k * size
            pay_ref[row : row + size, :] = coef[:size]


def lon_expand(tiles, memb, rest):
    return jnp.concatenate([tiles[:8]] * memb + [tiles[8:]] * (memb * rest // 8), axis=0)


def lon_parts(pay, half):
    coef = pay[2 * half :]
    a, b, d = (lane_of(coef, k, 16) for k in range(3))
    return pay[:half], pay[half : 2 * half], a, b, d


def lon_join(left, right, memb, rest):
    half = memb * (8 + rest)
    lh1, lh2, la, lb, ld = lon_parts(left, half)
    rh1, rh2, ra, rb, rd = lon_parts(right, half)
    inv = 1.0 / (ld + ra)
    ca, cb = lb * inv, rb * inv
    grow = functools.partial(lon_expand, memb=memb, rest=rest)
    total = lh2 + rh1
    s = total * grow(inv)
    h1 = lh1 + grow(ca) * total
    h2 = rh2 + grow(cb) * total
    return h1, h2, la - lb * ca, lb * cb, rd - rb * cb, s, ca, cb


def on_right(axis, level):
    return ((lax.axis_index(axis) >> level) & 1) == 1


def lon_merge_kernel(mine_ref, other_ref, pay_ref, back_ref, *, level, memb, rest):
    right = on_right("lon", level)
    mine, other = mine_ref[...], other_ref[...]
    h1, h2, a, b, d, s, ca, cb = lon_join(
        jnp.where(right, other, mine), jnp.where(right, mine, other), memb, rest
    )
    half = h1.shape[0]
    lanes = lax.broadcasted_iota(jnp.int32, a.shape, 1)
    pay_ref[:half, :] = h1
    pay_ref[half : 2 * half, :] = h2
    pay_ref[2 * half :, :] = jnp.where(lanes == 0, a, jnp.where(lanes == 1, b, d))
    back_ref[:half, :] = s
    back_ref[half : half + 16, :] = ca
    back_ref[half + 16 :, :] = cb


def times_inverse(rows, weights):
    high = rows.astype(jnp.bfloat16)
    low = (rows - high.astype(F32)).astype(jnp.bfloat16)
    out = jnp.dot(jnp.concatenate([high, low], axis=1), weights, preferred_element_type=F32)
    return out[:, :LANES] + out[:, LANES:]


def vertical_kernel(diag_ref, sub_ref, part_ref, y_ref, weights_ref, line, ratio, inverse, factor, *, stride, rows):
    levels = diag_ref.shape[1]
    line[...] = jnp.zeros_like(line)
    line[0:1, 0 : levels - 1] = sub_ref[...]
    row_ids = lax.broadcasted_iota(jnp.int32, (levels, levels), 0)
    col_ids = lax.broadcasted_iota(jnp.int32, (levels, levels), 1)
    diag = jnp.sum(jnp.where(row_ids == col_ids, diag_ref[...], 0.0), axis=1, keepdims=True)
    below = jnp.sum(jnp.where(row_ids == col_ids + 1, line[0:1, :], 0.0), axis=1, keepdims=True)
    inv = 1.0 / jnp.broadcast_to(diag, (levels, levels))
    inverse[...] = inv
    ratio[...] = -jnp.broadcast_to(below, (levels, levels)) * inv
    lane = lax.broadcasted_iota(jnp.int32, (1, levels), 1)
    row = jnp.zeros((1, levels), F32)
    for i in range(levels):
        row = jnp.where(lane == i, inverse[i : i + 1, :], row * ratio[i : i + 1, :])
        factor[i : i + 1, :] = row
    low_inv = factor[...]
    full = jnp.dot(low_inv.T, low_inv, preferred_element_type=F32, precision=lax.Precision.HIGHEST)
    high = full.astype(jnp.bfloat16)
    low = (full - high.astype(F32)).astype(jnp.bfloat16)
    weights_ref[0:levels, 0:levels] = high
    weights_ref[0:levels, levels:] = low
    weights_ref[levels:, 0:levels] = high
    weights_ref[levels:, levels:] = jnp.zeros_like(low)
    weights = weights_ref[...]
    cells = part_ref.shape[0]
    for c in range(0, cells, 16):
        y = times_inverse(part_ref[c : c + 16].reshape(256, LANES), weights)
        for k in range(16):
            y_ref[pl.ds(c + k, 8, stride=stride), :] = y[16 * k : 16 * k + 8]
            y_ref[pl.ds(8 * stride + c + k, rows - 8, stride=stride), :] = y[16 * k + 8 : 16 * k + rows]


def spread(out_ref, tiles, i, memb, stride, rows):
    for m in range(memb):
        out_ref[pl.ds(i * memb + m, 8, stride=stride), :] = tiles[0]
        out_ref[pl.ds(8 * stride + i * memb + m, rows - 8, stride=stride), :] = tiles[1][: rows - 8]


def expand_kernel(phi_ref, psi_ref, phi_out, psi_out, *, memb, stride, rows):
    for i in range(phi_ref.shape[0]):
        for src, dst in ((phi_ref, phi_out), (psi_ref, psi_out)):
            spread(dst, (src[i, 0:8, :], src[i, 8:16, :]), i, memb, stride, rows)


def lat_coef_kernel(diff_ref, step_out, phi_out, psi_out, coef_out, small_out, cos_out, *, memb, stride, bands):
    rows, cols = diff_ref.shape
    cells = cols * memb
    band = lax.axis_index("lat")
    row_ids = lax.broadcasted_iota(jnp.int32, (rows, cols), 0)
    last = jnp.logical_and(row_ids == rows - 1, band == bands - 1)
    step = split_rows(jnp.where(last, 0.0, 1.0 / diff_ref[...]))
    for i in range(cols):
        spread(step_out, [lane_of(s, i, 8) for s in step], i, memb, stride, rows)
    tile_ids = lax.broadcasted_iota(jnp.int32, (16, LANES), 0) + band * rows
    cosine = jnp.cos(-jnp.pi / 2 + (tile_ids.astype(F32) + 0.5) * jnp.pi / (bands * rows))
    cos_out[...] = cosine
    acc = [jnp.zeros((8, LANES), F32) for _ in range(3)]
    lane = lax.broadcasted_iota(jnp.int32, (PART, LANES), 1)
    for c in range(0, cells, PART):
        phi = jnp.ones((PART, LANES), F32)
        psi = jnp.zeros((PART, LANES), F32)
        phi_f, psi_f = psi, phi
        for j in range(rows):
            cos_j = jnp.broadcast_to(cosine[j : j + 1, :], (PART, LANES))
            t = step_out[j * stride + c : j * stride + c + PART, :]
            now_phi, now_psi = cos_j * phi, cos_j * psi
            phi_out[j * cells + c : j * cells + c + PART, :] = now_phi
            psi_out[j * cells + c : j * cells + c + PART, :] = now_psi
            phi_f = phi_f + now_phi
            psi_f = psi_f + now_psi
            phi = phi + t * phi_f
            psi = psi + t * psi_f
        b = 1.0 / psi
        picked = lax.broadcasted_iota(jnp.int32, (PART, LANES), 0) + c == lane * memb
        for k, value in enumerate((phi * b, b, psi_f * b)):
            coef_out[k * cells + c : k * cells + c + PART, :] = value
            chosen = jnp.where(picked, value, 0.0)
            for r in range(0, PART, 8):
                acc[k] = acc[k] + chosen[r : r + 8]
    small_out[...] = pack_small([jnp.sum(a, axis=0, keepdims=True) for a in acc])


def pack_small(lines):
    tile = lax.broadcasted_iota(jnp.int32, (8, LANES), 0)
    out = jnp.zeros((8, LANES), F32)
    for k, line in enumerate(lines):
        out = jnp.where(tile == k, jnp.broadcast_to(line, (8, LANES)), out)
    return out


def lat_sweep_kernel(*refs, levels, memb, rest, stride):
    own_ref, mine_ref, other_ref = refs[:3]
    backs = refs[3 : 3 + levels - 1]
    (y_ref, phi_ref, psi_ref, weights_ref, step_ref, coef_ref, small_ref, cos_ref, q_ref, pay_ref, ends, tiles) = refs[
        3 + levels - 1 :
    ]
    rows = 8 + rest
    half = memb * rows
    grow = functools.partial(lon_expand, memb=memb, rest=rest)
    right = on_right("lon", levels - 1)
    mine, other = mine_ref[...], other_ref[...]
    h1, h2, a, b, d, s, ca, cb = lon_join(
        jnp.where(right, other, mine), jnp.where(right, mine, other), memb, rest
    )
    outer = -(h1 + h2) * grow(1.0 / (a + d - 2.0 * b))
    middle = grow(ca + cb) * outer - s
    u_in, u_out = jnp.where(right, middle, outer), jnp.where(right, outer, middle)
    for level in reversed(range(levels - 1)):
        back = backs[level]
        middle = grow(back[half : half + 16, :]) * u_in + grow(back[half + 16 :, :]) * u_out - back[:half, :]
        right = on_right("lon", level)
        u_in, u_out = jnp.where(right, middle, u_in), jnp.where(right, u_out, middle)
    oh1, _, oa, ob, _ = lon_parts(own_ref[...], half)
    f_in = grow(ob) * u_out - grow(oa) * u_in - oh1
    weights = weights_ref[...]
    ends[...] = times_inverse(jnp.concatenate([u_in, f_in], axis=0), weights)
    for k in range(2):
        for j in range(rows):
            if j < 8:
                value = ends[pl.ds(k * half + j, memb, stride=8), :]
            else:
                value = ends[pl.ds(k * half + 8 * memb + j - 8, memb, stride=rest), :]
            tiles[8 * (k * rows + j) : 8 * (k * rows + j) + 8, :] = jnp.concatenate([value] * (8 // memb), axis=0)
    cells = coef_ref.shape[0] // 3
    for c in range(0, cells, PART):
        v = jnp.zeros((PART, LANES), F32)
        flux = v
        for j in range(rows):
            at = slice(j * stride + c, j * stride + c + PART)
            u_tile = jnp.concatenate([tiles[8 * j : 8 * j + 8, :]] * (PART // 8), axis=0)
            f_tile = jnp.concatenate([tiles[8 * (rows + j) : 8 * (rows + j) + 8, :]] * (PART // 8), axis=0)
            u = y_ref[at, :] + phi_ref[at, :] * u_tile + psi_ref[at, :] * f_tile
            now = jnp.broadcast_to(cos_ref[j : j + 1, :], (PART, LANES)) * v
            q_ref[j * cells + c : j * cells + c + PART, :] = now
            flux = flux + (now - u)
            v = v + step_ref[at, :] * flux
        b = coef_ref[cells + c : cells + c + PART, :]
        d = coef_ref[2 * cells + c : 2 * cells + c + PART, :]
        pay_ref[c : c + PART, :] = v * b
        pay_ref[cells + c : cells + c + PART, :] = flux - d * v
    pay_ref[2 * cells :, :] = small_ref[...]


def unpack_small(tile, k, c, memb):
    row = lax.broadcasted_iota(jnp.int32, (PART, LANES), 0) + c
    lane = lax.broadcasted_iota(jnp.int32, (PART, LANES), 1) * memb
    mask = jnp.logical_and(row >= lane, row < lane + memb)
    line = jnp.broadcast_to(tile[k : k + 1, :], (PART, LANES))
    return jnp.broadcast_to(jnp.sum(jnp.where(mask, line, 0.0), axis=1, keepdims=True), (PART, LANES))


def lat_merge_kernel(mine_ref, coef_ref, other_ref, *outs, level, levels, memb):
    ready = level == levels - 2
    if ready:
        pay_ref, back_ref, end_ref = outs
    else:
        pay_ref, back_ref, next_ref = outs
    cells = coef_ref.shape[0] // 3
    right = on_right("lat", level)
    upper = on_right("lat", level + 1)
    small = other_ref[2 * cells :, :]
    acc = [jnp.zeros((8, LANES), F32) for _ in range(3)]
    for c in range(0, cells, PART):
        at = slice(c, c + PART)
        lo, mid, hi = (slice(k * cells + c, k * cells + c + PART) for k in range(3))
        mine = [mine_ref[lo, :], mine_ref[mid, :], coef_ref[lo, :], coef_ref[mid, :], coef_ref[hi, :]]
        other = [other_ref[lo, :], other_ref[mid, :]] + [unpack_small(small, k, c, memb) for k in range(3)]
        lh1, lh2, la, lb, ld = (jnp.where(right, o, m) for m, o in zip(mine, other))
        rh1, rh2, ra, rb, rd = (jnp.where(right, m, o) for m, o in zip(mine, other))
        inv = 1.0 / (ld + ra)
        ca, cb = lb * inv, rb * inv
        total = lh2 + rh1
        back_ref[lo, :] = total * inv
        back_ref[mid, :] = ca
        back_ref[hi, :] = cb
        h1, h2 = lh1 + ca * total, rh2 + cb * total
        a, b, d = la - lb * ca, lb * cb, rd - rb * cb
        picked = lax.broadcasted_iota(jnp.int32, (PART, LANES), 0) + c == lax.broadcasted_iota(
            jnp.int32, (PART, LANES), 1
        ) * memb
        if ready:
            free, tied = jnp.where(upper, d, a), jnp.where(upper, a, d)
            h_free, h_tied = jnp.where(upper, h2, h1), jnp.where(upper, h1, h2)
            free_inv = 1.0 / free
            lean = b * free_inv
            pay_ref[at, :] = h_tied + lean * h_free
            stiff = tied - b * lean
            end_ref[lo, :] = lean
            end_ref[mid, :] = h_free * free_inv
            end_ref[hi, :] = stiff
            values = (stiff,)
        else:
            pay_ref[lo, :] = h1
            pay_ref[mid, :] = h2
            values = (a, b, d)
            for k, value in enumerate(values):
                next_ref[k * cells + c : k * cells + c + PART, :] = value
        for k, value in enumerate(values):
            chosen = jnp.where(picked, value, 0.0)
            for r in range(0, PART, 8):
                acc[k] = acc[k] + chosen[r : r + 8]
    lines = [jnp.sum(x, axis=0, keepdims=True) for x in acc[: 1 if ready else 3]]
    pay_ref[cells * (1 if ready else 2) :, :] = pack_small(lines)


def finish_kernel(*refs, levels, memb):
    own_ref, coef_ref, mine_ref, other_ref, end_ref = refs[:5]
    backs = refs[5 : 5 + levels - 1]
    q_ref, phi_ref, psi_ref, out_hbm, values, fluxes, out, sem = refs[5 + levels - 1 :]
    cells = coef_ref.shape[0] // 3
    rows = q_ref.shape[0] // cells
    upper = on_right("lat", levels - 1)
    small = other_ref[cells:, :]
    for c in range(0, cells, PART):
        lo, mid, hi = (slice(k * cells + c, k * cells + c + PART) for k in range(3))
        stiff = end_ref[hi, :] + unpack_small(small, 0, c, memb)
        middle = -(mine_ref[lo, :] + other_ref[lo, :]) / stiff
        outer = end_ref[lo, :] * middle - end_ref[mid, :]
        u_in, u_out = jnp.where(upper, middle, outer), jnp.where(upper, outer, middle)
        for level in reversed(range(levels - 1)):
            back = backs[level]
            middle = back[mid, :] * u_in + back[hi, :] * u_out - back[lo, :]
            right = on_right("lat", level)
            u_in, u_out = jnp.where(right, middle, u_in), jnp.where(right, u_out, middle)
        values[lo, :] = u_in
        fluxes[lo, :] = coef_ref[mid, :] * u_out - coef_ref[lo, :] * u_in - own_ref[lo, :]
    copies = []
    for j in range(rows):
        for c in range(0, cells, PART):
            at = slice(j * cells + c, j * cells + c + PART)
            lo = slice(c, c + PART)
            out[at, :] = q_ref[at, :] + phi_ref[at, :] * values[lo, :] + psi_ref[at, :] * fluxes[lo, :]
        copy = pltpu.make_async_copy(out.at[pl.ds(j * cells, cells), :], out_hbm.at[j], sem.at[j])
        copy.start()
        copies.append(copy)
    for copy in copies:
        copy.wait()


def swapped(value, axis, mask):
    return lax.ppermute(value, axis, [(s, s ^ mask) for s in range(lax.axis_size(axis))])


def shards(ensemble, grad_increment, normalization, lon_diffusion, lat_diffusion, vert_diag, vert_sub):
    rows, cols, memb, lev = ensemble.shape
    bands, blocks = lax.axis_size("lat"), lax.axis_size("lon")
    lat_levels, lon_levels = int(math.log2(bands)), int(math.log2(blocks))
    assert lev == LANES and 8 < rows <= 16 and 8 % memb == 0 and cols <= LANES and cols % CHUNK == 0
    assert 2**lat_levels == bands and 2**lon_levels == blocks and lat_levels >= 2 and lon_levels >= 2
    rest, cells = rows - 8, cols * memb
    assert 8 % rest == 0 and memb * rest % 8 == 0 and cells % PART == 0
    stride = cells + 1
    spaced = -(-rows * stride // 8) * 8
    half = memb * rows
    any_spec = pl.BlockSpec(memory_space=pl.ANY)
    vmem_spec = pl.BlockSpec(memory_space=pltpu.VMEM)

    part, phi_t, psi_t, pay = call(
        lon_sweep_kernel,
        (shape(cells, 16, LANES), shape(cols, 16, LANES), shape(cols, 16, LANES), shape(2 * half + 16, LANES)),
        scratch=[
            pltpu.VMEM((cells, 16, LANES), F32),
            pltpu.VMEM((cols, 16, LANES), F32),
            pltpu.SemaphoreType.DMA((cols // CHUNK, 2, rows)),
        ],
        in_specs=[any_spec, any_spec, vmem_spec, vmem_spec],
        cost=cost(2),
    )(ensemble.reshape(rows, cells, lev), grad_increment, normalization, lon_diffusion)

    y, weights = call(
        functools.partial(vertical_kernel, stride=stride, rows=rows),
        (shape(spaced, LANES), shape(2 * LANES, 2 * LANES, dtype=jnp.bfloat16)),
        scratch=[pltpu.VMEM((8, LANES), F32)] + [pltpu.VMEM((LANES, LANES), F32)] * 3,
        cost=cost(2),
    )(vert_diag.reshape(1, lev), vert_sub.reshape(1, lev - 1), part)
    phi, psi = call(
        functools.partial(expand_kernel, memb=memb, stride=stride, rows=rows),
        (shape(spaced, LANES), shape(spaced, LANES)),
        cost=cost(1),
    )(phi_t, psi_t)
    step, lat_phi, lat_psi, coef, small, cosine = call(
        functools.partial(lat_coef_kernel, memb=memb, stride=stride, bands=bands),
        (
            shape(spaced, LANES),
            shape(rows * cells, LANES),
            shape(rows * cells, LANES),
            shape(3 * cells, LANES),
            shape(8, LANES),
            shape(16, LANES),
        ),
        cost=cost(1),
    )(lat_diffusion)

    own, backs = pay, []
    for level in range(lon_levels - 1):
        other = swapped(pay, "lon", 1 << level)
        pay, back = call(
            functools.partial(lon_merge_kernel, level=level, memb=memb, rest=rest),
            (shape(2 * half + 16, LANES), shape(half + 32, LANES)),
            cost=cost(1),
        )(pay, other)
        backs.append(back)
    other = swapped(pay, "lon", 3 << (lon_levels - 2))
    q, lat_pay = call(
        functools.partial(lat_sweep_kernel, levels=lon_levels, memb=memb, rest=rest, stride=stride),
        (shape(rows * cells, LANES), shape(2 * cells + 8, LANES)),
        scratch=[pltpu.VMEM((2 * half, LANES), F32), pltpu.VMEM((16 * rows, LANES), F32)],
        cost=cost(1),
    )(own, pay, other, *backs, y, phi, psi, weights, step, coef, small, cosine)

    pay, group, lat_backs = lat_pay, coef, []
    for level in range(lat_levels - 1):
        other = swapped(pay, "lat", 1 << level)
        ready = level == lat_levels - 2
        pay, back, group = call(
            functools.partial(lat_merge_kernel, level=level, levels=lat_levels, memb=memb),
            (shape((1 if ready else 2) * cells + 8, LANES), shape(3 * cells, LANES), shape(3 * cells, LANES)),
            cost=cost(1),
        )(pay, group, other)
        lat_backs.append(back)
    other = swapped(pay, "lat", 1 << (lat_levels - 1))
    out = call(
        functools.partial(finish_kernel, levels=lat_levels, memb=memb),
        shape(rows, cells, LANES),
        scratch=[
            pltpu.VMEM((cells, LANES), F32),
            pltpu.VMEM((cells, LANES), F32),
            pltpu.VMEM((rows * cells, LANES), F32),
            pltpu.SemaphoreType.DMA((rows,)),
        ],
        out_specs=any_spec,
        cost=cost(1),
    )(lat_pay, coef, pay, other, group, *lat_backs, q, lat_phi, lat_psi)
    return out.reshape(rows, cols, memb, lev)


def cost(microseconds):
    return pl.CostEstimate(flops=0, bytes_accessed=int(microseconds * 3e6), transcendentals=0)


def solution(mesh):
    in_specs = (
        P("lat", "lon", None, None),
        P("lat", "lon", None),
        P("lat", "lon"),
        P("lat", "lon"),
        P("lat", "lon"),
        P(),
        P(),
    )
    out_specs = P("lat", "lon", None, None)
    return jax.shard_map(shards, mesh=mesh, in_specs=in_specs, out_specs=out_specs, check_vma=False)
```

```python
import functools
import math

import jax
import jax.numpy as jnp
from jax import lax
from jax.experimental import pallas as pl
from jax.experimental.pallas import tpu as pltpu
from jax.sharding import PartitionSpec as P

F32 = jnp.float32
LANES = 128
CHUNK = 16
PART = 64
VMEM_BYTES = 16 * 2**20


def call(kernel, outs, scratch=(), in_specs=None, out_specs=None, cost=None):
    specs = {k: v for k, v in (("in_specs", in_specs), ("out_specs", out_specs)) if v is not None}
    return pl.pallas_call(
        kernel,
        out_shape=outs,
        **specs,
        scratch_shapes=scratch,
        cost_estimate=cost,
        compiler_params=pltpu.CompilerParams(vmem_limit_bytes=VMEM_BYTES),
    )


def shape(*dims, dtype=F32):
    return jax.ShapeDtypeStruct(dims, dtype)


def lane_of(value, lane, rows):
    return jnp.broadcast_to(value[:, lane : lane + 1], (rows, LANES))


def split_rows(value):
    rest = value.shape[0] - 8
    fill = jnp.ones((8 - rest, value.shape[1]), F32)
    return value[:8], jnp.concatenate([value[8:], fill], axis=0)


def lon_sweep_kernel(
    ens_hbm, grad_hbm, norm_hbm, diff_hbm, part_ref, phi_ref, psi_ref, pay_ref, ens, grad, norm_ref, diff_ref, sem, sem2
):
    rows, cells, _ = ens_hbm.shape
    cols = grad_hbm.shape[1]
    memb = cells // cols
    rest = rows - 8
    small = [
        pltpu.make_async_copy(diff_hbm, diff_ref, sem2.at[0]),
        pltpu.make_async_copy(norm_hbm, norm_ref, sem2.at[1]),
    ]
    for copy in small:
        copy.start()
    copies = []
    for c in range(cols // CHUNK):
        group = []
        for j in range(rows):
            g_rows, e_rows = pl.ds(c * CHUNK, CHUNK), pl.ds(c * CHUNK * memb, CHUNK * memb)
            group.append(pltpu.make_async_copy(grad_hbm.at[j, g_rows], grad.at[g_rows, j, :], sem.at[c, 0, j]))
            group.append(pltpu.make_async_copy(ens_hbm.at[j, e_rows], ens.at[e_rows, j, :], sem.at[c, 1, j]))
        copies.append(group)
    for group in copies:
        for copy in group:
            copy.start()
    for copy in small:
        copy.wait()
    step = split_rows(1.0 / diff_ref[...])
    norm = split_rows(norm_ref[...])
    zero, one = jnp.zeros((8, LANES), F32), jnp.ones((8, LANES), F32)
    u = [[zero] * memb for _ in range(2)]
    flux = [[zero] * memb for _ in range(2)]
    phi, phi_f, psi, psi_f = [one] * 2, [zero] * 2, [zero] * 2, [one] * 2
    for i in range(cols):
        if i % CHUNK == 0:
            for copy in copies[i // CHUNK]:
                copy.wait()
        for g in range(2):
            tile = slice(8 * g, 8 * g + 8)
            t = lane_of(step[g], i, 8)
            w = lane_of(norm[g], i, 8) * grad[i, tile, :]
            for m in range(memb):
                part_ref[i * memb + m, tile, :] = u[g][m]
                f = w * ens[i * memb + m, tile, :]
                flux[g][m] = flux[g][m] + (u[g][m] - f)
                u[g][m] = u[g][m] + t * flux[g][m]
            phi_ref[i, tile, :] = phi[g]
            psi_ref[i, tile, :] = psi[g]
            phi_f[g] = phi_f[g] + phi[g]
            psi_f[g] = psi_f[g] + psi[g]
            phi[g] = phi[g] + t * phi_f[g]
            psi[g] = psi[g] + t * psi_f[g]
    lanes = lax.broadcasted_iota(jnp.int32, (8, LANES), 1)
    half = memb * rows
    for g in range(2):
        b = 1.0 / psi[g]
        a, d = phi[g] * b, psi_f[g] * b
        first = 0 if g == 0 else 8 * memb
        size = 8 if g == 0 else rest
        for m in range(memb):
            pay_ref[first + m * size : first + (m + 1) * size, :] = (u[g][m] * b)[:size]
            pay_ref[half + first + m * size : half + first + (m + 1) * size, :] = (flux[g][m] - d * u[g][m])[:size]
        coef = jnp.where(lanes == 0, a, jnp.where(lanes == 1, b, d))
        for k in range(8 // size):
            row = 2 * half + 8 * g + k * size
            pay_ref[row : row + size, :] = coef[:size]


def lon_expand(tiles, memb, rest):
    return jnp.concatenate([tiles[:8]] * memb + [tiles[8:]] * (memb * rest // 8), axis=0)


def lon_parts(pay, half):
    coef = pay[2 * half :]
    a, b, d = (lane_of(coef, k, 16) for k in range(3))
    return pay[:half], pay[half : 2 * half], a, b, d


def lon_join(left, right, memb, rest):
    half = memb * (8 + rest)
    lh1, lh2, la, lb, ld = lon_parts(left, half)
    rh1, rh2, ra, rb, rd = lon_parts(right, half)
    inv = 1.0 / (ld + ra)
    ca, cb = lb * inv, rb * inv
    grow = functools.partial(lon_expand, memb=memb, rest=rest)
    total = lh2 + rh1
    s = total * grow(inv)
    h1 = lh1 + grow(ca) * total
    h2 = rh2 + grow(cb) * total
    return h1, h2, la - lb * ca, lb * cb, rd - rb * cb, s, ca, cb


def on_right(axis, level):
    return ((lax.axis_index(axis) >> level) & 1) == 1


def lon_merge_kernel(mine_ref, other_ref, pay_ref, back_ref, *, level, memb, rest):
    right = on_right("lon", level)
    mine, other = mine_ref[...], other_ref[...]
    h1, h2, a, b, d, s, ca, cb = lon_join(
        jnp.where(right, other, mine), jnp.where(right, mine, other), memb, rest
    )
    half = h1.shape[0]
    lanes = lax.broadcasted_iota(jnp.int32, a.shape, 1)
    pay_ref[:half, :] = h1
    pay_ref[half : 2 * half, :] = h2
    pay_ref[2 * half :, :] = jnp.where(lanes == 0, a, jnp.where(lanes == 1, b, d))
    back_ref[:half, :] = s
    back_ref[half : half + 16, :] = ca
    back_ref[half + 16 :, :] = cb


def times_inverse(rows, weights):
    high = rows.astype(jnp.bfloat16)
    low = (rows - high.astype(F32)).astype(jnp.bfloat16)
    out = jnp.dot(jnp.concatenate([high, low], axis=1), weights, preferred_element_type=F32)
    return out[:, :LANES] + out[:, LANES:]


def vertical_kernel(diag_ref, sub_ref, part_ref, y_ref, weights_ref, line, ratio, inverse, factor, *, stride, rows):
    levels = diag_ref.shape[1]
    line[...] = jnp.zeros_like(line)
    line[0:1, 0 : levels - 1] = sub_ref[...]
    row_ids = lax.broadcasted_iota(jnp.int32, (levels, levels), 0)
    col_ids = lax.broadcasted_iota(jnp.int32, (levels, levels), 1)
    diag = jnp.sum(jnp.where(row_ids == col_ids, diag_ref[...], 0.0), axis=1, keepdims=True)
    below = jnp.sum(jnp.where(row_ids == col_ids + 1, line[0:1, :], 0.0), axis=1, keepdims=True)
    inv = 1.0 / jnp.broadcast_to(diag, (levels, levels))
    inverse[...] = inv
    ratio[...] = -jnp.broadcast_to(below, (levels, levels)) * inv
    lane = lax.broadcasted_iota(jnp.int32, (1, levels), 1)
    row = jnp.zeros((1, levels), F32)
    for i in range(levels):
        row = jnp.where(lane == i, inverse[i : i + 1, :], row * ratio[i : i + 1, :])
        factor[i : i + 1, :] = row
    low_inv = factor[...]
    full = jnp.dot(low_inv.T, low_inv, preferred_element_type=F32, precision=lax.Precision.HIGHEST)
    high = full.astype(jnp.bfloat16)
    low = (full - high.astype(F32)).astype(jnp.bfloat16)
    weights_ref[0:levels, 0:levels] = high
    weights_ref[0:levels, levels:] = low
    weights_ref[levels:, 0:levels] = high
    weights_ref[levels:, levels:] = jnp.zeros_like(low)
    weights = weights_ref[...]
    cells = part_ref.shape[0]
    for c in range(0, cells, 16):
        y = times_inverse(part_ref[c : c + 16].reshape(256, LANES), weights)
        for k in range(16):
            y_ref[pl.ds(c + k, 8, stride=stride), :] = y[16 * k : 16 * k + 8]
            y_ref[pl.ds(8 * stride + c + k, rows - 8, stride=stride), :] = y[16 * k + 8 : 16 * k + rows]


def spread(out_ref, tiles, i, memb, stride, rows):
    for m in range(memb):
        out_ref[pl.ds(i * memb + m, 8, stride=stride), :] = tiles[0]
        out_ref[pl.ds(8 * stride + i * memb + m, rows - 8, stride=stride), :] = tiles[1][: rows - 8]


def expand_kernel(phi_ref, psi_ref, phi_out, psi_out, *, memb, stride, rows):
    for i in range(phi_ref.shape[0]):
        for src, dst in ((phi_ref, phi_out), (psi_ref, psi_out)):
            spread(dst, (src[i, 0:8, :], src[i, 8:16, :]), i, memb, stride, rows)


def lat_coef_kernel(diff_ref, step_out, phi_out, psi_out, coef_out, small_out, cos_out, *, memb, stride, bands):
    rows, cols = diff_ref.shape
    cells = cols * memb
    band = lax.axis_index("lat")
    row_ids = lax.broadcasted_iota(jnp.int32, (rows, cols), 0)
    last = jnp.logical_and(row_ids == rows - 1, band == bands - 1)
    step = split_rows(jnp.where(last, 0.0, 1.0 / diff_ref[...]))
    for i in range(cols):
        spread(step_out, [lane_of(s, i, 8) for s in step], i, memb, stride, rows)
    tile_ids = lax.broadcasted_iota(jnp.int32, (16, LANES), 0) + band * rows
    cosine = jnp.cos(-jnp.pi / 2 + (tile_ids.astype(F32) + 0.5) * jnp.pi / (bands * rows))
    cos_out[...] = cosine
    acc = [jnp.zeros((8, LANES), F32) for _ in range(3)]
    lane = lax.broadcasted_iota(jnp.int32, (PART, LANES), 1)
    for c in range(0, cells, PART):
        phi = jnp.ones((PART, LANES), F32)
        psi = jnp.zeros((PART, LANES), F32)
        phi_f, psi_f = psi, phi
        for j in range(rows):
            cos_j = jnp.broadcast_to(cosine[j : j + 1, :], (PART, LANES))
            t = step_out[j * stride + c : j * stride + c + PART, :]
            now_phi, now_psi = cos_j * phi, cos_j * psi
            phi_out[j * cells + c : j * cells + c + PART, :] = now_phi
            psi_out[j * cells + c : j * cells + c + PART, :] = now_psi
            phi_f = phi_f + now_phi
            psi_f = psi_f + now_psi
            phi = phi + t * phi_f
            psi = psi + t * psi_f
        b = 1.0 / psi
        picked = lax.broadcasted_iota(jnp.int32, (PART, LANES), 0) + c == lane * memb
        for k, value in enumerate((phi * b, b, psi_f * b)):
            coef_out[k * cells + c : k * cells + c + PART, :] = value
            chosen = jnp.where(picked, value, 0.0)
            for r in range(0, PART, 8):
                acc[k] = acc[k] + chosen[r : r + 8]
    small_out[...] = pack_small([jnp.sum(a, axis=0, keepdims=True) for a in acc])


def pack_small(lines):
    tile = lax.broadcasted_iota(jnp.int32, (8, LANES), 0)
    out = jnp.zeros((8, LANES), F32)
    for k, line in enumerate(lines):
        out = jnp.where(tile == k, jnp.broadcast_to(line, (8, LANES)), out)
    return out


def lat_sweep_kernel(*refs, levels, memb, rest, stride):
    own_ref, mine_ref, other_ref = refs[:3]
    backs = refs[3 : 3 + levels - 1]
    (y_ref, phi_ref, psi_ref, weights_ref, step_ref, coef_ref, small_ref, cos_ref, q_ref, pay_ref, ends, tiles) = refs[
        3 + levels - 1 :
    ]
    rows = 8 + rest
    half = memb * rows
    grow = functools.partial(lon_expand, memb=memb, rest=rest)
    right = on_right("lon", levels - 1)
    mine, other = mine_ref[...], other_ref[...]
    h1, h2, a, b, d, s, ca, cb = lon_join(
        jnp.where(right, other, mine), jnp.where(right, mine, other), memb, rest
    )
    outer = -(h1 + h2) * grow(1.0 / (a + d - 2.0 * b))
    middle = grow(ca + cb) * outer - s
    u_in, u_out = jnp.where(right, middle, outer), jnp.where(right, outer, middle)
    for level in reversed(range(levels - 1)):
        back = backs[level]
        middle = grow(back[half : half + 16, :]) * u_in + grow(back[half + 16 :, :]) * u_out - back[:half, :]
        right = on_right("lon", level)
        u_in, u_out = jnp.where(right, middle, u_in), jnp.where(right, u_out, middle)
    oh1, _, oa, ob, _ = lon_parts(own_ref[...], half)
    f_in = grow(ob) * u_out - grow(oa) * u_in - oh1
    weights = weights_ref[...]
    ends[: 2 * half, :] = times_inverse(jnp.concatenate([u_in, f_in], axis=0), weights)
    for k in range(2):
        for j in range(rows):
            if j < 8:
                value = ends[pl.ds(k * half + j, memb, stride=8), :]
            else:
                value = ends[pl.ds(k * half + 8 * memb + j - 8, memb, stride=rest), :]
            tiles[8 * (k * rows + j) : 8 * (k * rows + j) + 8, :] = jnp.concatenate([value] * (8 // memb), axis=0)
    cells = coef_ref.shape[0] // 3
    for c in range(0, cells, PART):
        v = jnp.zeros((PART, LANES), F32)
        flux = v
        for j in range(rows):
            at = slice(j * stride + c, j * stride + c + PART)
            u_tile = jnp.concatenate([tiles[8 * j : 8 * j + 8, :]] * (PART // 8), axis=0)
            f_tile = jnp.concatenate([tiles[8 * (rows + j) : 8 * (rows + j) + 8, :]] * (PART // 8), axis=0)
            u = y_ref[at, :] + phi_ref[at, :] * u_tile + psi_ref[at, :] * f_tile
            now = jnp.broadcast_to(cos_ref[j : j + 1, :], (PART, LANES)) * v
            q_ref[j * cells + c : j * cells + c + PART, :] = now
            flux = flux + (now - u)
            v = v + step_ref[at, :] * flux
        b = coef_ref[cells + c : cells + c + PART, :]
        d = coef_ref[2 * cells + c : 2 * cells + c + PART, :]
        pay_ref[c : c + PART, :] = v * b
        pay_ref[cells + c : cells + c + PART, :] = flux - d * v
    pay_ref[2 * cells :, :] = small_ref[...]


def unpack_small(tile, k, c, memb):
    row = lax.broadcasted_iota(jnp.int32, (PART, LANES), 0) + c
    lane = lax.broadcasted_iota(jnp.int32, (PART, LANES), 1) * memb
    mask = jnp.logical_and(row >= lane, row < lane + memb)
    line = jnp.broadcast_to(tile[k : k + 1, :], (PART, LANES))
    return jnp.broadcast_to(jnp.sum(jnp.where(mask, line, 0.0), axis=1, keepdims=True), (PART, LANES))


def lat_merge_kernel(mine_ref, coef_ref, other_ref, *outs, level, levels, memb):
    ready = level == levels - 2
    if ready:
        pay_ref, back_ref, end_ref = outs
    else:
        pay_ref, back_ref, next_ref = outs
    cells = coef_ref.shape[0] // 3
    right = on_right("lat", level)
    upper = on_right("lat", level + 1)
    small = other_ref[2 * cells :, :]
    acc = [jnp.zeros((8, LANES), F32) for _ in range(3)]
    for c in range(0, cells, PART):
        at = slice(c, c + PART)
        lo, mid, hi = (slice(k * cells + c, k * cells + c + PART) for k in range(3))
        mine = [mine_ref[lo, :], mine_ref[mid, :], coef_ref[lo, :], coef_ref[mid, :], coef_ref[hi, :]]
        other = [other_ref[lo, :], other_ref[mid, :]] + [unpack_small(small, k, c, memb) for k in range(3)]
        lh1, lh2, la, lb, ld = (jnp.where(right, o, m) for m, o in zip(mine, other))
        rh1, rh2, ra, rb, rd = (jnp.where(right, m, o) for m, o in zip(mine, other))
        inv = 1.0 / (ld + ra)
        ca, cb = lb * inv, rb * inv
        total = lh2 + rh1
        back_ref[lo, :] = total * inv
        back_ref[mid, :] = ca
        back_ref[hi, :] = cb
        h1, h2 = lh1 + ca * total, rh2 + cb * total
        a, b, d = la - lb * ca, lb * cb, rd - rb * cb
        picked = lax.broadcasted_iota(jnp.int32, (PART, LANES), 0) + c == lax.broadcasted_iota(
            jnp.int32, (PART, LANES), 1
        ) * memb
        if ready:
            free, tied = jnp.where(upper, d, a), jnp.where(upper, a, d)
            h_free, h_tied = jnp.where(upper, h2, h1), jnp.where(upper, h1, h2)
            free_inv = 1.0 / free
            lean = b * free_inv
            pay_ref[at, :] = h_tied + lean * h_free
            stiff = tied - b * lean
            end_ref[lo, :] = lean
            end_ref[mid, :] = h_free * free_inv
            end_ref[hi, :] = stiff
            values = (stiff,)
        else:
            pay_ref[lo, :] = h1
            pay_ref[mid, :] = h2
            values = (a, b, d)
            for k, value in enumerate(values):
                next_ref[k * cells + c : k * cells + c + PART, :] = value
        for k, value in enumerate(values):
            chosen = jnp.where(picked, value, 0.0)
            for r in range(0, PART, 8):
                acc[k] = acc[k] + chosen[r : r + 8]
    lines = [jnp.sum(x, axis=0, keepdims=True) for x in acc[: 1 if ready else 3]]
    pay_ref[cells * (1 if ready else 2) :, :] = pack_small(lines)


def finish_kernel(*refs, levels, memb):
    own_ref, coef_ref, mine_ref, other_ref, end_ref = refs[:5]
    backs = refs[5 : 5 + levels - 1]
    q_ref, phi_ref, psi_ref, out_hbm, values, fluxes, out, sem = refs[5 + levels - 1 :]
    cells = coef_ref.shape[0] // 3
    rows = q_ref.shape[0] // cells
    upper = on_right("lat", levels - 1)
    small = other_ref[cells:, :]
    for c in range(0, cells, PART):
        lo, mid, hi = (slice(k * cells + c, k * cells + c + PART) for k in range(3))
        stiff = end_ref[hi, :] + unpack_small(small, 0, c, memb)
        middle = -(mine_ref[lo, :] + other_ref[lo, :]) / stiff
        outer = end_ref[lo, :] * middle - end_ref[mid, :]
        u_in, u_out = jnp.where(upper, middle, outer), jnp.where(upper, outer, middle)
        for level in reversed(range(levels - 1)):
            back = backs[level]
            middle = back[mid, :] * u_in + back[hi, :] * u_out - back[lo, :]
            right = on_right("lat", level)
            u_in, u_out = jnp.where(right, middle, u_in), jnp.where(right, u_out, middle)
        values[lo, :] = u_in
        fluxes[lo, :] = coef_ref[mid, :] * u_out - coef_ref[lo, :] * u_in - own_ref[lo, :]
    copies = []
    for j in range(rows):
        for c in range(0, cells, PART):
            at = slice(j * cells + c, j * cells + c + PART)
            lo = slice(c, c + PART)
            out[at, :] = q_ref[at, :] + phi_ref[at, :] * values[lo, :] + psi_ref[at, :] * fluxes[lo, :]
        copy = pltpu.make_async_copy(out.at[pl.ds(j * cells, cells), :], out_hbm.at[j], sem.at[j])
        copy.start()
        copies.append(copy)
    for copy in copies:
        copy.wait()


def swapped(value, axis, mask):
    return lax.ppermute(value, axis, [(s, s ^ mask) for s in range(lax.axis_size(axis))])


def shards(ensemble, grad_increment, normalization, lon_diffusion, lat_diffusion, vert_diag, vert_sub):
    rows, cols, memb, lev = ensemble.shape
    bands, blocks = lax.axis_size("lat"), lax.axis_size("lon")
    lat_levels, lon_levels = int(math.log2(bands)), int(math.log2(blocks))
    assert lev == LANES and 8 < rows <= 16 and 8 % memb == 0 and cols <= LANES and cols % CHUNK == 0
    assert 2**lat_levels == bands and 2**lon_levels == blocks and lat_levels >= 2 and lon_levels >= 2
    rest, cells = rows - 8, cols * memb
    assert 8 % rest == 0 and memb * rest % 8 == 0 and cells % PART == 0
    stride = cells + 1
    spaced = -(-(rows + 1) * stride // 8) * 8
    half = memb * rows
    hbm_spec = pl.BlockSpec(memory_space=pltpu.HBM)

    part, phi_t, psi_t, pay = call(
        lon_sweep_kernel,
        (shape(cells, 16, LANES), shape(cols, 16, LANES), shape(cols, 16, LANES), shape(2 * half + 16, LANES)),
        scratch=[
            pltpu.VMEM((cells, 16, LANES), F32),
            pltpu.VMEM((cols, 16, LANES), F32),
            pltpu.VMEM((rows, cols), F32),
            pltpu.VMEM((rows, cols), F32),
            pltpu.SemaphoreType.DMA((cols // CHUNK, 2, rows)),
            pltpu.SemaphoreType.DMA((2,)),
        ],
        in_specs=[hbm_spec] * 4,
        cost=cost(2),
    )(*(in_hbm(x) for x in (ensemble.reshape(rows, cells, lev), grad_increment, normalization, lon_diffusion)))

    y, weights = call(
        functools.partial(vertical_kernel, stride=stride, rows=rows),
        (shape(spaced, LANES), shape(2 * LANES, 2 * LANES, dtype=jnp.bfloat16)),
        scratch=[pltpu.VMEM((8, LANES), F32)] + [pltpu.VMEM((LANES, LANES), F32)] * 3,
        cost=cost(2),
    )(vert_diag.reshape(1, lev), vert_sub.reshape(1, lev - 1), part)
    phi, psi = call(
        functools.partial(expand_kernel, memb=memb, stride=stride, rows=rows),
        (shape(spaced, LANES), shape(spaced, LANES)),
        cost=cost(1),
    )(phi_t, psi_t)
    step, lat_phi, lat_psi, coef, small, cosine = call(
        functools.partial(lat_coef_kernel, memb=memb, stride=stride, bands=bands),
        (
            shape(spaced, LANES),
            shape(rows * cells, LANES),
            shape(rows * cells, LANES),
            shape(3 * cells, LANES),
            shape(8, LANES),
            shape(16, LANES),
        ),
        cost=cost(1),
    )(lat_diffusion)

    own, backs = pay, []
    for level in range(lon_levels - 1):
        other = swapped(pay, "lon", 1 << level)
        pay, back = call(
            functools.partial(lon_merge_kernel, level=level, memb=memb, rest=rest),
            (shape(2 * half + 16, LANES), shape(half + 32, LANES)),
            cost=cost(1),
        )(pay, other)
        backs.append(back)
    other = swapped(pay, "lon", 1 << (lon_levels - 1))
    q, lat_pay = call(
        functools.partial(lat_sweep_kernel, levels=lon_levels, memb=memb, rest=rest, stride=stride),
        (shape(rows * cells, LANES), shape(2 * cells + 8, LANES)),
        scratch=[pltpu.VMEM((2 * half + 8, LANES), F32), pltpu.VMEM((16 * rows, LANES), F32)],
        cost=cost(1),
    )(own, pay, other, *backs, y, phi, psi, weights, step, coef, small, cosine)

    pay, group, lat_backs = lat_pay, coef, []
    for level in range(lat_levels - 1):
        other = swapped(pay, "lat", 1 << level)
        ready = level == lat_levels - 2
        pay, back, group = call(
            functools.partial(lat_merge_kernel, level=level, levels=lat_levels, memb=memb),
            (shape((1 if ready else 2) * cells + 8, LANES), shape(3 * cells, LANES), shape(3 * cells, LANES)),
            cost=cost(1),
        )(pay, group, other)
        lat_backs.append(back)
    other = swapped(pay, "lat", 1 << (lat_levels - 1))
    out = call(
        functools.partial(finish_kernel, levels=lat_levels, memb=memb),
        shape(rows, cells, LANES),
        scratch=[
            pltpu.VMEM((cells, LANES), F32),
            pltpu.VMEM((cells, LANES), F32),
            pltpu.VMEM((rows * cells, LANES), F32),
            pltpu.SemaphoreType.DMA((rows,)),
        ],
        out_specs=hbm_spec,
        cost=cost(1),
    )(lat_pay, coef, pay, other, group, *lat_backs, q, lat_phi, lat_psi)
    return out.reshape(rows, cols, memb, lev)


def in_hbm(value):
    return pltpu.with_memory_space_constraint(value, pltpu.HBM)


def cost(microseconds):
    return pl.CostEstimate(flops=0, bytes_accessed=int(microseconds * 3e6), transcendentals=0)


def solution(mesh):
    in_specs = (
        P("lat", "lon", None, None),
        P("lat", "lon", None),
        P("lat", "lon"),
        P("lat", "lon"),
        P("lat", "lon"),
        P(),
        P(),
    )
    out_specs = P("lat", "lon", None, None)
    return jax.shard_map(shards, mesh=mesh, in_specs=in_specs, out_specs=out_specs, check_vma=False)
```

```python
import functools
import math

import jax
import jax.numpy as jnp
from jax import lax
from jax.experimental import pallas as pl
from jax.experimental.pallas import tpu as pltpu
from jax.sharding import PartitionSpec as P

F32 = jnp.float32
LANES = 128
CHUNK = 16
PART = 64
VMEM_BYTES = 16 * 2**20


def call(kernel, outs, scratch=(), in_specs=None, out_specs=None, cost=None):
    specs = {k: v for k, v in (("in_specs", in_specs), ("out_specs", out_specs)) if v is not None}
    return pl.pallas_call(
        kernel,
        out_shape=outs,
        **specs,
        scratch_shapes=scratch,
        cost_estimate=cost,
        compiler_params=pltpu.CompilerParams(vmem_limit_bytes=VMEM_BYTES),
    )


def shape(*dims, dtype=F32):
    return jax.ShapeDtypeStruct(dims, dtype)


def lane_of(value, lane, rows):
    return jnp.broadcast_to(value[:, lane : lane + 1], (rows, LANES))


def split_rows(value):
    rest = value.shape[0] - 8
    fill = jnp.ones((8 - rest, value.shape[1]), F32)
    return value[:8], jnp.concatenate([value[8:], fill], axis=0)


def lon_sweep_kernel(
    ens_hbm,
    grad_hbm,
    norm_hbm,
    diff_hbm,
    part_ref,
    phi_ref,
    psi_ref,
    pay_ref,
    ens,
    grad,
    norm_ref,
    diff_ref,
    step_b,
    norm_b,
    sem,
):
    rows, cells, _ = ens_hbm.shape
    cols = grad_hbm.shape[1]
    memb = cells // cols
    rest = rows - 8
    half = memb * rows
    chunks = cols // CHUNK
    first = pltpu.make_async_copy(diff_hbm, diff_ref, sem.at[2 * chunks])
    second = pltpu.make_async_copy(norm_hbm, norm_ref, sem.at[2 * chunks + 1])
    first.start()
    second.start()
    arrivals = []
    for c in range(chunks):
        g_rows, e_rows = pl.ds(c * CHUNK, CHUNK), pl.ds(c * CHUNK * memb, CHUNK * memb)
        for j in range(rows):
            pltpu.make_async_copy(grad_hbm.at[j, g_rows], grad.at[g_rows, j, :], sem.at[2 * c]).start()
            pltpu.make_async_copy(ens_hbm.at[j, e_rows], ens.at[e_rows, j, :], sem.at[2 * c + 1]).start()
        arrivals.append(
            (
                pltpu.make_async_copy(grad_hbm.at[:, g_rows], grad_hbm.at[:, g_rows], sem.at[2 * c]),
                pltpu.make_async_copy(ens_hbm.at[:, e_rows], ens_hbm.at[:, e_rows], sem.at[2 * c + 1]),
            )
        )
    zero, one = jnp.zeros((8, LANES), F32), jnp.ones((8, LANES), F32)
    tiles = [slice(0, 8), slice(8, 16)]

    first.wait()
    second.wait()
    step = split_rows(1.0 / diff_ref[...])
    norm = split_rows(norm_ref[...])
    phi, phi_f, psi, psi_f = [one] * 2, [zero] * 2, [zero] * 2, [one] * 2
    for i in range(cols):
        for g in range(2):
            t = lane_of(step[g], i, 8)
            step_b[i, tiles[g], :] = t
            norm_b[i, tiles[g], :] = lane_of(norm[g], i, 8)
            phi_ref[i, tiles[g], :] = phi[g]
            psi_ref[i, tiles[g], :] = psi[g]
            phi_f[g] = phi_f[g] + phi[g]
            psi_f[g] = psi_f[g] + psi[g]
            phi[g] = phi[g] + t * phi_f[g]
            psi[g] = psi[g] + t * psi_f[g]
    lanes = lax.broadcasted_iota(jnp.int32, (8, LANES), 1)
    ends = []
    for g in range(2):
        b = 1.0 / psi[g]
        a, d = phi[g] * b, psi_f[g] * b
        ends.append((b, d))
        size = 8 if g == 0 else rest
        coef = jnp.where(lanes == 0, a, jnp.where(lanes == 1, b, d))
        for k in range(8 // size):
            row = 2 * half + 8 * g + k * size
            pay_ref[row : row + size, :] = coef[:size]

    u = [[zero] * memb for _ in range(2)]
    flux = [[zero] * memb for _ in range(2)]
    for i in range(cols):
        if i % CHUNK == 0:
            for copy in arrivals[i // CHUNK]:
                copy.wait()
        for g in range(2):
            t = step_b[i, tiles[g], :]
            w = norm_b[i, tiles[g], :] * grad[i, tiles[g], :]
            for m in range(memb):
                part_ref[i * memb + m, tiles[g], :] = u[g][m]
                f = w * ens[i * memb + m, tiles[g], :]
                flux[g][m] = flux[g][m] + (u[g][m] - f)
                u[g][m] = u[g][m] + t * flux[g][m]
    for g in range(2):
        b, d = ends[g]
        start = 0 if g == 0 else 8 * memb
        size = 8 if g == 0 else rest
        for m in range(memb):
            at = start + m * size
            pay_ref[at : at + size, :] = (u[g][m] * b)[:size]
            pay_ref[half + at : half + at + size, :] = (flux[g][m] - d * u[g][m])[:size]


def lon_expand(tiles, memb, rest):
    return jnp.concatenate([tiles[:8]] * memb + [tiles[8:]] * (memb * rest // 8), axis=0)


def lon_parts(pay, half):
    coef = pay[2 * half :]
    a, b, d = (lane_of(coef, k, 16) for k in range(3))
    return pay[:half], pay[half : 2 * half], a, b, d


def lon_join(left, right, memb, rest):
    half = memb * (8 + rest)
    lh1, lh2, la, lb, ld = lon_parts(left, half)
    rh1, rh2, ra, rb, rd = lon_parts(right, half)
    inv = 1.0 / (ld + ra)
    ca, cb = lb * inv, rb * inv
    grow = functools.partial(lon_expand, memb=memb, rest=rest)
    total = lh2 + rh1
    s = total * grow(inv)
    h1 = lh1 + grow(ca) * total
    h2 = rh2 + grow(cb) * total
    return h1, h2, la - lb * ca, lb * cb, rd - rb * cb, s, ca, cb


def on_right(axis, level):
    return ((lax.axis_index(axis) >> level) & 1) == 1


def lon_merge_kernel(mine_ref, other_ref, pay_ref, back_ref, *, level, memb, rest):
    right = on_right("lon", level)
    mine, other = mine_ref[...], other_ref[...]
    h1, h2, a, b, d, s, ca, cb = lon_join(
        jnp.where(right, other, mine), jnp.where(right, mine, other), memb, rest
    )
    half = h1.shape[0]
    lanes = lax.broadcasted_iota(jnp.int32, a.shape, 1)
    pay_ref[:half, :] = h1
    pay_ref[half : 2 * half, :] = h2
    pay_ref[2 * half :, :] = jnp.where(lanes == 0, a, jnp.where(lanes == 1, b, d))
    back_ref[:half, :] = s
    back_ref[half : half + 16, :] = ca
    back_ref[half + 16 :, :] = cb


def times_inverse(rows, weights):
    high = rows.astype(jnp.bfloat16)
    low = (rows - high.astype(F32)).astype(jnp.bfloat16)
    out = jnp.dot(jnp.concatenate([high, low], axis=1), weights, preferred_element_type=F32)
    return out[:, :LANES] + out[:, LANES:]


def vertical_kernel(diag_ref, sub_ref, part_ref, y_ref, weights_ref, line, ratio, inverse, factor, *, stride, rows):
    levels = diag_ref.shape[1]
    line[...] = jnp.zeros_like(line)
    line[0:1, 0 : levels - 1] = sub_ref[...]
    row_ids = lax.broadcasted_iota(jnp.int32, (levels, levels), 0)
    col_ids = lax.broadcasted_iota(jnp.int32, (levels, levels), 1)
    diag = jnp.sum(jnp.where(row_ids == col_ids, diag_ref[...], 0.0), axis=1, keepdims=True)
    below = jnp.sum(jnp.where(row_ids == col_ids + 1, line[0:1, :], 0.0), axis=1, keepdims=True)
    inv = 1.0 / jnp.broadcast_to(diag, (levels, levels))
    inverse[...] = inv
    ratio[...] = -jnp.broadcast_to(below, (levels, levels)) * inv
    lane = lax.broadcasted_iota(jnp.int32, (1, levels), 1)
    row = jnp.zeros((1, levels), F32)
    for i in range(levels):
        row = jnp.where(lane == i, inverse[i : i + 1, :], row * ratio[i : i + 1, :])
        factor[i : i + 1, :] = row
    low_inv = factor[...]
    full = jnp.dot(low_inv.T, low_inv, preferred_element_type=F32, precision=lax.Precision.HIGHEST)
    high = full.astype(jnp.bfloat16)
    low = (full - high.astype(F32)).astype(jnp.bfloat16)
    weights_ref[0:levels, 0:levels] = high
    weights_ref[0:levels, levels:] = low
    weights_ref[levels:, 0:levels] = high
    weights_ref[levels:, levels:] = jnp.zeros_like(low)
    weights = weights_ref[...]
    cells = part_ref.shape[0]
    for c in range(0, cells, 16):
        y = times_inverse(part_ref[c : c + 16].reshape(256, LANES), weights)
        for k in range(16):
            y_ref[pl.ds(c + k, 8, stride=stride), :] = y[16 * k : 16 * k + 8]
            y_ref[pl.ds(8 * stride + c + k, rows - 8, stride=stride), :] = y[16 * k + 8 : 16 * k + rows]


def spread(out_ref, tiles, i, memb, stride, rows):
    for m in range(memb):
        out_ref[pl.ds(i * memb + m, 8, stride=stride), :] = tiles[0]
        out_ref[pl.ds(8 * stride + i * memb + m, rows - 8, stride=stride), :] = tiles[1][: rows - 8]


def expand_kernel(phi_ref, psi_ref, phi_out, psi_out, *, memb, stride, rows):
    for i in range(phi_ref.shape[0]):
        for src, dst in ((phi_ref, phi_out), (psi_ref, psi_out)):
            spread(dst, (src[i, 0:8, :], src[i, 8:16, :]), i, memb, stride, rows)


def lat_coef_kernel(diff_ref, step_out, phi_out, psi_out, coef_out, small_out, cos_out, *, memb, stride, bands):
    rows, cols = diff_ref.shape
    cells = cols * memb
    band = lax.axis_index("lat")
    row_ids = lax.broadcasted_iota(jnp.int32, (rows, cols), 0)
    last = jnp.logical_and(row_ids == rows - 1, band == bands - 1)
    step = split_rows(jnp.where(last, 0.0, 1.0 / diff_ref[...]))
    for i in range(cols):
        spread(step_out, [lane_of(s, i, 8) for s in step], i, memb, stride, rows)
    tile_ids = lax.broadcasted_iota(jnp.int32, (16, LANES), 0) + band * rows
    cosine = jnp.cos(-jnp.pi / 2 + (tile_ids.astype(F32) + 0.5) * jnp.pi / (bands * rows))
    cos_out[...] = cosine
    acc = [jnp.zeros((8, LANES), F32) for _ in range(3)]
    lane = lax.broadcasted_iota(jnp.int32, (PART, LANES), 1)
    for c in range(0, cells, PART):
        phi = jnp.ones((PART, LANES), F32)
        psi = jnp.zeros((PART, LANES), F32)
        phi_f, psi_f = psi, phi
        for j in range(rows):
            cos_j = jnp.broadcast_to(cosine[j : j + 1, :], (PART, LANES))
            t = step_out[j * stride + c : j * stride + c + PART, :]
            now_phi, now_psi = cos_j * phi, cos_j * psi
            phi_out[j * cells + c : j * cells + c + PART, :] = now_phi
            psi_out[j * cells + c : j * cells + c + PART, :] = now_psi
            phi_f = phi_f + now_phi
            psi_f = psi_f + now_psi
            phi = phi + t * phi_f
            psi = psi + t * psi_f
        b = 1.0 / psi
        picked = lax.broadcasted_iota(jnp.int32, (PART, LANES), 0) + c == lane * memb
        for k, value in enumerate((phi * b, b, psi_f * b)):
            coef_out[k * cells + c : k * cells + c + PART, :] = value
            chosen = jnp.where(picked, value, 0.0)
            for r in range(0, PART, 8):
                acc[k] = acc[k] + chosen[r : r + 8]
    small_out[...] = pack_small([jnp.sum(a, axis=0, keepdims=True) for a in acc])


def pack_small(lines):
    tile = lax.broadcasted_iota(jnp.int32, (8, LANES), 0)
    out = jnp.zeros((8, LANES), F32)
    for k, line in enumerate(lines):
        out = jnp.where(tile == k, jnp.broadcast_to(line, (8, LANES)), out)
    return out


def lat_sweep_kernel(*refs, levels, memb, rest, stride):
    own_ref, mine_ref, other_ref = refs[:3]
    backs = refs[3 : 3 + levels - 1]
    (y_ref, phi_ref, psi_ref, weights_ref, step_ref, coef_ref, small_ref, cos_ref, q_ref, pay_ref, ends, tiles) = refs[
        3 + levels - 1 :
    ]
    rows = 8 + rest
    half = memb * rows
    grow = functools.partial(lon_expand, memb=memb, rest=rest)
    right = on_right("lon", levels - 1)
    mine, other = mine_ref[...], other_ref[...]
    h1, h2, a, b, d, s, ca, cb = lon_join(
        jnp.where(right, other, mine), jnp.where(right, mine, other), memb, rest
    )
    outer = -(h1 + h2) * grow(1.0 / (a + d - 2.0 * b))
    middle = grow(ca + cb) * outer - s
    u_in, u_out = jnp.where(right, middle, outer), jnp.where(right, outer, middle)
    for level in reversed(range(levels - 1)):
        back = backs[level]
        middle = grow(back[half : half + 16, :]) * u_in + grow(back[half + 16 :, :]) * u_out - back[:half, :]
        right = on_right("lon", level)
        u_in, u_out = jnp.where(right, middle, u_in), jnp.where(right, u_out, middle)
    oh1, _, oa, ob, _ = lon_parts(own_ref[...], half)
    f_in = grow(ob) * u_out - grow(oa) * u_in - oh1
    weights = weights_ref[...]
    ends[: 2 * half, :] = times_inverse(jnp.concatenate([u_in, f_in], axis=0), weights)
    for k in range(2):
        for j in range(rows):
            if j < 8:
                value = ends[pl.ds(k * half + j, memb, stride=8), :]
            else:
                value = ends[pl.ds(k * half + 8 * memb + j - 8, memb, stride=rest), :]
            tiles[8 * (k * rows + j) : 8 * (k * rows + j) + 8, :] = jnp.concatenate([value] * (8 // memb), axis=0)
    cells = coef_ref.shape[0] // 3
    for c in range(0, cells, PART):
        v = jnp.zeros((PART, LANES), F32)
        flux = v
        for j in range(rows):
            at = slice(j * stride + c, j * stride + c + PART)
            u_tile = jnp.concatenate([tiles[8 * j : 8 * j + 8, :]] * (PART // 8), axis=0)
            f_tile = jnp.concatenate([tiles[8 * (rows + j) : 8 * (rows + j) + 8, :]] * (PART // 8), axis=0)
            u = y_ref[at, :] + phi_ref[at, :] * u_tile + psi_ref[at, :] * f_tile
            now = jnp.broadcast_to(cos_ref[j : j + 1, :], (PART, LANES)) * v
            q_ref[j * cells + c : j * cells + c + PART, :] = now
            flux = flux + (now - u)
            v = v + step_ref[at, :] * flux
        b = coef_ref[cells + c : cells + c + PART, :]
        d = coef_ref[2 * cells + c : 2 * cells + c + PART, :]
        pay_ref[c : c + PART, :] = v * b
        pay_ref[cells + c : cells + c + PART, :] = flux - d * v
    pay_ref[2 * cells :, :] = small_ref[...]


def unpack_small(tile, k, c, memb):
    row = lax.broadcasted_iota(jnp.int32, (PART, LANES), 0) + c
    lane = lax.broadcasted_iota(jnp.int32, (PART, LANES), 1) * memb
    mask = jnp.logical_and(row >= lane, row < lane + memb)
    line = jnp.broadcast_to(tile[k : k + 1, :], (PART, LANES))
    return jnp.broadcast_to(jnp.sum(jnp.where(mask, line, 0.0), axis=1, keepdims=True), (PART, LANES))


def lat_merge_kernel(mine_ref, coef_ref, other_ref, *outs, level, levels, memb):
    ready = level == levels - 2
    if ready:
        pay_ref, back_ref, end_ref = outs
    else:
        pay_ref, back_ref, next_ref = outs
    cells = coef_ref.shape[0] // 3
    right = on_right("lat", level)
    upper = on_right("lat", level + 1)
    small = other_ref[2 * cells :, :]
    acc = [jnp.zeros((8, LANES), F32) for _ in range(3)]
    for c in range(0, cells, PART):
        at = slice(c, c + PART)
        lo, mid, hi = (slice(k * cells + c, k * cells + c + PART) for k in range(3))
        mine = [mine_ref[lo, :], mine_ref[mid, :], coef_ref[lo, :], coef_ref[mid, :], coef_ref[hi, :]]
        other = [other_ref[lo, :], other_ref[mid, :]] + [unpack_small(small, k, c, memb) for k in range(3)]
        lh1, lh2, la, lb, ld = (jnp.where(right, o, m) for m, o in zip(mine, other))
        rh1, rh2, ra, rb, rd = (jnp.where(right, m, o) for m, o in zip(mine, other))
        inv = 1.0 / (ld + ra)
        ca, cb = lb * inv, rb * inv
        total = lh2 + rh1
        back_ref[lo, :] = total * inv
        back_ref[mid, :] = ca
        back_ref[hi, :] = cb
        h1, h2 = lh1 + ca * total, rh2 + cb * total
        a, b, d = la - lb * ca, lb * cb, rd - rb * cb
        picked = lax.broadcasted_iota(jnp.int32, (PART, LANES), 0) + c == lax.broadcasted_iota(
            jnp.int32, (PART, LANES), 1
        ) * memb
        if ready:
            free, tied = jnp.where(upper, d, a), jnp.where(upper, a, d)
            h_free, h_tied = jnp.where(upper, h2, h1), jnp.where(upper, h1, h2)
            free_inv = 1.0 / free
            lean = b * free_inv
            pay_ref[at, :] = h_tied + lean * h_free
            stiff = tied - b * lean
            end_ref[lo, :] = lean
            end_ref[mid, :] = h_free * free_inv
            end_ref[hi, :] = stiff
            values = (stiff,)
        else:
            pay_ref[lo, :] = h1
            pay_ref[mid, :] = h2
            values = (a, b, d)
            for k, value in enumerate(values):
                next_ref[k * cells + c : k * cells + c + PART, :] = value
        for k, value in enumerate(values):
            chosen = jnp.where(picked, value, 0.0)
            for r in range(0, PART, 8):
                acc[k] = acc[k] + chosen[r : r + 8]
    lines = [jnp.sum(x, axis=0, keepdims=True) for x in acc[: 1 if ready else 3]]
    pay_ref[cells * (1 if ready else 2) :, :] = pack_small(lines)


def finish_kernel(*refs, levels, memb):
    own_ref, coef_ref, mine_ref, other_ref, end_ref = refs[:5]
    backs = refs[5 : 5 + levels - 1]
    q_ref, phi_ref, psi_ref, out_hbm, out, sem = refs[5 + levels - 1 :]
    cells = coef_ref.shape[0] // 3
    rows = q_ref.shape[0] // cells
    upper = on_right("lat", levels - 1)
    small = other_ref[cells:, :]

    def chunk_copy(k):
        at = pl.ds(pl.multiple_of(k * PART, PART), PART)
        return pltpu.make_async_copy(out.at[:, at, :], out_hbm.at[:, at, :], sem.at[k])

    @pl.loop(0, cells // PART)
    def _(k):
        c = pl.multiple_of(k * PART, PART)
        lo, mid, hi = (pl.ds(pl.multiple_of(p * cells + c, PART), PART) for p in range(3))
        stiff = end_ref[hi, :] + unpack_small(small, 0, c, memb)
        middle = -(mine_ref[lo, :] + other_ref[lo, :]) / stiff
        outer = end_ref[lo, :] * middle - end_ref[mid, :]
        u_in, u_out = jnp.where(upper, middle, outer), jnp.where(upper, outer, middle)
        for level in reversed(range(levels - 1)):
            back = backs[level]
            middle = back[mid, :] * u_in + back[hi, :] * u_out - back[lo, :]
            right = on_right("lat", level)
            u_in, u_out = jnp.where(right, middle, u_in), jnp.where(right, u_out, middle)
        flux = coef_ref[mid, :] * u_out - coef_ref[lo, :] * u_in - own_ref[lo, :]
        for j in range(rows):
            at = pl.ds(pl.multiple_of(j * cells + c, PART), PART)
            out[j, lo, :] = q_ref[at, :] + phi_ref[at, :] * u_in + psi_ref[at, :] * flux
        chunk_copy(k).start()

    for k in range(cells // PART):
        chunk_copy(k).wait()


def swapped(value, axis, mask):
    return lax.ppermute(value, axis, [(s, s ^ mask) for s in range(lax.axis_size(axis))])


def shards(ensemble, grad_increment, normalization, lon_diffusion, lat_diffusion, vert_diag, vert_sub):
    rows, cols, memb, lev = ensemble.shape
    bands, blocks = lax.axis_size("lat"), lax.axis_size("lon")
    lat_levels, lon_levels = int(math.log2(bands)), int(math.log2(blocks))
    assert lev == LANES and 8 < rows <= 16 and 8 % memb == 0 and cols <= LANES and cols % CHUNK == 0
    assert 2**lat_levels == bands and 2**lon_levels == blocks and lat_levels >= 2 and lon_levels >= 2
    rest, cells = rows - 8, cols * memb
    assert 8 % rest == 0 and memb * rest % 8 == 0 and cells % PART == 0
    stride = cells + 1
    spaced = -(-(rows + 1) * stride // 8) * 8
    half = memb * rows
    hbm_spec = pl.BlockSpec(memory_space=pltpu.HBM)

    part, phi_t, psi_t, pay = call(
        lon_sweep_kernel,
        (shape(cells, 16, LANES), shape(cols, 16, LANES), shape(cols, 16, LANES), shape(2 * half + 16, LANES)),
        scratch=[
            pltpu.VMEM((cells, 16, LANES), F32),
            pltpu.VMEM((cols, 16, LANES), F32),
            pltpu.VMEM((rows, cols), F32),
            pltpu.VMEM((rows, cols), F32),
            pltpu.VMEM((cols, 16, LANES), F32),
            pltpu.VMEM((cols, 16, LANES), F32),
            pltpu.SemaphoreType.DMA((2 * (cols // CHUNK) + 2,)),
        ],
        in_specs=[hbm_spec] * 4,
        cost=cost(2),
    )(*(in_hbm(x) for x in (ensemble.reshape(rows, cells, lev), grad_increment, normalization, lon_diffusion)))

    own, backs = pay, []
    for level in range(lon_levels - 1):
        other = swapped(pay, "lon", 1 << level)
        if level == 0:
            phi, psi = call(
                functools.partial(expand_kernel, memb=memb, stride=stride, rows=rows),
                (shape(spaced, LANES), shape(spaced, LANES)),
                cost=cost(1),
            )(phi_t, psi_t)
            step, lat_phi, lat_psi, coef, small, cosine = call(
                functools.partial(lat_coef_kernel, memb=memb, stride=stride, bands=bands),
                (
                    shape(spaced, LANES),
                    shape(rows * cells, LANES),
                    shape(rows * cells, LANES),
                    shape(3 * cells, LANES),
                    shape(8, LANES),
                    shape(16, LANES),
                ),
                cost=cost(1),
            )(lat_diffusion)
            other, phi, psi, step, lat_phi, lat_psi, coef = lax.optimization_barrier(
                (other, phi, psi, step, lat_phi, lat_psi, coef)
            )
        elif level == 1:
            pay, part = lax.optimization_barrier((pay, part))
            y, weights = call(
                functools.partial(vertical_kernel, stride=stride, rows=rows),
                (shape(spaced, LANES), shape(2 * LANES, 2 * LANES, dtype=jnp.bfloat16)),
                scratch=[pltpu.VMEM((8, LANES), F32)] + [pltpu.VMEM((LANES, LANES), F32)] * 3,
                cost=cost(2),
            )(vert_diag.reshape(1, lev), vert_sub.reshape(1, lev - 1), part)
            other, y, weights = lax.optimization_barrier((other, y, weights))
        pay, back = call(
            functools.partial(lon_merge_kernel, level=level, memb=memb, rest=rest),
            (shape(2 * half + 16, LANES), shape(half + 32, LANES)),
            cost=cost(1),
        )(pay, other)
        backs.append(back)
    other = swapped(pay, "lon", 1 << (lon_levels - 1))
    q, lat_pay = call(
        functools.partial(lat_sweep_kernel, levels=lon_levels, memb=memb, rest=rest, stride=stride),
        (shape(rows * cells, LANES), shape(2 * cells + 8, LANES)),
        scratch=[pltpu.VMEM((2 * half + 8, LANES), F32), pltpu.VMEM((16 * rows, LANES), F32)],
        cost=cost(1),
    )(own, pay, other, *backs, y, phi, psi, weights, step, coef, small, cosine)

    pay, group, lat_backs = lat_pay, coef, []
    for level in range(lat_levels - 1):
        other = swapped(pay, "lat", 1 << level)
        ready = level == lat_levels - 2
        pay, back, group = call(
            functools.partial(lat_merge_kernel, level=level, levels=lat_levels, memb=memb),
            (shape((1 if ready else 2) * cells + 8, LANES), shape(3 * cells, LANES), shape(3 * cells, LANES)),
            cost=cost(1),
        )(pay, group, other)
        lat_backs.append(back)
    other = swapped(pay, "lat", 1 << (lat_levels - 1))
    out = call(
        functools.partial(finish_kernel, levels=lat_levels, memb=memb),
        shape(rows, cells, LANES),
        scratch=[
            pltpu.VMEM((rows, cells, LANES), F32),
            pltpu.SemaphoreType.DMA((cells // PART,)),
        ],
        out_specs=hbm_spec,
        cost=cost(1),
    )(lat_pay, coef, pay, other, group, *lat_backs, q, lat_phi, lat_psi)
    return out.reshape(rows, cols, memb, lev)


def in_hbm(value):
    return pltpu.with_memory_space_constraint(value, pltpu.HBM)


def cost(microseconds):
    return pl.CostEstimate(flops=0, bytes_accessed=int(microseconds * 3e6), transcendentals=0)


def solution(mesh):
    in_specs = (
        P("lat", "lon", None, None),
        P("lat", "lon", None),
        P("lat", "lon"),
        P("lat", "lon"),
        P("lat", "lon"),
        P(),
        P(),
    )
    out_specs = P("lat", "lon", None, None)
    return jax.shard_map(shards, mesh=mesh, in_specs=in_specs, out_specs=out_specs, check_vma=False)
```

```python
import functools
import math

import jax
import jax.numpy as jnp
from jax import lax
from jax.experimental import pallas as pl
from jax.experimental.pallas import tpu as pltpu
from jax.sharding import PartitionSpec as P

F32 = jnp.float32
LANES = 128
CHUNK = 16
PART = 64
VMEM_BYTES = 16 * 2**20
LOCAL_ROUND = 1


def call(kernel, outs, scratch=(), in_specs=None, out_specs=None, cost=None):
    specs = {k: v for k, v in (("in_specs", in_specs), ("out_specs", out_specs)) if v is not None}
    return pl.pallas_call(
        kernel,
        out_shape=outs,
        **specs,
        scratch_shapes=scratch,
        cost_estimate=cost,
        compiler_params=pltpu.CompilerParams(vmem_limit_bytes=VMEM_BYTES),
    )


def shape(*dims, dtype=F32):
    return jax.ShapeDtypeStruct(dims, dtype)


def lane_of(value, lane, rows):
    return jnp.broadcast_to(value[:, lane : lane + 1], (rows, LANES))


def split_rows(value):
    rest = value.shape[0] - 8
    fill = jnp.ones((8 - rest, value.shape[1]), F32)
    return value[:8], jnp.concatenate([value[8:], fill], axis=0)


def lon_sweep_kernel(
    ens_hbm,
    grad_hbm,
    norm_hbm,
    diff_hbm,
    part_ref,
    phi_ref,
    psi_ref,
    pay_ref,
    ens,
    grad,
    norm_ref,
    diff_ref,
    step_b,
    norm_b,
    sem,
):
    rows, cells, _ = ens_hbm.shape
    cols = grad_hbm.shape[1]
    memb = cells // cols
    rest = rows - 8
    half = memb * rows
    chunks = cols // CHUNK
    first = pltpu.make_async_copy(diff_hbm, diff_ref, sem.at[2 * chunks])
    second = pltpu.make_async_copy(norm_hbm, norm_ref, sem.at[2 * chunks + 1])
    first.start()
    second.start()
    arrivals = []
    for c in range(chunks):
        g_rows, e_rows = pl.ds(c * CHUNK, CHUNK), pl.ds(c * CHUNK * memb, CHUNK * memb)
        for j in range(rows):
            pltpu.make_async_copy(grad_hbm.at[j, g_rows], grad.at[g_rows, j, :], sem.at[2 * c]).start()
            pltpu.make_async_copy(ens_hbm.at[j, e_rows], ens.at[e_rows, j, :], sem.at[2 * c + 1]).start()
        arrivals.append(
            (
                pltpu.make_async_copy(grad_hbm.at[:, g_rows], grad_hbm.at[:, g_rows], sem.at[2 * c]),
                pltpu.make_async_copy(ens_hbm.at[:, e_rows], ens_hbm.at[:, e_rows], sem.at[2 * c + 1]),
            )
        )
    zero, one = jnp.zeros((8, LANES), F32), jnp.ones((8, LANES), F32)
    tiles = [slice(0, 8), slice(8, 16)]

    first.wait()
    second.wait()
    step = split_rows(1.0 / diff_ref[...])
    norm = split_rows(norm_ref[...])
    phi, phi_f, psi, psi_f = [one] * 2, [zero] * 2, [zero] * 2, [one] * 2
    for i in range(cols):
        for g in range(2):
            t = lane_of(step[g], i, 8)
            step_b[i, tiles[g], :] = t
            norm_b[i, tiles[g], :] = lane_of(norm[g], i, 8)
            phi_ref[i, tiles[g], :] = phi[g]
            psi_ref[i, tiles[g], :] = psi[g]
            phi_f[g] = phi_f[g] + phi[g]
            psi_f[g] = psi_f[g] + psi[g]
            phi[g] = phi[g] + t * phi_f[g]
            psi[g] = psi[g] + t * psi_f[g]
    lanes = lax.broadcasted_iota(jnp.int32, (8, LANES), 1)
    ends = []
    for g in range(2):
        b = 1.0 / psi[g]
        a, d = phi[g] * b, psi_f[g] * b
        ends.append((b, d))
        size = 8 if g == 0 else rest
        coef = jnp.where(lanes == 0, a, jnp.where(lanes == 1, b, d))
        for k in range(8 // size):
            row = 2 * half + 8 * g + k * size
            pay_ref[row : row + size, :] = coef[:size]

    u = [[zero] * memb for _ in range(2)]
    flux = [[zero] * memb for _ in range(2)]
    for i in range(cols):
        if i % CHUNK == 0:
            for copy in arrivals[i // CHUNK]:
                copy.wait()
        for g in range(2):
            t = step_b[i, tiles[g], :]
            w = norm_b[i, tiles[g], :] * grad[i, tiles[g], :]
            for m in range(memb):
                part_ref[i * memb + m, tiles[g], :] = u[g][m]
                f = w * ens[i * memb + m, tiles[g], :]
                flux[g][m] = flux[g][m] + (u[g][m] - f)
                u[g][m] = u[g][m] + t * flux[g][m]
    for g in range(2):
        b, d = ends[g]
        start = 0 if g == 0 else 8 * memb
        size = 8 if g == 0 else rest
        for m in range(memb):
            at = start + m * size
            pay_ref[at : at + size, :] = (u[g][m] * b)[:size]
            pay_ref[half + at : half + at + size, :] = (flux[g][m] - d * u[g][m])[:size]


def lon_expand(tiles, memb, rest):
    return jnp.concatenate([tiles[:8]] * memb + [tiles[8:]] * (memb * rest // 8), axis=0)


def lon_parts(pay, half):
    coef = pay[2 * half :]
    return (pay[:half], pay[half : 2 * half]) + tuple(lane_of(coef, k, 16) for k in range(3))


def lon_join(mine, other, right, memb, rest):
    lh1, lh2, la, lb, ld = (jnp.where(right, o, m) for m, o in zip(mine, other))
    rh1, rh2, ra, rb, rd = (jnp.where(right, m, o) for m, o in zip(mine, other))
    inv = 1.0 / (ld + ra)
    ca, cb = lb * inv, rb * inv
    grow = functools.partial(lon_expand, memb=memb, rest=rest)
    total = lh2 + rh1
    joined = (lh1 + grow(ca) * total, rh2 + grow(cb) * total, la - lb * ca, lb * cb, rd - rb * cb)
    return joined, (total * grow(inv), ca, cb)


def lon_join_round(pays, levels, memb, rest):
    half = memb * (8 + rest)
    groups = [lon_parts(p[...], half) for p in pays]
    backs = []
    for level in levels:
        right = on_right("lon", level)
        pairs = [lon_join(groups[k], groups[k + 1], right, memb, rest) for k in range(0, len(groups), 2)]
        groups = [joined for joined, _ in pairs]
        backs.append(pairs[0][1])
    return groups[0], backs


def on_right(axis, level):
    return ((lax.axis_index(axis) >> level) & 1) == 1


def lon_merge_kernel(*refs, levels, memb, rest):
    pays, (pay_ref, *back_refs) = refs[: 1 << len(levels)], refs[1 << len(levels) :]
    (h1, h2, a, b, d), backs = lon_join_round(pays, levels, memb, rest)
    half = h1.shape[0]
    lanes = lax.broadcasted_iota(jnp.int32, a.shape, 1)
    pay_ref[:half, :] = h1
    pay_ref[half : 2 * half, :] = h2
    pay_ref[2 * half :, :] = jnp.where(lanes == 0, a, jnp.where(lanes == 1, b, d))
    for back_ref, (s, ca, cb) in zip(back_refs, backs):
        back_ref[:half, :] = s
        back_ref[half : half + 16, :] = ca
        back_ref[half + 16 :, :] = cb


def times_inverse(rows, weights):
    high = rows.astype(jnp.bfloat16)
    low = (rows - high.astype(F32)).astype(jnp.bfloat16)
    out = jnp.dot(jnp.concatenate([high, low], axis=1), weights, preferred_element_type=F32)
    return out[:, :LANES] + out[:, LANES:]


def vertical_kernel(diag_ref, sub_ref, part_ref, y_ref, weights_ref, line, ratio, inverse, factor, *, stride, rows):
    levels = diag_ref.shape[1]
    line[...] = jnp.zeros_like(line)
    line[0:1, 0 : levels - 1] = sub_ref[...]
    row_ids = lax.broadcasted_iota(jnp.int32, (levels, levels), 0)
    col_ids = lax.broadcasted_iota(jnp.int32, (levels, levels), 1)
    diag = jnp.sum(jnp.where(row_ids == col_ids, diag_ref[...], 0.0), axis=1, keepdims=True)
    below = jnp.sum(jnp.where(row_ids == col_ids + 1, line[0:1, :], 0.0), axis=1, keepdims=True)
    inv = 1.0 / jnp.broadcast_to(diag, (levels, levels))
    inverse[...] = inv
    ratio[...] = -jnp.broadcast_to(below, (levels, levels)) * inv
    lane = lax.broadcasted_iota(jnp.int32, (1, levels), 1)
    row = jnp.zeros((1, levels), F32)
    for i in range(levels):
        row = jnp.where(lane == i, inverse[i : i + 1, :], row * ratio[i : i + 1, :])
        factor[i : i + 1, :] = row
    low_inv = factor[...]
    full = jnp.dot(low_inv.T, low_inv, preferred_element_type=F32, precision=lax.Precision.HIGHEST)
    high = full.astype(jnp.bfloat16)
    low = (full - high.astype(F32)).astype(jnp.bfloat16)
    weights_ref[0:levels, 0:levels] = high
    weights_ref[0:levels, levels:] = low
    weights_ref[levels:, 0:levels] = high
    weights_ref[levels:, levels:] = jnp.zeros_like(low)
    weights = weights_ref[...]
    cells = part_ref.shape[0]
    for c in range(0, cells, 16):
        y = times_inverse(part_ref[c : c + 16].reshape(256, LANES), weights)
        for k in range(16):
            y_ref[pl.ds(c + k, 8, stride=stride), :] = y[16 * k : 16 * k + 8]
            y_ref[pl.ds(8 * stride + c + k, rows - 8, stride=stride), :] = y[16 * k + 8 : 16 * k + rows]


def spread(out_ref, tiles, i, memb, stride, rows):
    for m in range(memb):
        out_ref[pl.ds(i * memb + m, 8, stride=stride), :] = tiles[0]
        out_ref[pl.ds(8 * stride + i * memb + m, rows - 8, stride=stride), :] = tiles[1][: rows - 8]


def expand_kernel(phi_ref, psi_ref, phi_out, psi_out, *, memb, stride, rows):
    for i in range(phi_ref.shape[0]):
        for src, dst in ((phi_ref, phi_out), (psi_ref, psi_out)):
            spread(dst, (src[i, 0:8, :], src[i, 8:16, :]), i, memb, stride, rows)


def lat_coef_kernel(diff_ref, step_out, phi_out, psi_out, coef_out, small_out, cos_out, *, memb, stride, bands):
    rows, cols = diff_ref.shape
    cells = cols * memb
    band = lax.axis_index("lat")
    row_ids = lax.broadcasted_iota(jnp.int32, (rows, cols), 0)
    last = jnp.logical_and(row_ids == rows - 1, band == bands - 1)
    step = split_rows(jnp.where(last, 0.0, 1.0 / diff_ref[...]))
    for i in range(cols):
        spread(step_out, [lane_of(s, i, 8) for s in step], i, memb, stride, rows)
    tile_ids = lax.broadcasted_iota(jnp.int32, (16, LANES), 0) + band * rows
    cosine = jnp.cos(-jnp.pi / 2 + (tile_ids.astype(F32) + 0.5) * jnp.pi / (bands * rows))
    cos_out[...] = cosine
    acc = [jnp.zeros((8, LANES), F32) for _ in range(3)]
    lane = lax.broadcasted_iota(jnp.int32, (PART, LANES), 1)
    for c in range(0, cells, PART):
        phi = jnp.ones((PART, LANES), F32)
        psi = jnp.zeros((PART, LANES), F32)
        phi_f, psi_f = psi, phi
        for j in range(rows):
            cos_j = jnp.broadcast_to(cosine[j : j + 1, :], (PART, LANES))
            t = step_out[j * stride + c : j * stride + c + PART, :]
            now_phi, now_psi = cos_j * phi, cos_j * psi
            phi_out[j * cells + c : j * cells + c + PART, :] = now_phi
            psi_out[j * cells + c : j * cells + c + PART, :] = now_psi
            phi_f = phi_f + now_phi
            psi_f = psi_f + now_psi
            phi = phi + t * phi_f
            psi = psi + t * psi_f
        b = 1.0 / psi
        picked = lax.broadcasted_iota(jnp.int32, (PART, LANES), 0) + c == lane * memb
        for k, value in enumerate((phi * b, b, psi_f * b)):
            coef_out[k * cells + c : k * cells + c + PART, :] = value
            chosen = jnp.where(picked, value, 0.0)
            for r in range(0, PART, 8):
                acc[k] = acc[k] + chosen[r : r + 8]
    small_out[...] = pack_small([jnp.sum(a, axis=0, keepdims=True) for a in acc])


def pack_small(lines):
    tile = lax.broadcasted_iota(jnp.int32, (8, LANES), 0)
    out = jnp.zeros((8, LANES), F32)
    for k, line in enumerate(lines):
        out = jnp.where(tile == k, jnp.broadcast_to(line, (8, LANES)), out)
    return out


def lat_sweep_kernel(*refs, levels, memb, rest, stride):
    count = 1 << len(levels)
    own_ref, pays, backs = refs[0], refs[1 : 1 + count], refs[1 + count : 1 + count + levels[0]]
    (y_ref, phi_ref, psi_ref, weights_ref, step_ref, coef_ref, small_ref, cos_ref, q_ref, pay_ref, ends, tiles) = refs[
        1 + count + levels[0] :
    ]
    rows = 8 + rest
    half = memb * rows
    grow = functools.partial(lon_expand, memb=memb, rest=rest)
    (h1, h2, a, b, d), last = lon_join_round(pays, levels, memb, rest)
    u_in = -(h1 + h2) * grow(1.0 / (a + d - 2.0 * b))
    u_out = u_in
    stored = [(back[:half, :], back[half : half + 16, :], back[half + 16 :, :]) for back in backs]
    for level, (s, ca, cb) in reversed(list(enumerate(stored + last))):
        middle = grow(ca) * u_in + grow(cb) * u_out - s
        right = on_right("lon", level)
        u_in, u_out = jnp.where(right, middle, u_in), jnp.where(right, u_out, middle)
    oh1, _, oa, ob, _ = lon_parts(own_ref[...], half)
    f_in = grow(ob) * u_out - grow(oa) * u_in - oh1
    weights = weights_ref[...]
    ends[: 2 * half, :] = times_inverse(jnp.concatenate([u_in, f_in], axis=0), weights)
    for k in range(2):
        for j in range(rows):
            if j < 8:
                value = ends[pl.ds(k * half + j, memb, stride=8), :]
            else:
                value = ends[pl.ds(k * half + 8 * memb + j - 8, memb, stride=rest), :]
            tiles[8 * (k * rows + j) : 8 * (k * rows + j) + 8, :] = jnp.concatenate([value] * (8 // memb), axis=0)
    cells = coef_ref.shape[0] // 3
    for c in range(0, cells, PART):
        v = jnp.zeros((PART, LANES), F32)
        flux = v
        for j in range(rows):
            at = slice(j * stride + c, j * stride + c + PART)
            u_tile = jnp.concatenate([tiles[8 * j : 8 * j + 8, :]] * (PART // 8), axis=0)
            f_tile = jnp.concatenate([tiles[8 * (rows + j) : 8 * (rows + j) + 8, :]] * (PART // 8), axis=0)
            u = y_ref[at, :] + phi_ref[at, :] * u_tile + psi_ref[at, :] * f_tile
            now = jnp.broadcast_to(cos_ref[j : j + 1, :], (PART, LANES)) * v
            q_ref[j * cells + c : j * cells + c + PART, :] = now
            flux = flux + (now - u)
            v = v + step_ref[at, :] * flux
        b = coef_ref[cells + c : cells + c + PART, :]
        d = coef_ref[2 * cells + c : 2 * cells + c + PART, :]
        pay_ref[c : c + PART, :] = v * b
        pay_ref[cells + c : cells + c + PART, :] = flux - d * v
    pay_ref[2 * cells :, :] = small_ref[...]


def unpack_small(tile, k, c, memb):
    row = lax.broadcasted_iota(jnp.int32, (PART, LANES), 0) + c
    lane = lax.broadcasted_iota(jnp.int32, (PART, LANES), 1) * memb
    mask = jnp.logical_and(row >= lane, row < lane + memb)
    line = jnp.broadcast_to(tile[k : k + 1, :], (PART, LANES))
    return jnp.broadcast_to(jnp.sum(jnp.where(mask, line, 0.0), axis=1, keepdims=True), (PART, LANES))


def lat_merge_kernel(mine_ref, coef_ref, other_ref, *outs, level, levels, memb):
    ready = level == levels - 2
    if ready:
        pay_ref, back_ref, end_ref = outs
    else:
        pay_ref, back_ref, next_ref = outs
    cells = coef_ref.shape[0] // 3
    right = on_right("lat", level)
    upper = on_right("lat", level + 1)
    small = other_ref[2 * cells :, :]
    acc = [jnp.zeros((8, LANES), F32) for _ in range(3)]
    for c in range(0, cells, PART):
        at = slice(c, c + PART)
        lo, mid, hi = (slice(k * cells + c, k * cells + c + PART) for k in range(3))
        mine = [mine_ref[lo, :], mine_ref[mid, :], coef_ref[lo, :], coef_ref[mid, :], coef_ref[hi, :]]
        other = [other_ref[lo, :], other_ref[mid, :]] + [unpack_small(small, k, c, memb) for k in range(3)]
        lh1, lh2, la, lb, ld = (jnp.where(right, o, m) for m, o in zip(mine, other))
        rh1, rh2, ra, rb, rd = (jnp.where(right, m, o) for m, o in zip(mine, other))
        inv = 1.0 / (ld + ra)
        ca, cb = lb * inv, rb * inv
        total = lh2 + rh1
        back_ref[lo, :] = total * inv
        back_ref[mid, :] = ca
        back_ref[hi, :] = cb
        h1, h2 = lh1 + ca * total, rh2 + cb * total
        a, b, d = la - lb * ca, lb * cb, rd - rb * cb
        picked = lax.broadcasted_iota(jnp.int32, (PART, LANES), 0) + c == lax.broadcasted_iota(
            jnp.int32, (PART, LANES), 1
        ) * memb
        if ready:
            free, tied = jnp.where(upper, d, a), jnp.where(upper, a, d)
            h_free, h_tied = jnp.where(upper, h2, h1), jnp.where(upper, h1, h2)
            free_inv = 1.0 / free
            lean = b * free_inv
            pay_ref[at, :] = h_tied + lean * h_free
            stiff = tied - b * lean
            end_ref[lo, :] = lean
            end_ref[mid, :] = h_free * free_inv
            end_ref[hi, :] = stiff
            values = (stiff,)
        else:
            pay_ref[lo, :] = h1
            pay_ref[mid, :] = h2
            values = (a, b, d)
            for k, value in enumerate(values):
                next_ref[k * cells + c : k * cells + c + PART, :] = value
        for k, value in enumerate(values):
            chosen = jnp.where(picked, value, 0.0)
            for r in range(0, PART, 8):
                acc[k] = acc[k] + chosen[r : r + 8]
    lines = [jnp.sum(x, axis=0, keepdims=True) for x in acc[: 1 if ready else 3]]
    pay_ref[cells * (1 if ready else 2) :, :] = pack_small(lines)


def finish_kernel(*refs, levels, memb):
    own_ref, coef_ref, mine_ref, other_ref, end_ref = refs[:5]
    backs = refs[5 : 5 + levels - 1]
    q_ref, phi_ref, psi_ref, out_hbm, out, sem = refs[5 + levels - 1 :]
    cells = coef_ref.shape[0] // 3
    rows = q_ref.shape[0] // cells
    upper = on_right("lat", levels - 1)
    small = other_ref[cells:, :]

    def chunk_copy(k):
        at = pl.ds(pl.multiple_of(k * PART, PART), PART)
        return pltpu.make_async_copy(out.at[:, at, :], out_hbm.at[:, at, :], sem.at[k])

    @pl.loop(0, cells // PART)
    def _(k):
        c = pl.multiple_of(k * PART, PART)
        lo, mid, hi = (pl.ds(pl.multiple_of(p * cells + c, PART), PART) for p in range(3))
        stiff = end_ref[hi, :] + unpack_small(small, 0, c, memb)
        middle = -(mine_ref[lo, :] + other_ref[lo, :]) / stiff
        outer = end_ref[lo, :] * middle - end_ref[mid, :]
        u_in, u_out = jnp.where(upper, middle, outer), jnp.where(upper, outer, middle)
        for level in reversed(range(levels - 1)):
            back = backs[level]
            middle = back[mid, :] * u_in + back[hi, :] * u_out - back[lo, :]
            right = on_right("lat", level)
            u_in, u_out = jnp.where(right, middle, u_in), jnp.where(right, u_out, middle)
        flux = coef_ref[mid, :] * u_out - coef_ref[lo, :] * u_in - own_ref[lo, :]
        for j in range(rows):
            at = pl.ds(pl.multiple_of(j * cells + c, PART), PART)
            out[j, lo, :] = q_ref[at, :] + phi_ref[at, :] * u_in + psi_ref[at, :] * flux
        chunk_copy(k).start()

    for k in range(cells // PART):
        chunk_copy(k).wait()


def swapped(value, axis, mask):
    return lax.ppermute(value, axis, [(s, s ^ mask) for s in range(lax.axis_size(axis))])


def shards(ensemble, grad_increment, normalization, lon_diffusion, lat_diffusion, vert_diag, vert_sub):
    rows, cols, memb, lev = ensemble.shape
    bands, blocks = lax.axis_size("lat"), lax.axis_size("lon")
    lat_levels, lon_levels = int(math.log2(bands)), int(math.log2(blocks))
    assert lev == LANES and 8 < rows <= 16 and 8 % memb == 0 and cols <= LANES and cols % CHUNK == 0
    assert 2**lat_levels == bands and 2**lon_levels == blocks and lat_levels >= 2 and lon_levels >= 2
    rest, cells = rows - 8, cols * memb
    assert 8 % rest == 0 and memb * rest % 8 == 0 and cells % PART == 0
    stride = cells + 1
    spaced = -(-(rows + 1) * stride // 8) * 8
    half = memb * rows
    hbm_spec = pl.BlockSpec(memory_space=pltpu.HBM)

    part, phi_t, psi_t, pay = call(
        lon_sweep_kernel,
        (shape(cells, 16, LANES), shape(cols, 16, LANES), shape(cols, 16, LANES), shape(2 * half + 16, LANES)),
        scratch=[
            pltpu.VMEM((cells, 16, LANES), F32),
            pltpu.VMEM((cols, 16, LANES), F32),
            pltpu.VMEM((rows, cols), F32),
            pltpu.VMEM((rows, cols), F32),
            pltpu.VMEM((cols, 16, LANES), F32),
            pltpu.VMEM((cols, 16, LANES), F32),
            pltpu.SemaphoreType.DMA((2 * (cols // CHUNK) + 2,)),
        ],
        in_specs=[hbm_spec] * 4,
        cost=cost(2),
    )(*(in_hbm(x) for x in (ensemble.reshape(rows, cells, lev), grad_increment, normalization, lon_diffusion)))

    own, backs = pay, []
    spans = lon_rounds(lon_levels)
    for index, span in enumerate(spans):
        others = [swapped(pay, "lon", k << span[0]) for k in reversed(range(1, 1 << len(span)))][::-1]
        if index == LOCAL_ROUND:
            pay, part, phi_t, psi_t, lat_diffusion = lax.optimization_barrier(
                (pay, part, phi_t, psi_t, lat_diffusion)
            )
            phi, psi = call(
                functools.partial(expand_kernel, memb=memb, stride=stride, rows=rows),
                (shape(spaced, LANES), shape(spaced, LANES)),
                cost=cost(1),
            )(phi_t, psi_t)
            step, lat_phi, lat_psi, coef, small, cosine = call(
                functools.partial(lat_coef_kernel, memb=memb, stride=stride, bands=bands),
                (
                    shape(spaced, LANES),
                    shape(rows * cells, LANES),
                    shape(rows * cells, LANES),
                    shape(3 * cells, LANES),
                    shape(8, LANES),
                    shape(16, LANES),
                ),
                cost=cost(1),
            )(lat_diffusion)
            y, weights = call(
                functools.partial(vertical_kernel, stride=stride, rows=rows),
                (shape(spaced, LANES), shape(2 * LANES, 2 * LANES, dtype=jnp.bfloat16)),
                scratch=[pltpu.VMEM((8, LANES), F32)] + [pltpu.VMEM((LANES, LANES), F32)] * 3,
                cost=cost(2),
            )(vert_diag.reshape(1, lev), vert_sub.reshape(1, lev - 1), part)
            others, phi, psi, step, lat_phi, lat_psi, coef, small, cosine, y, weights = lax.optimization_barrier(
                (others, phi, psi, step, lat_phi, lat_psi, coef, small, cosine, y, weights)
            )
        if index < len(spans) - 1:
            pay, *more = call(
                functools.partial(lon_merge_kernel, levels=span, memb=memb, rest=rest),
                (shape(2 * half + 16, LANES),) + (shape(half + 32, LANES),) * len(span),
                cost=cost(1),
            )(pay, *others)
            backs += more
    q, lat_pay = call(
        functools.partial(lat_sweep_kernel, levels=spans[-1], memb=memb, rest=rest, stride=stride),
        (shape(rows * cells, LANES), shape(2 * cells + 8, LANES)),
        scratch=[pltpu.VMEM((2 * half + 8, LANES), F32), pltpu.VMEM((16 * rows, LANES), F32)],
        cost=cost(1),
    )(own, pay, *others, *backs, y, phi, psi, weights, step, coef, small, cosine)

    pay, group, lat_backs = lat_pay, coef, []
    for level in range(lat_levels - 1):
        other = swapped(pay, "lat", 1 << level)
        ready = level == lat_levels - 2
        pay, back, group = call(
            functools.partial(lat_merge_kernel, level=level, levels=lat_levels, memb=memb),
            (shape((1 if ready else 2) * cells + 8, LANES), shape(3 * cells, LANES), shape(3 * cells, LANES)),
            cost=cost(1),
        )(pay, group, other)
        lat_backs.append(back)
    other = swapped(pay, "lat", 1 << (lat_levels - 1))
    out = call(
        functools.partial(finish_kernel, levels=lat_levels, memb=memb),
        shape(rows, cells, LANES),
        scratch=[
            pltpu.VMEM((rows, cells, LANES), F32),
            pltpu.SemaphoreType.DMA((cells // PART,)),
        ],
        out_specs=hbm_spec,
        cost=cost(1),
    )(lat_pay, coef, pay, other, group, *lat_backs, q, lat_phi, lat_psi)
    return out.reshape(rows, cols, memb, lev)


def lon_rounds(levels):
    return [tuple(range(k, min(k + 2, levels))) for k in range(0, levels, 2)]


def in_hbm(value):
    return pltpu.with_memory_space_constraint(value, pltpu.HBM)


def cost(microseconds):
    return pl.CostEstimate(flops=0, bytes_accessed=int(microseconds * 3e6), transcendentals=0)


def solution(mesh):
    in_specs = (
        P("lat", "lon", None, None),
        P("lat", "lon", None),
        P("lat", "lon"),
        P("lat", "lon"),
        P("lat", "lon"),
        P(),
        P(),
    )
    out_specs = P("lat", "lon", None, None)
    return jax.shard_map(shards, mesh=mesh, in_specs=in_specs, out_specs=out_specs, check_vma=False)
```

```python
import functools
import math

import jax
import jax.numpy as jnp
from jax import lax
from jax.experimental import pallas as pl
from jax.experimental.pallas import tpu as pltpu
from jax.sharding import PartitionSpec as P


F32 = jnp.float32
LANES = 128
CHUNK = 16
PART = 64
VMEM_BYTES = 16 * 2**20
LOCAL_ROUND = 1


def call(kernel, outs, scratch=(), in_specs=None, out_specs=None, cost=None):
    specs = {k: v for k, v in (("in_specs", in_specs), ("out_specs", out_specs)) if v is not None}
    return pl.pallas_call(
        kernel,
        out_shape=outs,
        **specs,
        scratch_shapes=scratch,
        cost_estimate=cost,
        compiler_params=pltpu.CompilerParams(vmem_limit_bytes=VMEM_BYTES),
    )


def shape(*dims, dtype=F32):
    return jax.ShapeDtypeStruct(dims, dtype)


def lane_of(value, lane, rows):
    return jnp.broadcast_to(value[:, lane : lane + 1], (rows, LANES))


def split_rows(value):
    rest = value.shape[0] - 8
    fill = jnp.ones((8 - rest, value.shape[1]), F32)
    return value[:8], jnp.concatenate([value[8:], fill], axis=0)


def lon_sweep_kernel(
    ens_hbm,
    grad_hbm,
    norm_hbm,
    diff_hbm,
    part_ref,
    phi_ref,
    psi_ref,
    pay_ref,
    ens,
    grad,
    norm_ref,
    diff_ref,
    step_b,
    norm_b,
    sem,
):
    rows, cells, _ = ens_hbm.shape
    cols = grad_hbm.shape[1]
    memb = cells // cols
    rest = rows - 8
    half = memb * rows
    chunks = cols // CHUNK
    first = pltpu.make_async_copy(diff_hbm, diff_ref, sem.at[2 * chunks])
    second = pltpu.make_async_copy(norm_hbm, norm_ref, sem.at[2 * chunks + 1])
    first.start()
    second.start()
    arrivals = []
    for c in range(chunks):
        g_rows, e_rows = pl.ds(c * CHUNK, CHUNK), pl.ds(c * CHUNK * memb, CHUNK * memb)
        for j in range(rows):
            pltpu.make_async_copy(grad_hbm.at[j, g_rows], grad.at[g_rows, j, :], sem.at[2 * c]).start()
            pltpu.make_async_copy(ens_hbm.at[j, e_rows], ens.at[e_rows, j, :], sem.at[2 * c + 1]).start()
        arrivals.append(
            (
                pltpu.make_async_copy(grad_hbm.at[:, g_rows], grad_hbm.at[:, g_rows], sem.at[2 * c]),
                pltpu.make_async_copy(ens_hbm.at[:, e_rows], ens_hbm.at[:, e_rows], sem.at[2 * c + 1]),
            )
        )
    zero, one = jnp.zeros((8, LANES), F32), jnp.ones((8, LANES), F32)
    tiles = [slice(0, 8), slice(8, 16)]

    first.wait()
    second.wait()
    step = split_rows(1.0 / diff_ref[...])
    norm = split_rows(norm_ref[...])
    phi, phi_f, psi, psi_f = [one] * 2, [zero] * 2, [zero] * 2, [one] * 2
    for i in range(cols):
        for g in range(2):
            t = lane_of(step[g], i, 8)
            step_b[i, tiles[g], :] = t
            norm_b[i, tiles[g], :] = lane_of(norm[g], i, 8)
            phi_ref[i, tiles[g], :] = phi[g]
            psi_ref[i, tiles[g], :] = psi[g]
            phi_f[g] = phi_f[g] + phi[g]
            psi_f[g] = psi_f[g] + psi[g]
            phi[g] = phi[g] + t * phi_f[g]
            psi[g] = psi[g] + t * psi_f[g]
    lanes = lax.broadcasted_iota(jnp.int32, (8, LANES), 1)
    ends = []
    for g in range(2):
        b = 1.0 / psi[g]
        a, d = phi[g] * b, psi_f[g] * b
        ends.append((b, d))
        size = 8 if g == 0 else rest
        coef = jnp.where(lanes == 0, a, jnp.where(lanes == 1, b, d))
        for k in range(8 // size):
            row = 2 * half + 8 * g + k * size
            pay_ref[row : row + size, :] = coef[:size]

    u = [[zero] * memb for _ in range(2)]
    flux = [[zero] * memb for _ in range(2)]
    for i in range(cols):
        if i % CHUNK == 0:
            for copy in arrivals[i // CHUNK]:
                copy.wait()
        for g in range(2):
            t = step_b[i, tiles[g], :]
            w = norm_b[i, tiles[g], :] * grad[i, tiles[g], :]
            for m in range(memb):
                part_ref[i * memb + m, tiles[g], :] = u[g][m]
                f = w * ens[i * memb + m, tiles[g], :]
                flux[g][m] = flux[g][m] + (u[g][m] - f)
                u[g][m] = u[g][m] + t * flux[g][m]
    for g in range(2):
        b, d = ends[g]
        start = 0 if g == 0 else 8 * memb
        size = 8 if g == 0 else rest
        for m in range(memb):
            at = start + m * size
            pay_ref[at : at + size, :] = (u[g][m] * b)[:size]
            pay_ref[half + at : half + at + size, :] = (flux[g][m] - d * u[g][m])[:size]


def lon_expand(tiles, memb, rest):
    return jnp.concatenate([tiles[:8]] * memb + [tiles[8:]] * (memb * rest // 8), axis=0)


def lon_parts(pay, half):
    coef = pay[2 * half :]
    return (pay[:half], pay[half : 2 * half]) + tuple(lane_of(coef, k, 16) for k in range(3))


def lon_join(mine, other, right, memb, rest):
    lh1, lh2, la, lb, ld = (jnp.where(right, o, m) for m, o in zip(mine, other))
    rh1, rh2, ra, rb, rd = (jnp.where(right, m, o) for m, o in zip(mine, other))
    inv = 1.0 / (ld + ra)
    ca, cb = lb * inv, rb * inv
    grow = functools.partial(lon_expand, memb=memb, rest=rest)
    total = lh2 + rh1
    joined = (lh1 + grow(ca) * total, rh2 + grow(cb) * total, la - lb * ca, lb * cb, rd - rb * cb)
    return joined, (total * grow(inv), ca, cb)


def lon_join_round(pays, levels, memb, rest):
    half = memb * (8 + rest)
    groups = [lon_parts(p[...], half) for p in pays]
    backs = []
    for level in levels:
        right = on_right("lon", level)
        pairs = [lon_join(groups[k], groups[k + 1], right, memb, rest) for k in range(0, len(groups), 2)]
        groups = [joined for joined, _ in pairs]
        backs.append(pairs[0][1])
    return groups[0], backs


def on_right(axis, level):
    return ((lax.axis_index(axis) >> level) & 1) == 1


def lon_merge_kernel(*refs, levels, memb, rest):
    pays, (pay_ref, *back_refs) = refs[: 1 << len(levels)], refs[1 << len(levels) :]
    (h1, h2, a, b, d), backs = lon_join_round(pays, levels, memb, rest)
    half = h1.shape[0]
    lanes = lax.broadcasted_iota(jnp.int32, a.shape, 1)
    pay_ref[:half, :] = h1
    pay_ref[half : 2 * half, :] = h2
    pay_ref[2 * half :, :] = jnp.where(lanes == 0, a, jnp.where(lanes == 1, b, d))
    for back_ref, (s, ca, cb) in zip(back_refs, backs):
        back_ref[:half, :] = s
        back_ref[half : half + 16, :] = ca
        back_ref[half + 16 :, :] = cb


def times_inverse(rows, weights):
    high = rows.astype(jnp.bfloat16)
    low = (rows - high.astype(F32)).astype(jnp.bfloat16)
    out = jnp.dot(jnp.concatenate([high, low], axis=1), weights, preferred_element_type=F32)
    return out[:, :LANES] + out[:, LANES:]


def vertical_kernel(diag_ref, sub_ref, part_ref, y_ref, weights_ref, line, ratio, inverse, factor, *, stride, rows):
    levels = diag_ref.shape[1]
    line[...] = jnp.zeros_like(line)
    line[0:1, 0 : levels - 1] = sub_ref[...]
    row_ids = lax.broadcasted_iota(jnp.int32, (levels, levels), 0)
    col_ids = lax.broadcasted_iota(jnp.int32, (levels, levels), 1)
    diag = jnp.sum(jnp.where(row_ids == col_ids, diag_ref[...], 0.0), axis=1, keepdims=True)
    below = jnp.sum(jnp.where(row_ids == col_ids + 1, line[0:1, :], 0.0), axis=1, keepdims=True)
    inv = 1.0 / jnp.broadcast_to(diag, (levels, levels))
    inverse[...] = inv
    ratio[...] = -jnp.broadcast_to(below, (levels, levels)) * inv
    lane = lax.broadcasted_iota(jnp.int32, (1, levels), 1)
    row = jnp.zeros((1, levels), F32)
    for i in range(levels):
        row = jnp.where(lane == i, inverse[i : i + 1, :], row * ratio[i : i + 1, :])
        factor[i : i + 1, :] = row
    low_inv = factor[...]
    full = jnp.dot(low_inv.T, low_inv, preferred_element_type=F32, precision=lax.Precision.HIGHEST)
    high = full.astype(jnp.bfloat16)
    low = (full - high.astype(F32)).astype(jnp.bfloat16)
    weights_ref[0:levels, 0:levels] = high
    weights_ref[0:levels, levels:] = low
    weights_ref[levels:, 0:levels] = high
    weights_ref[levels:, levels:] = jnp.zeros_like(low)
    weights = weights_ref[...]
    cells = part_ref.shape[0]
    for c in range(0, cells, 16):
        y = times_inverse(part_ref[c : c + 16].reshape(256, LANES), weights)
        for k in range(16):
            y_ref[pl.ds(c + k, 8, stride=stride), :] = y[16 * k : 16 * k + 8]
            y_ref[pl.ds(8 * stride + c + k, rows - 8, stride=stride), :] = y[16 * k + 8 : 16 * k + rows]


def spread(out_ref, tiles, i, memb, stride, rows):
    for m in range(memb):
        out_ref[pl.ds(i * memb + m, 8, stride=stride), :] = tiles[0]
        out_ref[pl.ds(8 * stride + i * memb + m, rows - 8, stride=stride), :] = tiles[1][: rows - 8]


def expand_kernel(phi_ref, psi_ref, phi_out, psi_out, *, memb, stride, rows):
    for i in range(phi_ref.shape[0]):
        for src, dst in ((phi_ref, phi_out), (psi_ref, psi_out)):
            spread(dst, (src[i, 0:8, :], src[i, 8:16, :]), i, memb, stride, rows)


def lat_coef_kernel(diff_ref, step_out, phi_out, psi_out, coef_out, small_out, cos_out, *, memb, stride, bands):
    rows, cols = diff_ref.shape
    cells = cols * memb
    band = lax.axis_index("lat")
    row_ids = lax.broadcasted_iota(jnp.int32, (rows, cols), 0)
    last = jnp.logical_and(row_ids == rows - 1, band == bands - 1)
    step = split_rows(jnp.where(last, 0.0, 1.0 / diff_ref[...]))
    for i in range(cols):
        spread(step_out, [lane_of(s, i, 8) for s in step], i, memb, stride, rows)
    tile_ids = lax.broadcasted_iota(jnp.int32, (16, LANES), 0) + band * rows
    cosine = jnp.cos(-jnp.pi / 2 + (tile_ids.astype(F32) + 0.5) * jnp.pi / (bands * rows))
    cos_out[...] = cosine
    acc = [jnp.zeros((8, LANES), F32) for _ in range(3)]
    lane = lax.broadcasted_iota(jnp.int32, (PART, LANES), 1)
    for c in range(0, cells, PART):
        phi = jnp.ones((PART, LANES), F32)
        psi = jnp.zeros((PART, LANES), F32)
        phi_f, psi_f = psi, phi
        for j in range(rows):
            cos_j = jnp.broadcast_to(cosine[j : j + 1, :], (PART, LANES))
            t = step_out[j * stride + c : j * stride + c + PART, :]
            now_phi, now_psi = cos_j * phi, cos_j * psi
            phi_out[j * cells + c : j * cells + c + PART, :] = now_phi
            psi_out[j * cells + c : j * cells + c + PART, :] = now_psi
            phi_f = phi_f + now_phi
            psi_f = psi_f + now_psi
            phi = phi + t * phi_f
            psi = psi + t * psi_f
        b = 1.0 / psi
        picked = lax.broadcasted_iota(jnp.int32, (PART, LANES), 0) + c == lane * memb
        for k, value in enumerate((phi * b, b, psi_f * b)):
            coef_out[k * cells + c : k * cells + c + PART, :] = value
            chosen = jnp.where(picked, value, 0.0)
            for r in range(0, PART, 8):
                acc[k] = acc[k] + chosen[r : r + 8]
    small_out[...] = pack_small([jnp.sum(a, axis=0, keepdims=True) for a in acc])


def pack_small(lines):
    tile = lax.broadcasted_iota(jnp.int32, (8, LANES), 0)
    out = jnp.zeros((8, LANES), F32)
    for k, line in enumerate(lines):
        out = jnp.where(tile == k, jnp.broadcast_to(line, (8, LANES)), out)
    return out


def lat_sweep_kernel(*refs, levels, memb, rest, stride, paired):
    count = 1 << len(levels)
    own_ref, pays, backs = refs[0], refs[1 : 1 + count], refs[1 + count : 1 + count + levels[0]]
    refs = refs[1 + count + levels[0] :]
    y_ref, phi_ref, psi_ref, weights_ref, step_ref, coef_ref, small_ref, cos_ref = refs[:8]
    weight_ref, sum_ref = (refs[8], refs[11]) if paired else (None, None)
    (q_ref, pay_ref), (ends, tiles) = refs[8 + paired : 10 + paired], refs[-2:]
    rows = 8 + rest
    half = memb * rows
    grow = functools.partial(lon_expand, memb=memb, rest=rest)
    (h1, h2, a, b, d), last = lon_join_round(pays, levels, memb, rest)
    u_in = -(h1 + h2) * grow(1.0 / (a + d - 2.0 * b))
    u_out = u_in
    stored = [(back[:half, :], back[half : half + 16, :], back[half + 16 :, :]) for back in backs]
    for level, (s, ca, cb) in reversed(list(enumerate(stored + last))):
        middle = grow(ca) * u_in + grow(cb) * u_out - s
        right = on_right("lon", level)
        u_in, u_out = jnp.where(right, middle, u_in), jnp.where(right, u_out, middle)
    oh1, _, oa, ob, _ = lon_parts(own_ref[...], half)
    f_in = grow(ob) * u_out - grow(oa) * u_in - oh1
    weights = weights_ref[...]
    ends[: 2 * half, :] = times_inverse(jnp.concatenate([u_in, f_in], axis=0), weights)
    for k in range(2):
        for j in range(rows):
            if j < 8:
                value = ends[pl.ds(k * half + j, memb, stride=8), :]
            else:
                value = ends[pl.ds(k * half + 8 * memb + j - 8, memb, stride=rest), :]
            tiles[8 * (k * rows + j) : 8 * (k * rows + j) + 8, :] = jnp.concatenate([value] * (8 // memb), axis=0)
    cells = coef_ref.shape[0] // 3
    for c in range(0, cells, PART):
        v = jnp.zeros((PART, LANES), F32)
        flux = v
        for j in range(rows):
            at = slice(j * stride + c, j * stride + c + PART)
            u_tile = jnp.concatenate([tiles[8 * j : 8 * j + 8, :]] * (PART // 8), axis=0)
            f_tile = jnp.concatenate([tiles[8 * (rows + j) : 8 * (rows + j) + 8, :]] * (PART // 8), axis=0)
            u = y_ref[at, :] + phi_ref[at, :] * u_tile + psi_ref[at, :] * f_tile
            now = jnp.broadcast_to(cos_ref[j : j + 1, :], (PART, LANES)) * v
            q_ref[j * cells + c : j * cells + c + PART, :] = now
            flux = flux + (now - u)
            v = v + step_ref[at, :] * flux
        b = coef_ref[cells + c : cells + c + PART, :]
        d = coef_ref[2 * cells + c : 2 * cells + c + PART, :]
        h1, h2 = v * b, flux - d * v
        pay_ref[c : c + PART, :] = h1
        pay_ref[cells + c : cells + c + PART, :] = h2
        if paired:
            sum_ref[c : c + PART, :] = (
                weight_ref[c : c + PART, :] * h1 + weight_ref[cells + c : cells + c + PART, :] * h2
            )
    pay_ref[2 * cells :, :] = small_ref[...]


def unpack_small(tile, k, c, memb):
    row = lax.broadcasted_iota(jnp.int32, (PART, LANES), 0) + c
    lane = lax.broadcasted_iota(jnp.int32, (PART, LANES), 1) * memb
    mask = jnp.logical_and(row >= lane, row < lane + memb)
    line = jnp.broadcast_to(tile[k : k + 1, :], (PART, LANES))
    return jnp.broadcast_to(jnp.sum(jnp.where(mask, line, 0.0), axis=1, keepdims=True), (PART, LANES))


def lat_merge_kernel(mine_ref, coef_ref, other_ref, *outs, level, levels, memb):
    ready = level == levels - 2
    if ready:
        pay_ref, back_ref, end_ref = outs
    else:
        pay_ref, back_ref, next_ref = outs
    cells = coef_ref.shape[0] // 3
    right = on_right("lat", level)
    upper = on_right("lat", level + 1)
    small = other_ref[2 * cells :, :]
    acc = [jnp.zeros((8, LANES), F32) for _ in range(3)]
    for c in range(0, cells, PART):
        at = slice(c, c + PART)
        lo, mid, hi = (slice(k * cells + c, k * cells + c + PART) for k in range(3))
        mine = [mine_ref[lo, :], mine_ref[mid, :], coef_ref[lo, :], coef_ref[mid, :], coef_ref[hi, :]]
        other = [other_ref[lo, :], other_ref[mid, :]] + [unpack_small(small, k, c, memb) for k in range(3)]
        lh1, lh2, la, lb, ld = (jnp.where(right, o, m) for m, o in zip(mine, other))
        rh1, rh2, ra, rb, rd = (jnp.where(right, m, o) for m, o in zip(mine, other))
        inv = 1.0 / (ld + ra)
        ca, cb = lb * inv, rb * inv
        total = lh2 + rh1
        back_ref[lo, :] = total * inv
        back_ref[mid, :] = ca
        back_ref[hi, :] = cb
        h1, h2 = lh1 + ca * total, rh2 + cb * total
        a, b, d = la - lb * ca, lb * cb, rd - rb * cb
        picked = lax.broadcasted_iota(jnp.int32, (PART, LANES), 0) + c == lax.broadcasted_iota(
            jnp.int32, (PART, LANES), 1
        ) * memb
        if ready:
            free, tied = jnp.where(upper, d, a), jnp.where(upper, a, d)
            h_free, h_tied = jnp.where(upper, h2, h1), jnp.where(upper, h1, h2)
            free_inv = 1.0 / free
            lean = b * free_inv
            pay_ref[at, :] = h_tied + lean * h_free
            stiff = tied - b * lean
            end_ref[lo, :] = lean
            end_ref[mid, :] = h_free * free_inv
            values = (stiff,)
        else:
            pay_ref[lo, :] = h1
            pay_ref[mid, :] = h2
            values = (a, b, d)
            for k, value in enumerate(values):
                next_ref[k * cells + c : k * cells + c + PART, :] = value
        for k, value in enumerate(values):
            chosen = jnp.where(picked, value, 0.0)
            for r in range(0, PART, 8):
                acc[k] = acc[k] + chosen[r : r + 8]
    lines = [jnp.sum(x, axis=0, keepdims=True) for x in acc[: 1 if ready else 3]]
    pay_ref[cells * (1 if ready else 2) :, :] = pack_small(lines)


def lat_pair_kernel(coef_ref, other_ref, weight_ref, small_ref, *, memb):
    cells = coef_ref.shape[0] // 3
    right, upper = on_right("lat", 0), on_right("lat", 1)
    small = other_ref[...]
    acc = jnp.zeros((8, LANES), F32)
    one = jnp.ones((PART, LANES), F32)
    for c in range(0, cells, PART):
        lo, mid, hi = (slice(k * cells + c, k * cells + c + PART) for k in range(3))
        mine = [coef_ref[lo, :], coef_ref[mid, :], coef_ref[hi, :]]
        other = [unpack_small(small, k, c, memb) for k in range(3)]
        la, lb, ld = (jnp.where(right, o, m) for m, o in zip(mine, other))
        ra, rb, rd = (jnp.where(right, m, o) for m, o in zip(mine, other))
        inv = 1.0 / (ld + ra)
        ca, cb = lb * inv, rb * inv
        a, b, d = la - lb * ca, lb * cb, rd - rb * cb
        free, tied = jnp.where(upper, d, a), jnp.where(upper, a, d)
        lean = b / free
        shared = jnp.where(upper, ca + lean * cb, cb + lean * ca)
        own = jnp.where(right == upper, lean, one)
        weight_ref[lo, :] = jnp.where(right, shared, own)
        weight_ref[mid, :] = jnp.where(right, own, shared)
        acc = pick_small(acc, tied - b * lean, c, memb)
    small_ref[...] = pack_small([jnp.sum(acc, axis=0, keepdims=True)])


def pick_small(acc, value, c, memb):
    row = lax.broadcasted_iota(jnp.int32, (PART, LANES), 0) + c
    chosen = jnp.where(row == lax.broadcasted_iota(jnp.int32, (PART, LANES), 1) * memb, value, 0.0)
    for r in range(0, PART, 8):
        acc = acc + chosen[r : r + 8]
    return acc


def lat_add_kernel(mine_ref, other_ref, small_ref, pay_ref):
    cells = mine_ref.shape[0]
    pay_ref[:cells, :] = mine_ref[...] + other_ref[...]
    pay_ref[cells:, :] = small_ref[...]


def finish_kernel(*refs, levels, memb):
    own_ref, coef_ref, mine_ref, other_ref, end_ref = refs[:5]
    backs = refs[5 : 5 + levels - 1]
    q_ref, phi_ref, psi_ref, out_hbm, out, middles, sem = refs[5 + levels - 1 :]
    cells = coef_ref.shape[0] // 3
    rows = q_ref.shape[0] // cells
    upper = on_right("lat", levels - 1)
    soft = 1.0 / (mine_ref[cells:, :] + other_ref[cells:, :])
    for c in range(0, cells, PART):
        middles[c : c + PART, :] = -(mine_ref[c : c + PART, :] + other_ref[c : c + PART, :]) * unpack_small(
            soft, 0, c, memb
        )

    def chunk_copy(k):
        at = pl.ds(pl.multiple_of(k * PART, PART), PART)
        return pltpu.make_async_copy(out.at[:, at, :], out_hbm.at[:, at, :], sem.at[k])

    @pl.loop(0, cells // PART)
    def _(k):
        c = pl.multiple_of(k * PART, PART)
        lo, mid, hi = (pl.ds(pl.multiple_of(p * cells + c, PART), PART) for p in range(3))
        middle = middles[lo, :]
        outer = end_ref[lo, :] * middle - end_ref[mid, :]
        u_in, u_out = jnp.where(upper, middle, outer), jnp.where(upper, outer, middle)
        for level in reversed(range(levels - 1)):
            back = backs[level]
            middle = back[mid, :] * u_in + back[hi, :] * u_out - back[lo, :]
            right = on_right("lat", level)
            u_in, u_out = jnp.where(right, middle, u_in), jnp.where(right, u_out, middle)
        flux = coef_ref[mid, :] * u_out - coef_ref[lo, :] * u_in - own_ref[lo, :]
        for j in range(rows):
            at = pl.ds(pl.multiple_of(j * cells + c, PART), PART)
            out[j, lo, :] = q_ref[at, :] + phi_ref[at, :] * u_in + psi_ref[at, :] * flux
        chunk_copy(k).start()

    for k in range(cells // PART):
        chunk_copy(k).wait()


def swapped(value, axis, mask):
    return lax.ppermute(value, axis, [(s, s ^ mask) for s in range(lax.axis_size(axis))])


def shards(ensemble, grad_increment, normalization, lon_diffusion, lat_diffusion, vert_diag, vert_sub):
    rows, cols, memb, lev = ensemble.shape
    bands, blocks = lax.axis_size("lat"), lax.axis_size("lon")
    lat_levels, lon_levels = levels_of(bands), levels_of(blocks)
    assert lev == LANES and 8 < rows <= 16 and 8 % memb == 0 and cols <= LANES and cols % CHUNK == 0
    assert 2**lat_levels == bands and 2**lon_levels == blocks and lat_levels >= 2 and lon_levels >= 2
    rest, cells = rows - 8, cols * memb
    assert 8 % rest == 0 and memb * rest % 8 == 0 and cells % PART == 0
    stride = cells + 1
    spaced = -(-(rows + 1) * stride // 8) * 8
    half = memb * rows
    hbm_spec = pl.BlockSpec(memory_space=pltpu.HBM)

    part, phi_t, psi_t, pay = call(
        lon_sweep_kernel,
        (shape(cells, 16, LANES), shape(cols, 16, LANES), shape(cols, 16, LANES), shape(2 * half + 16, LANES)),
        scratch=[
            pltpu.VMEM((cells, 16, LANES), F32),
            pltpu.VMEM((cols, 16, LANES), F32),
            pltpu.VMEM((rows, cols), F32),
            pltpu.VMEM((rows, cols), F32),
            pltpu.VMEM((cols, 16, LANES), F32),
            pltpu.VMEM((cols, 16, LANES), F32),
            pltpu.SemaphoreType.DMA((2 * (cols // CHUNK) + 2,)),
        ],
        in_specs=[hbm_spec] * 4,
        cost=cost(2),
    )(*(in_hbm(x) for x in (ensemble.reshape(rows, cells, lev), grad_increment, normalization, lon_diffusion)))

    own, backs = pay, []
    paired = lat_levels == 2
    spans = lon_rounds(lon_levels)
    for index, span in enumerate(spans):
        others = [swapped(pay, "lon", k << span[0]) for k in reversed(range(1, 1 << len(span)))][::-1]
        if index == LOCAL_ROUND:
            pay, part, phi_t, psi_t, lat_diffusion = lax.optimization_barrier(
                (pay, part, phi_t, psi_t, lat_diffusion)
            )
            phi, psi = call(
                functools.partial(expand_kernel, memb=memb, stride=stride, rows=rows),
                (shape(spaced, LANES), shape(spaced, LANES)),
                cost=cost(1),
            )(phi_t, psi_t)
            step, lat_phi, lat_psi, coef, small, cosine = call(
                functools.partial(lat_coef_kernel, memb=memb, stride=stride, bands=bands),
                (
                    shape(spaced, LANES),
                    shape(rows * cells, LANES),
                    shape(rows * cells, LANES),
                    shape(3 * cells, LANES),
                    shape(8, LANES),
                    shape(16, LANES),
                ),
                cost=cost(1),
            )(lat_diffusion)
            if paired:
                pair_weight, pair_small = call(
                    functools.partial(lat_pair_kernel, memb=memb),
                    (shape(2 * cells, LANES), shape(8, LANES)),
                    cost=cost(1),
                )(coef, swapped(small, "lat", 1))
            else:
                pair_weight = pair_small = small
            y, weights = call(
                functools.partial(vertical_kernel, stride=stride, rows=rows),
                (shape(spaced, LANES), shape(2 * LANES, 2 * LANES, dtype=jnp.bfloat16)),
                scratch=[pltpu.VMEM((8, LANES), F32)] + [pltpu.VMEM((LANES, LANES), F32)] * 3,
                cost=cost(2),
            )(vert_diag.reshape(1, lev), vert_sub.reshape(1, lev - 1), part)
            others, phi, psi, step, lat_phi, lat_psi, coef, cosine, y, weights, pair_weight, pair_small = (
                lax.optimization_barrier(
                    (others, phi, psi, step, lat_phi, lat_psi, coef, cosine, y, weights, pair_weight, pair_small)
                )
            )
        if index < len(spans) - 1:
            pay, *more = call(
                functools.partial(lon_merge_kernel, levels=span, memb=memb, rest=rest),
                (shape(2 * half + 16, LANES),) + (shape(half + 32, LANES),) * len(span),
                cost=cost(1),
            )(pay, *others)
            backs += more
    q, lat_pay, *sums = call(
        functools.partial(
            lat_sweep_kernel, levels=spans[-1], memb=memb, rest=rest, stride=stride, paired=paired
        ),
        (shape(rows * cells, LANES), shape(2 * cells + 8, LANES)) + (shape(cells, LANES),) * paired,
        scratch=[pltpu.VMEM((2 * half + 8, LANES), F32), pltpu.VMEM((16 * rows, LANES), F32)],
        cost=cost(1),
    )(own, pay, *others, *backs, y, phi, psi, weights, step, coef, small, cosine, *(pair_weight,) * paired)

    if paired:
        pay = call(lat_add_kernel, shape(cells + 8, LANES), cost=cost(1))(
            sums[0], swapped(sums[0], "lat", 1), pair_small
        )
        final = swapped(pay, "lat", 3)
        behind, _ = lax.optimization_barrier((lat_pay, pay))
        inner = swapped(behind, "lat", 1)
        _, back, group = call(
            functools.partial(lat_merge_kernel, level=0, levels=2, memb=memb),
            (shape(cells + 8, LANES), shape(3 * cells, LANES), shape(2 * cells, LANES)),
            cost=cost(1),
        )(lat_pay, coef, inner)
        lat_backs = [back]
        final, group, back = lax.optimization_barrier((final, group, back))
    else:
        pay, group, lat_backs = lat_pay, coef, []
        for level in range(lat_levels - 1):
            other = swapped(pay, "lat", 1 << level)
            ready = level == lat_levels - 2
            pay, back, group = call(
                functools.partial(lat_merge_kernel, level=level, levels=lat_levels, memb=memb),
                (
                    shape((1 if ready else 2) * cells + 8, LANES),
                    shape(3 * cells, LANES),
                    shape((2 if ready else 3) * cells, LANES),
                ),
                cost=cost(1),
            )(pay, group, other)
            lat_backs.append(back)
        final = swapped(pay, "lat", 1 << (lat_levels - 1) | 1)
    out = call(
        functools.partial(finish_kernel, levels=lat_levels, memb=memb),
        shape(rows, cells, LANES),
        scratch=[
            pltpu.VMEM((rows, cells, LANES), F32),
            pltpu.VMEM((cells, LANES), F32),
            pltpu.SemaphoreType.DMA((cells // PART,)),
        ],
        out_specs=hbm_spec,
        cost=cost(1),
    )(lat_pay, coef, pay, final, group, *lat_backs, q, lat_phi, lat_psi)
    return out.reshape(rows, cols, memb, lev)


def levels_of(count):
    return int(math.log2(count))


def lon_rounds(levels):
    return [tuple(range(k, min(k + 2, levels))) for k in range(0, levels, 2)]


def in_hbm(value):
    return pltpu.with_memory_space_constraint(value, pltpu.HBM)


def cost(microseconds):
    return pl.CostEstimate(flops=0, bytes_accessed=int(microseconds * 3e6), transcendentals=0)


def solution(mesh):
    in_specs = (
        P("lat", "lon", None, None),
        P("lat", "lon", None),
        P("lat", "lon"),
        P("lat", "lon"),
        P("lat", "lon"),
        P(),
        P(),
    )
    out_specs = P("lat", "lon", None, None)
    return jax.shard_map(shards, mesh=mesh, in_specs=in_specs, out_specs=out_specs, check_vma=False)
```

```python
import functools
import math

import jax
import jax.numpy as jnp
from jax import lax
from jax.experimental import pallas as pl
from jax.experimental.pallas import tpu as pltpu
from jax.sharding import PartitionSpec as P


F32 = jnp.float32
LANES = 128
CHUNK = 16
PART = 64
BLOCK = 64
VMEM_BYTES = 16 * 2**20


def call(kernel, outs, scratch=(), in_specs=None, out_specs=None, cost=None):
    specs = {k: v for k, v in (("in_specs", in_specs), ("out_specs", out_specs)) if v is not None}
    return pl.pallas_call(
        kernel,
        out_shape=outs,
        **specs,
        scratch_shapes=scratch,
        cost_estimate=cost,
        compiler_params=pltpu.CompilerParams(vmem_limit_bytes=VMEM_BYTES),
    )


def shape(*dims, dtype=F32):
    return jax.ShapeDtypeStruct(dims, dtype)


def lane_of(value, lane, rows):
    return jnp.broadcast_to(value[:, lane : lane + 1], (rows, LANES))


def split_rows(value):
    rest = value.shape[0] - 8
    fill = jnp.ones((8 - rest, value.shape[1]), F32)
    return value[:8], jnp.concatenate([value[8:], fill], axis=0)


def lon_sweep_kernel(
    ens_hbm,
    grad_hbm,
    norm_hbm,
    diff_hbm,
    part_ref,
    phi_ref,
    psi_ref,
    pay_ref,
    ens,
    grad,
    norm_ref,
    diff_ref,
    step_b,
    norm_b,
    sem,
):
    rows, cells, _ = ens_hbm.shape
    cols = grad_hbm.shape[1]
    memb = cells // cols
    rest = rows - 8
    half = memb * rows
    chunks = cols // CHUNK
    first = pltpu.make_async_copy(diff_hbm, diff_ref, sem.at[2 * chunks])
    second = pltpu.make_async_copy(norm_hbm, norm_ref, sem.at[2 * chunks + 1])
    first.start()
    second.start()
    arrivals = []
    for c in range(chunks):
        g_rows, e_rows = pl.ds(c * CHUNK, CHUNK), pl.ds(c * CHUNK * memb, CHUNK * memb)
        for j in range(rows):
            pltpu.make_async_copy(grad_hbm.at[j, g_rows], grad.at[g_rows, j, :], sem.at[2 * c]).start()
            pltpu.make_async_copy(ens_hbm.at[j, e_rows], ens.at[e_rows, j, :], sem.at[2 * c + 1]).start()
        arrivals.append(
            (
                pltpu.make_async_copy(grad_hbm.at[:, g_rows], grad_hbm.at[:, g_rows], sem.at[2 * c]),
                pltpu.make_async_copy(ens_hbm.at[:, e_rows], ens_hbm.at[:, e_rows], sem.at[2 * c + 1]),
            )
        )
    zero, one = jnp.zeros((8, LANES), F32), jnp.ones((8, LANES), F32)
    tiles = [slice(0, 8), slice(8, 16)]

    first.wait()
    second.wait()
    step = split_rows(1.0 / diff_ref[...])
    norm = split_rows(norm_ref[...])
    phi, phi_f, psi, psi_f = [one] * 2, [zero] * 2, [zero] * 2, [one] * 2
    for i in range(cols):
        for g in range(2):
            t = lane_of(step[g], i, 8)
            step_b[i, tiles[g], :] = t
            norm_b[i, tiles[g], :] = lane_of(norm[g], i, 8)
            phi_ref[i, tiles[g], :] = phi[g]
            psi_ref[i, tiles[g], :] = psi[g]
            phi_f[g] = phi_f[g] + phi[g]
            psi_f[g] = psi_f[g] + psi[g]
            phi[g] = phi[g] + t * phi_f[g]
            psi[g] = psi[g] + t * psi_f[g]
    ends, coefs = [], []
    for g in range(2):
        b = 1.0 / psi[g]
        a, d = phi[g] * b, psi_f[g] * b
        ends.append((b, d))
        coefs.append((a, b, d))
    pay_ref[2 * half :, :] = lon_coef_tile(coefs, rest)

    u = [[zero] * memb for _ in range(2)]
    flux = [[zero] * memb for _ in range(2)]
    for i in range(cols):
        if i % CHUNK == 0:
            for copy in arrivals[i // CHUNK]:
                copy.wait()
        for g in range(2):
            t = step_b[i, tiles[g], :]
            w = norm_b[i, tiles[g], :] * grad[i, tiles[g], :]
            for m in range(memb):
                part_ref[i * memb + m, tiles[g], :] = u[g][m]
                f = w * ens[i * memb + m, tiles[g], :]
                flux[g][m] = flux[g][m] + (u[g][m] - f)
                u[g][m] = u[g][m] + t * flux[g][m]
    for g in range(2):
        b, d = ends[g]
        start = 0 if g == 0 else 8 * memb
        size = 8 if g == 0 else rest
        for m in range(memb):
            at = start + m * size
            pay_ref[at : at + size, :] = (u[g][m] * b)[:size]
            pay_ref[half + at : half + at + size, :] = (flux[g][m] - d * u[g][m])[:size]


def lon_expand(tiles, memb, rest):
    return jnp.concatenate([tiles[:8]] * memb + [tiles[8:]] * (memb * rest // 8), axis=0)


def lon_coef_tile(groups, rest):
    lane = lax.broadcasted_iota(jnp.int32, (8, LANES), 1)
    tile = jnp.zeros((8, LANES), F32)
    for g, group in enumerate(groups):
        for k, value in enumerate(group):
            if g == 1:
                value = jnp.concatenate([value[:rest]] * (8 // rest), axis=0)
            tile = jnp.where(lane == 3 * g + k, value, tile)
    return tile


def lon_parts(pay, half):
    coef = pay[2 * half :]
    coefs = tuple(jnp.concatenate([lane_of(coef, k, 8), lane_of(coef, 3 + k, 8)], axis=0) for k in range(3))
    return (pay[:half], pay[half : 2 * half]) + coefs


def lon_join(mine, other, right, memb, rest):
    lh1, lh2, la, lb, ld = (jnp.where(right, o, m) for m, o in zip(mine, other))
    rh1, rh2, ra, rb, rd = (jnp.where(right, m, o) for m, o in zip(mine, other))
    inv = 1.0 / (ld + ra)
    ca, cb = lb * inv, rb * inv
    grow = functools.partial(lon_expand, memb=memb, rest=rest)
    total = lh2 + rh1
    joined = (lh1 + grow(ca) * total, rh2 + grow(cb) * total, la - lb * ca, lb * cb, rd - rb * cb)
    return joined, (total * grow(inv), ca, cb)


def lon_join_round(pays, levels, memb, rest):
    half = memb * (8 + rest)
    groups = [lon_parts(p[...], half) for p in pays]
    backs = []
    for level in levels:
        right = on_right("lon", level)
        pairs = [lon_join(groups[k], groups[k + 1], right, memb, rest) for k in range(0, len(groups), 2)]
        groups = [joined for joined, _ in pairs]
        backs.append(pairs[0][1])
    return groups[0], backs


def on_right(axis, level):
    return ((lax.axis_index(axis) >> level) & 1) == 1


def lon_merge_kernel(*refs, levels, memb, rest):
    pays, (pay_ref, *back_refs) = refs[: 1 << len(levels)], refs[1 << len(levels) :]
    (h1, h2, a, b, d), backs = lon_join_round(pays, levels, memb, rest)
    half = h1.shape[0]
    pay_ref[:half, :] = h1
    pay_ref[half : 2 * half, :] = h2
    pay_ref[2 * half :, :] = lon_coef_tile([(a[:8], b[:8], d[:8]), (a[8:], b[8:], d[8:])], rest)
    for back_ref, (s, ca, cb) in zip(back_refs, backs):
        back_ref[:half, :] = s
        back_ref[half : half + 16, :] = ca
        back_ref[half + 16 :, :] = cb


def times_inverse(rows, weights):
    high = rows.astype(jnp.bfloat16)
    low = (rows - high.astype(F32)).astype(jnp.bfloat16)
    out = jnp.dot(jnp.concatenate([high, low], axis=1), weights, preferred_element_type=F32)
    return out[:, :LANES] + out[:, LANES:]


def vertical_kernel(diag_ref, sub_ref, part_ref, y_ref, weights_ref, line, ratio, inverse, factor, *, stride, rows):
    levels = diag_ref.shape[1]
    line[...] = jnp.zeros_like(line)
    line[0:1, 0 : levels - 1] = sub_ref[...]
    row_ids = lax.broadcasted_iota(jnp.int32, (levels, levels), 0)
    col_ids = lax.broadcasted_iota(jnp.int32, (levels, levels), 1)
    diag = jnp.sum(jnp.where(row_ids == col_ids, diag_ref[...], 0.0), axis=1, keepdims=True)
    below = jnp.sum(jnp.where(row_ids == col_ids + 1, line[0:1, :], 0.0), axis=1, keepdims=True)
    inv = 1.0 / jnp.broadcast_to(diag, (levels, levels))
    inverse[...] = inv
    ratio[...] = -jnp.broadcast_to(below, (levels, levels)) * inv
    lane = lax.broadcasted_iota(jnp.int32, (1, levels), 1)
    row = jnp.zeros((1, levels), F32)
    for i in range(levels):
        row = jnp.where(lane == i, inverse[i : i + 1, :], row * ratio[i : i + 1, :])
        factor[i : i + 1, :] = row
    low_inv = factor[...]
    full = jnp.dot(low_inv.T, low_inv, preferred_element_type=F32, precision=lax.Precision.HIGHEST)
    high = full.astype(jnp.bfloat16)
    low = (full - high.astype(F32)).astype(jnp.bfloat16)
    weights_ref[0:levels, 0:levels] = high
    weights_ref[0:levels, levels:] = low
    weights_ref[levels:, 0:levels] = high
    weights_ref[levels:, levels:] = jnp.zeros_like(low)
    weights = weights_ref[...]
    cells = part_ref.shape[0]
    for c in range(0, cells, 16):
        y = times_inverse(part_ref[c : c + 16].reshape(256, LANES), weights)
        for k in range(16):
            y_ref[pl.ds(c + k, 8, stride=stride), :] = y[16 * k : 16 * k + 8]
            y_ref[pl.ds(8 * stride + c + k, rows - 8, stride=stride), :] = y[16 * k + 8 : 16 * k + rows]


def spread(out_ref, tiles, i, memb, stride, rows):
    for m in range(memb):
        out_ref[pl.ds(i * memb + m, 8, stride=stride), :] = tiles[0]
        out_ref[pl.ds(8 * stride + i * memb + m, rows - 8, stride=stride), :] = tiles[1][: rows - 8]


def expand_kernel(phi_ref, psi_ref, phi_out, psi_out, *, memb, stride, rows):
    for i in range(phi_ref.shape[0]):
        for src, dst in ((phi_ref, phi_out), (psi_ref, psi_out)):
            spread(dst, (src[i, 0:8, :], src[i, 8:16, :]), i, memb, stride, rows)


def lat_coef_kernel(diff_ref, step_out, phi_out, psi_out, coef_out, small_out, cos_out, *, memb, stride, bands):
    rows, cols = diff_ref.shape
    cells = cols * memb
    band = lax.axis_index("lat")
    row_ids = lax.broadcasted_iota(jnp.int32, (rows, cols), 0)
    last = jnp.logical_and(row_ids == rows - 1, band == bands - 1)
    step = split_rows(jnp.where(last, 0.0, 1.0 / diff_ref[...]))
    for i in range(cols):
        spread(step_out, [lane_of(s, i, 8) for s in step], i, memb, stride, rows)
    tile_ids = lax.broadcasted_iota(jnp.int32, (16, LANES), 0) + band * rows
    cosine = jnp.cos(-jnp.pi / 2 + (tile_ids.astype(F32) + 0.5) * jnp.pi / (bands * rows))
    cos_out[...] = cosine
    acc = [jnp.zeros((8, LANES), F32) for _ in range(3)]
    lane = lax.broadcasted_iota(jnp.int32, (PART, LANES), 1)
    for c in range(0, cells, PART):
        phi = jnp.ones((PART, LANES), F32)
        psi = jnp.zeros((PART, LANES), F32)
        phi_f, psi_f = psi, phi
        for j in range(rows):
            cos_j = jnp.broadcast_to(cosine[j : j + 1, :], (PART, LANES))
            t = step_out[j * stride + c : j * stride + c + PART, :]
            now_phi, now_psi = cos_j * phi, cos_j * psi
            phi_out[j * cells + c : j * cells + c + PART, :] = now_phi
            psi_out[j * cells + c : j * cells + c + PART, :] = now_psi
            phi_f = phi_f + now_phi
            psi_f = psi_f + now_psi
            phi = phi + t * phi_f
            psi = psi + t * psi_f
        b = 1.0 / psi
        picked = lax.broadcasted_iota(jnp.int32, (PART, LANES), 0) + c == lane * memb
        for k, value in enumerate((phi * b, b, psi_f * b)):
            coef_out[k * cells + c : k * cells + c + PART, :] = value
            chosen = jnp.where(picked, value, 0.0)
            for r in range(0, PART, 8):
                acc[k] = acc[k] + chosen[r : r + 8]
    small_out[...] = pack_small([jnp.sum(a, axis=0, keepdims=True) for a in acc])


def pack_small(lines):
    tile = lax.broadcasted_iota(jnp.int32, (8, LANES), 0)
    out = jnp.zeros((8, LANES), F32)
    for k, line in enumerate(lines):
        out = jnp.where(tile == k, jnp.broadcast_to(line, (8, LANES)), out)
    return out


def lon_close_kernel(*refs, levels, memb, rest):
    count = 1 << len(levels)
    own_ref, pays, backs = refs[0], refs[1 : 1 + count], refs[1 + count : 1 + count + levels[0]]
    weights_ref, *refs = refs[1 + count + levels[0] :]
    rows = 8 + rest
    half = memb * rows
    grow = functools.partial(lon_expand, memb=memb, rest=rest)
    (h1, h2, a, b, d), last = lon_join_round(pays, levels, memb, rest)
    u_in = -(h1 + h2) * grow(1.0 / (a + d - 2.0 * b))
    u_out = u_in
    stored = [(back[:half, :], back[half : half + 16, :], back[half + 16 :, :]) for back in backs]
    for level, (s, ca, cb) in reversed(list(enumerate(stored + last))):
        middle = grow(ca) * u_in + grow(cb) * u_out - s
        right = on_right("lon", level)
        u_in, u_out = jnp.where(right, middle, u_in), jnp.where(right, u_out, middle)
    oh1, _, oa, ob, _ = lon_parts(own_ref[...], half)
    f_in = grow(ob) * u_out - grow(oa) * u_in - oh1
    ends = times_inverse(jnp.concatenate([u_in, f_in], axis=0), weights_ref[...])
    full = jnp.concatenate([ends, jnp.zeros((LANES - 2 * half, LANES), F32)], axis=0)
    if len(refs) == 1:
        refs[0][...] = full
        return
    response_ref, part_ref, ends_ref, sum_ref = refs
    ends_ref[...] = full
    high = full.astype(jnp.bfloat16)
    low = (full - high.astype(F32)).astype(jnp.bfloat16)
    table = jnp.concatenate(
        [jnp.concatenate([high, low], axis=1), jnp.concatenate([high, jnp.zeros_like(low)], axis=1)], axis=0
    )
    out = jnp.dot(response_ref[...], table, preferred_element_type=F32)
    sum_ref[...] = part_ref[...] + (out[:, :LANES] + out[:, LANES:])


def lat_sweep_kernel(
    ends, y_ref, phi_ref, psi_ref, step_ref, coef_ref, small_ref, cos_ref, q_ref, pay_ref, tiles, *, memb, stride
):
    rows = step_ref.shape[0] // stride - 1
    rest, half = rows - 8, memb * rows
    for k in range(2):
        for j in range(rows):
            if j < 8:
                value = ends[pl.ds(k * half + j, memb, stride=8), :]
            else:
                value = ends[pl.ds(k * half + 8 * memb + j - 8, memb, stride=rest), :]
            tiles[8 * (k * rows + j) : 8 * (k * rows + j) + 8, :] = jnp.concatenate([value] * (8 // memb), axis=0)
    cells = coef_ref.shape[0] // 3
    for c in range(0, cells, PART):
        v = jnp.zeros((PART, LANES), F32)
        flux = v
        for j in range(rows):
            at = slice(j * stride + c, j * stride + c + PART)
            u_tile = jnp.concatenate([tiles[8 * j : 8 * j + 8, :]] * (PART // 8), axis=0)
            f_tile = jnp.concatenate([tiles[8 * (rows + j) : 8 * (rows + j) + 8, :]] * (PART // 8), axis=0)
            u = y_ref[at, :] + phi_ref[at, :] * u_tile + psi_ref[at, :] * f_tile
            now = jnp.broadcast_to(cos_ref[j : j + 1, :], (PART, LANES)) * v
            q_ref[j * cells + c : j * cells + c + PART, :] = now
            flux = flux + (now - u)
            v = v + step_ref[at, :] * flux
        b = coef_ref[cells + c : cells + c + PART, :]
        d = coef_ref[2 * cells + c : 2 * cells + c + PART, :]
        pay_ref[c : c + PART, :] = v * b
        pay_ref[cells + c : cells + c + PART, :] = flux - d * v
    pay_ref[2 * cells :, :] = small_ref[...]


def unpack_small(tile, k, c, memb):
    row = lax.broadcasted_iota(jnp.int32, (PART, LANES), 0) + c
    lane = lax.broadcasted_iota(jnp.int32, (PART, LANES), 1) * memb
    mask = jnp.logical_and(row >= lane, row < lane + memb)
    line = jnp.broadcast_to(tile[k : k + 1, :], (PART, LANES))
    return jnp.broadcast_to(jnp.sum(jnp.where(mask, line, 0.0), axis=1, keepdims=True), (PART, LANES))


def lat_merge_kernel(mine_ref, coef_ref, other_ref, *outs, level, levels, memb, send=True):
    ready = level == levels - 2
    if not send:
        back_ref, end_ref = outs
    elif ready:
        pay_ref, back_ref, end_ref = outs
    else:
        pay_ref, back_ref, next_ref = outs
    cells = coef_ref.shape[0] // 3
    right = on_right("lat", level)
    upper = on_right("lat", level + 1)
    small = other_ref[2 * cells :, :]
    acc = [jnp.zeros((8, LANES), F32) for _ in range(3)]
    for c in range(0, cells, PART):
        at = slice(c, c + PART)
        lo, mid, hi = (slice(k * cells + c, k * cells + c + PART) for k in range(3))
        mine = [mine_ref[lo, :], mine_ref[mid, :], coef_ref[lo, :], coef_ref[mid, :], coef_ref[hi, :]]
        other = [other_ref[lo, :], other_ref[mid, :]] + [unpack_small(small, k, c, memb) for k in range(3)]
        lh1, lh2, la, lb, ld = (jnp.where(right, o, m) for m, o in zip(mine, other))
        rh1, rh2, ra, rb, rd = (jnp.where(right, m, o) for m, o in zip(mine, other))
        inv = 1.0 / (ld + ra)
        ca, cb = lb * inv, rb * inv
        total = lh2 + rh1
        back_ref[lo, :] = total * inv
        back_ref[mid, :] = ca
        back_ref[hi, :] = cb
        h1, h2 = lh1 + ca * total, rh2 + cb * total
        a, b, d = la - lb * ca, lb * cb, rd - rb * cb
        picked = lax.broadcasted_iota(jnp.int32, (PART, LANES), 0) + c == lax.broadcasted_iota(
            jnp.int32, (PART, LANES), 1
        ) * memb
        if ready:
            free, tied = jnp.where(upper, d, a), jnp.where(upper, a, d)
            h_free, h_tied = jnp.where(upper, h2, h1), jnp.where(upper, h1, h2)
            free_inv = 1.0 / free
            lean = b * free_inv
            end_ref[lo, :] = lean
            end_ref[mid, :] = h_free * free_inv
            if not send:
                continue
            pay_ref[at, :] = h_tied + lean * h_free
            values = (tied - b * lean,)
        else:
            pay_ref[lo, :] = h1
            pay_ref[mid, :] = h2
            values = (a, b, d)
            for k, value in enumerate(values):
                next_ref[k * cells + c : k * cells + c + PART, :] = value
        for k, value in enumerate(values):
            chosen = jnp.where(picked, value, 0.0)
            for r in range(0, PART, 8):
                acc[k] = acc[k] + chosen[r : r + 8]
    if not send:
        return
    lines = [jnp.sum(x, axis=0, keepdims=True) for x in acc[: 1 if ready else 3]]
    pay_ref[cells * (1 if ready else 2) :, :] = pack_small(lines)


def lat_pair_kernel(coef_ref, other_ref, weight_ref, small_ref, *, memb):
    cells = coef_ref.shape[0] // 3
    right, upper = on_right("lat", 0), on_right("lat", 1)
    small = other_ref[...]
    acc = jnp.zeros((8, LANES), F32)
    one = jnp.ones((PART, LANES), F32)
    for c in range(0, cells, PART):
        lo, mid, hi = (slice(k * cells + c, k * cells + c + PART) for k in range(3))
        mine = [coef_ref[lo, :], coef_ref[mid, :], coef_ref[hi, :]]
        other = [unpack_small(small, k, c, memb) for k in range(3)]
        la, lb, ld = (jnp.where(right, o, m) for m, o in zip(mine, other))
        ra, rb, rd = (jnp.where(right, m, o) for m, o in zip(mine, other))
        inv = 1.0 / (ld + ra)
        ca, cb = lb * inv, rb * inv
        a, b, d = la - lb * ca, lb * cb, rd - rb * cb
        free, tied = jnp.where(upper, d, a), jnp.where(upper, a, d)
        lean = b / free
        shared = jnp.where(upper, ca + lean * cb, cb + lean * ca)
        own = jnp.where(right == upper, lean, one)
        weight_ref[lo, :] = jnp.where(right, shared, own)
        weight_ref[mid, :] = jnp.where(right, own, shared)
        acc = pick_small(acc, tied - b * lean, c, memb)
    small_ref[...] = pack_small([jnp.sum(acc, axis=0, keepdims=True)])


def sum_weights(weight_ref, coef_ref, c):
    cells = coef_ref.shape[0] // 3
    e1, e2 = (weight_ref[k * cells + c : k * cells + c + PART, :] for k in range(2))
    b, d = (coef_ref[k * cells + c : k * cells + c + PART, :] for k in (1, 2))
    return e1 * b - e2 * d, e2


def lat_response_kernel(step_ref, phi_ref, psi_ref, coef_ref, cos_ref, weight_ref, out_ref, *, memb, stride):
    cells = coef_ref.shape[0] // 3
    rows = step_ref.shape[0] // stride - 1
    rest, half = rows - 8, memb * rows
    lane = lax.broadcasted_iota(jnp.int32, (8, LANES), 1)
    member = lax.broadcasted_iota(jnp.int32, (8, LANES), 0) % memb
    for c in range(0, cells, PART):
        value, flux = sum_weights(weight_ref, coef_ref, c)
        tiles = [jnp.zeros((8, LANES), F32)] * (PART // 8)
        for j in reversed(range(rows)):
            at = slice(j * stride + c, j * stride + c + PART)
            flux = flux + step_ref[at, :] * value
            value = value + jnp.broadcast_to(cos_ref[j : j + 1, :], (PART, LANES)) * flux
            for end, source in enumerate((phi_ref, psi_ref)):
                first = end * half + (j if j < 8 else 8 * memb + j - 8)
                mask = lane == first + member * (8 if j < 8 else rest)
                entry = flux * source[at, :]
                tiles = [jnp.where(mask, entry[8 * r : 8 * r + 8], tile) for r, tile in enumerate(tiles)]
        full = -jnp.concatenate(tiles, axis=0)
        high = full.astype(jnp.bfloat16)
        out_ref[c : c + PART, :LANES] = high
        out_ref[c : c + PART, LANES:] = (full - high.astype(F32)).astype(jnp.bfloat16)


def lat_own_kernel(y_ref, step_ref, coef_ref, cos_ref, weight_ref, out_ref, *, stride):
    cells = coef_ref.shape[0] // 3
    rows = step_ref.shape[0] // stride - 1
    for c in range(0, cells, PART):
        v = jnp.zeros((PART, LANES), F32)
        flux = v
        for j in range(rows):
            at = slice(j * stride + c, j * stride + c + PART)
            flux = flux + (jnp.broadcast_to(cos_ref[j : j + 1, :], (PART, LANES)) * v - y_ref[at, :])
            v = v + step_ref[at, :] * flux
        of_value, of_flux = sum_weights(weight_ref, coef_ref, c)
        out_ref[c : c + PART, :] = of_value * v + of_flux * flux


def pick_small(acc, value, c, memb):
    row = lax.broadcasted_iota(jnp.int32, (PART, LANES), 0) + c
    chosen = jnp.where(row == lax.broadcasted_iota(jnp.int32, (PART, LANES), 1) * memb, value, 0.0)
    for r in range(0, PART, 8):
        acc = acc + chosen[r : r + 8]
    return acc


def lat_add_kernel(mine_ref, other_ref, small_ref, pay_ref):
    cells = mine_ref.shape[0]
    pay_ref[:cells, :] = mine_ref[...] + other_ref[...]
    pay_ref[cells:, :] = small_ref[...]


def finish_kernel(*refs, levels, memb):
    own_ref, coef_ref, mine_ref, other_ref, end_ref = refs[:5]
    backs = refs[5 : 5 + levels - 1]
    q_ref, phi_ref, psi_ref, out_hbm, out, middles, sem = refs[5 + levels - 1 :]
    cells = coef_ref.shape[0] // 3
    rows = q_ref.shape[0] // cells
    upper = on_right("lat", levels - 1)
    soft = 1.0 / (mine_ref[cells:, :] + other_ref[cells:, :])
    for c in range(0, cells, PART):
        middles[c : c + PART, :] = -(mine_ref[c : c + PART, :] + other_ref[c : c + PART, :]) * unpack_small(
            soft, 0, c, memb
        )

    def chunk_copy(k):
        at = pl.ds(pl.multiple_of(k * BLOCK, BLOCK), BLOCK)
        return pltpu.make_async_copy(out.at[:, at, :], out_hbm.at[:, at, :], sem.at[k])

    @pl.loop(0, cells // BLOCK)
    def _(k):
        c = pl.multiple_of(k * BLOCK, BLOCK)
        lo, mid, hi = (pl.ds(pl.multiple_of(p * cells + c, BLOCK), BLOCK) for p in range(3))
        middle = middles[lo, :]
        outer = end_ref[lo, :] * middle - end_ref[mid, :]
        u_in, u_out = jnp.where(upper, middle, outer), jnp.where(upper, outer, middle)
        for level in reversed(range(levels - 1)):
            back = backs[level]
            middle = back[mid, :] * u_in + back[hi, :] * u_out - back[lo, :]
            right = on_right("lat", level)
            u_in, u_out = jnp.where(right, middle, u_in), jnp.where(right, u_out, middle)
        flux = coef_ref[mid, :] * u_out - coef_ref[lo, :] * u_in - own_ref[lo, :]
        for j in range(rows):
            at = pl.ds(pl.multiple_of(j * cells + c, BLOCK), BLOCK)
            out[j, lo, :] = q_ref[at, :] + phi_ref[at, :] * u_in + psi_ref[at, :] * flux
        chunk_copy(k).start()

    for k in range(cells // BLOCK):
        chunk_copy(k).wait()


def swapped(value, axis, mask):
    return lax.ppermute(value, axis, [(s, s ^ mask) for s in range(lax.axis_size(axis))])


def shards(ensemble, grad_increment, normalization, lon_diffusion, lat_diffusion, vert_diag, vert_sub):
    rows, cols, memb, lev = ensemble.shape
    bands, blocks = lax.axis_size("lat"), lax.axis_size("lon")
    lat_levels, lon_levels = levels_of(bands), levels_of(blocks)
    assert lev == LANES and 8 < rows <= 16 and 8 % memb == 0 and cols <= LANES and cols % CHUNK == 0
    assert 2**lat_levels == bands and 2**lon_levels == blocks and lat_levels >= 2 and lon_levels >= 2
    rest, cells = rows - 8, cols * memb
    assert 8 % rest == 0 and memb * rest % 8 == 0 and cells % PART == 0
    stride = cells + 1
    spaced = -(-(rows + 1) * stride // 8) * 8
    half = memb * rows
    hbm_spec = pl.BlockSpec(memory_space=pltpu.HBM)

    part, phi_t, psi_t, pay = call(
        lon_sweep_kernel,
        (shape(cells, 16, LANES), shape(cols, 16, LANES), shape(cols, 16, LANES), shape(2 * half + 8, LANES)),
        scratch=[
            pltpu.VMEM((cells, 16, LANES), F32),
            pltpu.VMEM((cols, 16, LANES), F32),
            pltpu.VMEM((rows, cols), F32),
            pltpu.VMEM((rows, cols), F32),
            pltpu.VMEM((cols, 16, LANES), F32),
            pltpu.VMEM((cols, 16, LANES), F32),
            pltpu.SemaphoreType.DMA((2 * (cols // CHUNK) + 2,)),
        ],
        in_specs=[hbm_spec] * 4,
        cost=cost(2),
    )(*(in_hbm(x) for x in (ensemble.reshape(rows, cells, lev), grad_increment, normalization, lon_diffusion)))

    own, backs = pay, []
    paired = lat_levels == 2
    spans = lon_rounds(lon_levels)
    for index, span in enumerate(spans):
        others = []
        for k in range(1, 1 << len(span)):
            others.append(swapped(pay, "lon", k << span[0]))
        if index == 0:
            step, lat_phi, lat_psi, coef, small, cosine = call(
                functools.partial(lat_coef_kernel, memb=memb, stride=stride, bands=bands),
                (
                    shape(spaced, LANES),
                    shape(rows * cells, LANES),
                    shape(rows * cells, LANES),
                    shape(3 * cells, LANES),
                    shape(8, LANES),
                    shape(16, LANES),
                ),
                cost=cost(1),
            )(lat_diffusion)
            phi, psi = call(
                functools.partial(expand_kernel, memb=memb, stride=stride, rows=rows),
                (shape(spaced, LANES), shape(spaced, LANES)),
                cost=cost(1),
            )(phi_t, psi_t)
            if paired:
                pair_weight, pair_small = call(
                    functools.partial(lat_pair_kernel, memb=memb),
                    (shape(2 * cells, LANES), shape(8, LANES)),
                    cost=cost(1),
                )(coef, swapped(small, "lat", 1))
                response = call(
                    functools.partial(lat_response_kernel, memb=memb, stride=stride),
                    shape(cells, 2 * LANES, dtype=jnp.bfloat16),
                    cost=cost(1),
                )(step, phi, psi, coef, cosine, pair_weight)
            else:
                response = small
            others, phi, psi, lat_phi, lat_psi, response = lax.optimization_barrier(
                (others, phi, psi, lat_phi, lat_psi, response)
            )
        elif index == 1:
            pay, part = lax.optimization_barrier((pay, part))
            y, weights = call(
                functools.partial(vertical_kernel, stride=stride, rows=rows),
                (shape(spaced, LANES), shape(2 * LANES, 2 * LANES, dtype=jnp.bfloat16)),
                scratch=[pltpu.VMEM((8, LANES), F32)] + [pltpu.VMEM((LANES, LANES), F32)] * 3,
                cost=cost(2),
            )(vert_diag.reshape(1, lev), vert_sub.reshape(1, lev - 1), part)
            own_sum = ()
            if paired:
                own_sum = call(
                    functools.partial(lat_own_kernel, stride=stride), shape(cells, LANES), cost=cost(1)
                )(y, step, coef, cosine, pair_weight)
            others, y, weights, own_sum = lax.optimization_barrier((others, y, weights, own_sum))
        if index < len(spans) - 1:
            pay, *more = call(
                functools.partial(lon_merge_kernel, levels=span, memb=memb, rest=rest),
                (shape(2 * half + 8, LANES),) + (shape(half + 32, LANES),) * len(span),
                cost=cost(1),
            )(pay, *others)
            backs += more
    ends, *sums = call(
        functools.partial(lon_close_kernel, levels=spans[-1], memb=memb, rest=rest),
        (shape(LANES, LANES),) + (shape(cells, LANES),) * paired,
        cost=cost(1),
    )(own, pay, *others, *backs, weights, *(response, own_sum) * paired)

    def sweep(ends):
        return call(
            functools.partial(lat_sweep_kernel, memb=memb, stride=stride),
            (shape(rows * cells, LANES), shape(2 * cells + 8, LANES)),
            scratch=[pltpu.VMEM((16 * rows, LANES), F32)],
            cost=cost(1),
        )(ends, y, phi, psi, step, coef, small, cosine)

    if paired:
        pay = call(lat_add_kernel, shape(cells + 8, LANES), cost=cost(1))(
            sums[0], swapped(sums[0], "lat", 1), pair_small
        )
        final = swapped(pay, "lat", 3)
        behind, _ = lax.optimization_barrier((ends, pay))
        q, lat_pay = sweep(behind)
        inner = swapped(lat_pay, "lat", 1)
        back, group = call(
            functools.partial(lat_merge_kernel, level=0, levels=2, memb=memb, send=False),
            (shape(3 * cells, LANES), shape(2 * cells, LANES)),
            cost=cost(1),
        )(lat_pay, coef, inner)
        lat_backs = [back]
        final, group, back, q = lax.optimization_barrier((final, group, back, q))
    else:
        q, lat_pay = sweep(ends)
        pay, group, lat_backs = lat_pay, coef, []
        for level in range(lat_levels - 1):
            other = swapped(pay, "lat", 1 << level)
            ready = level == lat_levels - 2
            pay, back, group = call(
                functools.partial(lat_merge_kernel, level=level, levels=lat_levels, memb=memb),
                (
                    shape((1 if ready else 2) * cells + 8, LANES),
                    shape(3 * cells, LANES),
                    shape((2 if ready else 3) * cells, LANES),
                ),
                cost=cost(1),
            )(pay, group, other)
            lat_backs.append(back)
        final = swapped(pay, "lat", 1 << (lat_levels - 1) | 1)
    out = call(
        functools.partial(finish_kernel, levels=lat_levels, memb=memb),
        shape(rows, cells, LANES),
        scratch=[
            pltpu.VMEM((rows, cells, LANES), F32),
            pltpu.VMEM((cells, LANES), F32),
            pltpu.SemaphoreType.DMA((cells // BLOCK,)),
        ],
        out_specs=hbm_spec,
        cost=cost(1),
    )(lat_pay, coef, pay, final, group, *lat_backs, q, lat_phi, lat_psi)
    return out.reshape(rows, cols, memb, lev)


def levels_of(count):
    return int(math.log2(count))


def lon_rounds(levels):
    return [tuple(range(k, min(k + 2, levels))) for k in range(0, levels, 2)]


def in_hbm(value):
    return pltpu.with_memory_space_constraint(value, pltpu.HBM)


def cost(microseconds):
    return pl.CostEstimate(flops=0, bytes_accessed=int(microseconds * 3e6), transcendentals=0)


def solution(mesh):
    in_specs = (
        P("lat", "lon", None, None),
        P("lat", "lon", None),
        P("lat", "lon"),
        P("lat", "lon"),
        P("lat", "lon"),
        P(),
        P(),
    )
    out_specs = P("lat", "lon", None, None)
    return jax.shard_map(shards, mesh=mesh, in_specs=in_specs, out_specs=out_specs, check_vma=False)
```

```python
import functools
import math

import jax
import jax.numpy as jnp
from jax import lax
from jax.experimental import pallas as pl
from jax.experimental.pallas import tpu as pltpu
from jax.sharding import PartitionSpec as P


F32 = jnp.float32
LANES = 128
CHUNK = 16
PART = 64
BLOCK = 64
VMEM_BYTES = 16 * 2**20


def call(kernel, outs, scratch=(), in_specs=None, out_specs=None, cost=None):
    specs = {k: v for k, v in (("in_specs", in_specs), ("out_specs", out_specs)) if v is not None}
    return pl.pallas_call(
        kernel,
        out_shape=outs,
        **specs,
        scratch_shapes=scratch,
        cost_estimate=cost,
        compiler_params=pltpu.CompilerParams(vmem_limit_bytes=VMEM_BYTES),
    )


def shape(*dims, dtype=F32):
    return jax.ShapeDtypeStruct(dims, dtype)


def lane_of(value, lane, rows):
    return jnp.broadcast_to(value[:, lane : lane + 1], (rows, LANES))


def split_rows(value):
    rest = value.shape[0] - 8
    fill = jnp.ones((8 - rest, value.shape[1]), F32)
    return value[:8], jnp.concatenate([value[8:], fill], axis=0)


def lon_sweep_kernel(
    ens_hbm,
    grad_hbm,
    norm_hbm,
    diff_hbm,
    part_ref,
    phi_ref,
    psi_ref,
    pay_ref,
    ens,
    grad,
    norm_ref,
    diff_ref,
    step_b,
    norm_b,
    sem,
):
    rows, cells, _ = ens_hbm.shape
    cols = grad_hbm.shape[1]
    memb = cells // cols
    rest = rows - 8
    half = memb * rows
    chunks = cols // CHUNK
    first = pltpu.make_async_copy(diff_hbm, diff_ref, sem.at[2 * chunks])
    second = pltpu.make_async_copy(norm_hbm, norm_ref, sem.at[2 * chunks + 1])
    first.start()
    second.start()
    arrivals = []
    for c in range(chunks):
        g_rows, e_rows = pl.ds(c * CHUNK, CHUNK), pl.ds(c * CHUNK * memb, CHUNK * memb)
        for j in range(rows):
            pltpu.make_async_copy(grad_hbm.at[j, g_rows], grad.at[g_rows, j, :], sem.at[2 * c]).start()
            pltpu.make_async_copy(ens_hbm.at[j, e_rows], ens.at[e_rows, j, :], sem.at[2 * c + 1]).start()
        arrivals.append(
            (
                pltpu.make_async_copy(grad_hbm.at[:, g_rows], grad_hbm.at[:, g_rows], sem.at[2 * c]),
                pltpu.make_async_copy(ens_hbm.at[:, e_rows], ens_hbm.at[:, e_rows], sem.at[2 * c + 1]),
            )
        )
    zero, one = jnp.zeros((8, LANES), F32), jnp.ones((8, LANES), F32)
    tiles = [slice(0, 8), slice(8, 16)]

    first.wait()
    second.wait()
    step = split_rows(1.0 / diff_ref[...])
    norm = split_rows(norm_ref[...])
    phi, phi_f, psi, psi_f = [one] * 2, [zero] * 2, [zero] * 2, [one] * 2
    for i in range(cols):
        for g in range(2):
            t = lane_of(step[g], i, 8)
            step_b[i, tiles[g], :] = t
            norm_b[i, tiles[g], :] = lane_of(norm[g], i, 8)
            phi_ref[i, tiles[g], :] = phi[g]
            psi_ref[i, tiles[g], :] = psi[g]
            phi_f[g] = phi_f[g] + phi[g]
            psi_f[g] = psi_f[g] + psi[g]
            phi[g] = phi[g] + t * phi_f[g]
            psi[g] = psi[g] + t * psi_f[g]
    ends, coefs = [], []
    for g in range(2):
        b = 1.0 / psi[g]
        a, d = phi[g] * b, psi_f[g] * b
        ends.append((b, d))
        coefs.append((a, b, d))
    pay_ref[2 * half :, :] = lon_coef_tile(coefs, rest)

    u = [[zero] * memb for _ in range(2)]
    flux = [[zero] * memb for _ in range(2)]
    for i in range(cols):
        if i % CHUNK == 0:
            for copy in arrivals[i // CHUNK]:
                copy.wait()
        for g in range(2):
            t = step_b[i, tiles[g], :]
            w = norm_b[i, tiles[g], :] * grad[i, tiles[g], :]
            for m in range(memb):
                part_ref[i * memb + m, tiles[g], :] = u[g][m]
                f = w * ens[i * memb + m, tiles[g], :]
                flux[g][m] = flux[g][m] + (u[g][m] - f)
                u[g][m] = u[g][m] + t * flux[g][m]
    for g in range(2):
        b, d = ends[g]
        start = 0 if g == 0 else 8 * memb
        size = 8 if g == 0 else rest
        for m in range(memb):
            at = start + m * size
            pay_ref[at : at + size, :] = (u[g][m] * b)[:size]
            pay_ref[half + at : half + at + size, :] = (flux[g][m] - d * u[g][m])[:size]


def lon_expand(tiles, memb, rest):
    return jnp.concatenate([tiles[:8]] * memb + [tiles[8:]] * (memb * rest // 8), axis=0)


def lon_coef_tile(groups, rest):
    lane = lax.broadcasted_iota(jnp.int32, (8, LANES), 1)
    tile = jnp.zeros((8, LANES), F32)
    for g, group in enumerate(groups):
        for k, value in enumerate(group):
            if g == 1:
                value = jnp.concatenate([value[:rest]] * (8 // rest), axis=0)
            tile = jnp.where(lane == 3 * g + k, value, tile)
    return tile


def lon_parts(pay, half):
    coef = pay[2 * half :]
    coefs = tuple(jnp.concatenate([lane_of(coef, k, 8), lane_of(coef, 3 + k, 8)], axis=0) for k in range(3))
    return (pay[:half], pay[half : 2 * half]) + coefs


def lon_join(mine, other, right, memb, rest):
    lh1, lh2, la, lb, ld = (jnp.where(right, o, m) for m, o in zip(mine, other))
    rh1, rh2, ra, rb, rd = (jnp.where(right, m, o) for m, o in zip(mine, other))
    inv = 1.0 / (ld + ra)
    ca, cb = lb * inv, rb * inv
    grow = functools.partial(lon_expand, memb=memb, rest=rest)
    total = lh2 + rh1
    joined = (lh1 + grow(ca) * total, rh2 + grow(cb) * total, la - lb * ca, lb * cb, rd - rb * cb)
    return joined, (total * grow(inv), ca, cb)


def lon_join_round(pays, levels, memb, rest):
    half = memb * (8 + rest)
    groups = [lon_parts(p[...], half) for p in pays]
    backs = []
    for level in levels:
        right = on_right("lon", level)
        pairs = [lon_join(groups[k], groups[k + 1], right, memb, rest) for k in range(0, len(groups), 2)]
        groups = [joined for joined, _ in pairs]
        backs.append(pairs[0][1])
    return groups[0], backs


def on_right(axis, level):
    return ((lax.axis_index(axis) >> level) & 1) == 1


def lon_merge_kernel(*refs, levels, memb, rest):
    pays, (pay_ref, *back_refs) = refs[: 1 << len(levels)], refs[1 << len(levels) :]
    (h1, h2, a, b, d), backs = lon_join_round(pays, levels, memb, rest)
    half = h1.shape[0]
    pay_ref[:half, :] = h1
    pay_ref[half : 2 * half, :] = h2
    pay_ref[2 * half :, :] = lon_coef_tile([(a[:8], b[:8], d[:8]), (a[8:], b[8:], d[8:])], rest)
    for back_ref, (s, ca, cb) in zip(back_refs, backs):
        back_ref[:half, :] = s
        back_ref[half : half + 16, :] = ca
        back_ref[half + 16 :, :] = cb


def times_inverse(rows, weights):
    high = rows.astype(jnp.bfloat16)
    low = (rows - high.astype(F32)).astype(jnp.bfloat16)
    out = jnp.dot(jnp.concatenate([high, low], axis=1), weights, preferred_element_type=F32)
    return out[:, :LANES] + out[:, LANES:]


def vertical_kernel(diag_ref, sub_ref, part_ref, y_ref, weights_ref, line, ratio, inverse, factor, *, stride, rows):
    levels = diag_ref.shape[1]
    line[...] = jnp.zeros_like(line)
    line[0:1, 0 : levels - 1] = sub_ref[...]
    row_ids = lax.broadcasted_iota(jnp.int32, (levels, levels), 0)
    col_ids = lax.broadcasted_iota(jnp.int32, (levels, levels), 1)
    diag = jnp.sum(jnp.where(row_ids == col_ids, diag_ref[...], 0.0), axis=1, keepdims=True)
    below = jnp.sum(jnp.where(row_ids == col_ids + 1, line[0:1, :], 0.0), axis=1, keepdims=True)
    inv = 1.0 / jnp.broadcast_to(diag, (levels, levels))
    inverse[...] = inv
    ratio[...] = -jnp.broadcast_to(below, (levels, levels)) * inv
    lane = lax.broadcasted_iota(jnp.int32, (1, levels), 1)
    row = jnp.zeros((1, levels), F32)
    for i in range(levels):
        row = jnp.where(lane == i, inverse[i : i + 1, :], row * ratio[i : i + 1, :])
        factor[i : i + 1, :] = row
    low_inv = factor[...]
    full = jnp.dot(low_inv.T, low_inv, preferred_element_type=F32, precision=lax.Precision.HIGHEST)
    high = full.astype(jnp.bfloat16)
    low = (full - high.astype(F32)).astype(jnp.bfloat16)
    weights_ref[0:levels, 0:levels] = high
    weights_ref[0:levels, levels:] = low
    weights_ref[levels:, 0:levels] = high
    weights_ref[levels:, levels:] = jnp.zeros_like(low)
    weights = weights_ref[...]
    cells = part_ref.shape[0]
    for c in range(0, cells, 16):
        y = times_inverse(part_ref[c : c + 16].reshape(256, LANES), weights)
        for k in range(16):
            y_ref[pl.ds(c + k, 8, stride=stride), :] = y[16 * k : 16 * k + 8]
            y_ref[pl.ds(8 * stride + c + k, rows - 8, stride=stride), :] = y[16 * k + 8 : 16 * k + rows]


def spread(out_ref, tiles, i, memb, stride, rows):
    for m in range(memb):
        out_ref[pl.ds(i * memb + m, 8, stride=stride), :] = tiles[0]
        out_ref[pl.ds(8 * stride + i * memb + m, rows - 8, stride=stride), :] = tiles[1][: rows - 8]


def expand_kernel(phi_ref, psi_ref, phi_out, psi_out, *, memb, stride, rows):
    for i in range(phi_ref.shape[0]):
        for src, dst in ((phi_ref, phi_out), (psi_ref, psi_out)):
            spread(dst, (src[i, 0:8, :], src[i, 8:16, :]), i, memb, stride, rows)


def lat_coef_kernel(diff_ref, step_out, phi_out, psi_out, coef_out, small_out, cos_out, *, memb, stride, bands):
    rows, cols = diff_ref.shape
    cells = cols * memb
    band = lax.axis_index("lat")
    row_ids = lax.broadcasted_iota(jnp.int32, (rows, cols), 0)
    last = jnp.logical_and(row_ids == rows - 1, band == bands - 1)
    step = split_rows(jnp.where(last, 0.0, 1.0 / diff_ref[...]))
    for i in range(cols):
        spread(step_out, [lane_of(s, i, 8) for s in step], i, memb, stride, rows)
    tile_ids = lax.broadcasted_iota(jnp.int32, (16, LANES), 0) + band * rows
    cosine = jnp.cos(-jnp.pi / 2 + (tile_ids.astype(F32) + 0.5) * jnp.pi / (bands * rows))
    cos_out[...] = cosine
    acc = [jnp.zeros((8, LANES), F32) for _ in range(3)]
    lane = lax.broadcasted_iota(jnp.int32, (PART, LANES), 1)
    for c in range(0, cells, PART):
        phi = jnp.ones((PART, LANES), F32)
        psi = jnp.zeros((PART, LANES), F32)
        phi_f, psi_f = psi, phi
        for j in range(rows):
            cos_j = jnp.broadcast_to(cosine[j : j + 1, :], (PART, LANES))
            t = step_out[j * stride + c : j * stride + c + PART, :]
            now_phi, now_psi = cos_j * phi, cos_j * psi
            phi_out[j * cells + c : j * cells + c + PART, :] = now_phi
            psi_out[j * cells + c : j * cells + c + PART, :] = now_psi
            phi_f = phi_f + now_phi
            psi_f = psi_f + now_psi
            phi = phi + t * phi_f
            psi = psi + t * psi_f
        b = 1.0 / psi
        picked = lax.broadcasted_iota(jnp.int32, (PART, LANES), 0) + c == lane * memb
        for k, value in enumerate((phi * b, b, psi_f * b)):
            coef_out[k * cells + c : k * cells + c + PART, :] = value
            chosen = jnp.where(picked, value, 0.0)
            for r in range(0, PART, 8):
                acc[k] = acc[k] + chosen[r : r + 8]
    small_out[...] = pack_small([jnp.sum(a, axis=0, keepdims=True) for a in acc])


def pack_small(lines):
    tile = lax.broadcasted_iota(jnp.int32, (8, LANES), 0)
    out = jnp.zeros((8, LANES), F32)
    for k, line in enumerate(lines):
        out = jnp.where(tile == k, jnp.broadcast_to(line, (8, LANES)), out)
    return out


def lon_close_kernel(*refs, levels, memb, rest):
    count = 1 << len(levels)
    own_ref, pays, backs = refs[0], refs[1 : 1 + count], refs[1 + count : 1 + count + levels[0]]
    weights_ref, *refs = refs[1 + count + levels[0] :]
    rows = 8 + rest
    half = memb * rows
    grow = functools.partial(lon_expand, memb=memb, rest=rest)
    (h1, h2, a, b, d), last = lon_join_round(pays, levels, memb, rest)
    u_in = -(h1 + h2) * grow(1.0 / (a + d - 2.0 * b))
    u_out = u_in
    stored = [(back[:half, :], back[half : half + 16, :], back[half + 16 :, :]) for back in backs]
    for level, (s, ca, cb) in reversed(list(enumerate(stored + last))):
        middle = grow(ca) * u_in + grow(cb) * u_out - s
        right = on_right("lon", level)
        u_in, u_out = jnp.where(right, middle, u_in), jnp.where(right, u_out, middle)
    oh1, _, oa, ob, _ = lon_parts(own_ref[...], half)
    f_in = grow(ob) * u_out - grow(oa) * u_in - oh1
    ends = times_inverse(jnp.concatenate([u_in, f_in], axis=0), weights_ref[...])
    full = jnp.concatenate([ends, jnp.zeros((LANES - 2 * half, LANES), F32)], axis=0)
    if len(refs) == 1:
        refs[0][...] = full
        return
    response_ref, part_ref, ends_ref, sum_ref = refs
    ends_ref[...] = full
    high = full.astype(jnp.bfloat16)
    low = (full - high.astype(F32)).astype(jnp.bfloat16)
    table = jnp.concatenate(
        [jnp.concatenate([high, low], axis=1), jnp.concatenate([high, jnp.zeros_like(low)], axis=1)], axis=0
    )
    out = jnp.dot(response_ref[...], table, preferred_element_type=F32)
    sum_ref[...] = part_ref[...] + (out[:, :LANES] + out[:, LANES:])


def lat_sweep_kernel(
    ends, y_ref, phi_ref, psi_ref, step_ref, coef_ref, small_ref, cos_ref, q_ref, pay_ref, tiles, *, memb, stride
):
    rows = step_ref.shape[0] // stride - 1
    rest, half = rows - 8, memb * rows
    for k in range(2):
        for j in range(rows):
            if j < 8:
                value = ends[pl.ds(k * half + j, memb, stride=8), :]
            else:
                value = ends[pl.ds(k * half + 8 * memb + j - 8, memb, stride=rest), :]
            tiles[8 * (k * rows + j) : 8 * (k * rows + j) + 8, :] = jnp.concatenate([value] * (8 // memb), axis=0)
    cells = coef_ref.shape[0] // 3
    for c in range(0, cells, PART):
        v = jnp.zeros((PART, LANES), F32)
        flux = v
        for j in range(rows):
            at = slice(j * stride + c, j * stride + c + PART)
            u_tile = jnp.concatenate([tiles[8 * j : 8 * j + 8, :]] * (PART // 8), axis=0)
            f_tile = jnp.concatenate([tiles[8 * (rows + j) : 8 * (rows + j) + 8, :]] * (PART // 8), axis=0)
            u = y_ref[at, :] + phi_ref[at, :] * u_tile + psi_ref[at, :] * f_tile
            now = jnp.broadcast_to(cos_ref[j : j + 1, :], (PART, LANES)) * v
            q_ref[j * cells + c : j * cells + c + PART, :] = now
            flux = flux + (now - u)
            v = v + step_ref[at, :] * flux
        b = coef_ref[cells + c : cells + c + PART, :]
        d = coef_ref[2 * cells + c : 2 * cells + c + PART, :]
        pay_ref[c : c + PART, :] = v * b
        pay_ref[cells + c : cells + c + PART, :] = flux - d * v
    pay_ref[2 * cells :, :] = small_ref[...]


def unpack_small(tile, k, c, memb):
    row = lax.broadcasted_iota(jnp.int32, (PART, LANES), 0) + c
    lane = lax.broadcasted_iota(jnp.int32, (PART, LANES), 1) * memb
    mask = jnp.logical_and(row >= lane, row < lane + memb)
    line = jnp.broadcast_to(tile[k : k + 1, :], (PART, LANES))
    return jnp.broadcast_to(jnp.sum(jnp.where(mask, line, 0.0), axis=1, keepdims=True), (PART, LANES))


def lat_merge_kernel(mine_ref, coef_ref, other_ref, *outs, level, levels, memb, send=True):
    ready = level == levels - 2
    if not send:
        back_ref, end_ref = outs
    elif ready:
        pay_ref, back_ref, end_ref = outs
    else:
        pay_ref, back_ref, next_ref = outs
    cells = coef_ref.shape[0] // 3
    right = on_right("lat", level)
    upper = on_right("lat", level + 1)
    small = other_ref[2 * cells :, :]
    acc = [jnp.zeros((8, LANES), F32) for _ in range(3)]
    for c in range(0, cells, PART):
        at = slice(c, c + PART)
        lo, mid, hi = (slice(k * cells + c, k * cells + c + PART) for k in range(3))
        mine = [mine_ref[lo, :], mine_ref[mid, :], coef_ref[lo, :], coef_ref[mid, :], coef_ref[hi, :]]
        other = [other_ref[lo, :], other_ref[mid, :]] + [unpack_small(small, k, c, memb) for k in range(3)]
        lh1, lh2, la, lb, ld = (jnp.where(right, o, m) for m, o in zip(mine, other))
        rh1, rh2, ra, rb, rd = (jnp.where(right, m, o) for m, o in zip(mine, other))
        inv = 1.0 / (ld + ra)
        ca, cb = lb * inv, rb * inv
        total = lh2 + rh1
        back_ref[lo, :] = total * inv
        back_ref[mid, :] = ca
        back_ref[hi, :] = cb
        h1, h2 = lh1 + ca * total, rh2 + cb * total
        a, b, d = la - lb * ca, lb * cb, rd - rb * cb
        picked = lax.broadcasted_iota(jnp.int32, (PART, LANES), 0) + c == lax.broadcasted_iota(
            jnp.int32, (PART, LANES), 1
        ) * memb
        if ready:
            free, tied = jnp.where(upper, d, a), jnp.where(upper, a, d)
            h_free, h_tied = jnp.where(upper, h2, h1), jnp.where(upper, h1, h2)
            free_inv = 1.0 / free
            lean = b * free_inv
            end_ref[lo, :] = lean
            end_ref[mid, :] = h_free * free_inv
            if not send:
                continue
            pay_ref[at, :] = h_tied + lean * h_free
            values = (tied - b * lean,)
        else:
            pay_ref[lo, :] = h1
            pay_ref[mid, :] = h2
            values = (a, b, d)
            for k, value in enumerate(values):
                next_ref[k * cells + c : k * cells + c + PART, :] = value
        for k, value in enumerate(values):
            chosen = jnp.where(picked, value, 0.0)
            for r in range(0, PART, 8):
                acc[k] = acc[k] + chosen[r : r + 8]
    if not send:
        return
    lines = [jnp.sum(x, axis=0, keepdims=True) for x in acc[: 1 if ready else 3]]
    pay_ref[cells * (1 if ready else 2) :, :] = pack_small(lines)


def lat_pair_kernel(coef_ref, other_ref, weight_ref, small_ref, *, memb):
    cells = coef_ref.shape[0] // 3
    right, upper = on_right("lat", 0), on_right("lat", 1)
    small = other_ref[...]
    acc = jnp.zeros((8, LANES), F32)
    one = jnp.ones((PART, LANES), F32)
    for c in range(0, cells, PART):
        lo, mid, hi = (slice(k * cells + c, k * cells + c + PART) for k in range(3))
        mine = [coef_ref[lo, :], coef_ref[mid, :], coef_ref[hi, :]]
        other = [unpack_small(small, k, c, memb) for k in range(3)]
        la, lb, ld = (jnp.where(right, o, m) for m, o in zip(mine, other))
        ra, rb, rd = (jnp.where(right, m, o) for m, o in zip(mine, other))
        inv = 1.0 / (ld + ra)
        ca, cb = lb * inv, rb * inv
        a, b, d = la - lb * ca, lb * cb, rd - rb * cb
        free, tied = jnp.where(upper, d, a), jnp.where(upper, a, d)
        lean = b / free
        shared = jnp.where(upper, ca + lean * cb, cb + lean * ca)
        own = jnp.where(right == upper, lean, one)
        weight_ref[lo, :] = jnp.where(right, shared, own)
        weight_ref[mid, :] = jnp.where(right, own, shared)
        acc = pick_small(acc, tied - b * lean, c, memb)
    small_ref[...] = pack_small([jnp.sum(acc, axis=0, keepdims=True)])


def sum_weights(weight_ref, coef_ref, c):
    cells = coef_ref.shape[0] // 3
    e1, e2 = (weight_ref[k * cells + c : k * cells + c + PART, :] for k in range(2))
    b, d = (coef_ref[k * cells + c : k * cells + c + PART, :] for k in (1, 2))
    return e1 * b - e2 * d, e2


def lat_response_kernel(step_ref, phi_ref, psi_ref, coef_ref, cos_ref, weight_ref, out_ref, *, memb, stride):
    cells = coef_ref.shape[0] // 3
    rows = step_ref.shape[0] // stride - 1
    rest, half = rows - 8, memb * rows
    lane = lax.broadcasted_iota(jnp.int32, (8, LANES), 1)
    member = lax.broadcasted_iota(jnp.int32, (8, LANES), 0) % memb
    for c in range(0, cells, PART):
        value, flux = sum_weights(weight_ref, coef_ref, c)
        tiles = [jnp.zeros((8, LANES), F32)] * (PART // 8)
        for j in reversed(range(rows)):
            at = slice(j * stride + c, j * stride + c + PART)
            flux = flux + step_ref[at, :] * value
            value = value + jnp.broadcast_to(cos_ref[j : j + 1, :], (PART, LANES)) * flux
            for end, source in enumerate((phi_ref, psi_ref)):
                first = end * half + (j if j < 8 else 8 * memb + j - 8)
                mask = lane == first + member * (8 if j < 8 else rest)
                entry = flux * source[at, :]
                tiles = [jnp.where(mask, entry[8 * r : 8 * r + 8], tile) for r, tile in enumerate(tiles)]
        full = -jnp.concatenate(tiles, axis=0)
        high = full.astype(jnp.bfloat16)
        out_ref[c : c + PART, :LANES] = high
        out_ref[c : c + PART, LANES:] = (full - high.astype(F32)).astype(jnp.bfloat16)


def lat_own_kernel(y_ref, step_ref, coef_ref, cos_ref, weight_ref, out_ref, *, stride):
    cells = coef_ref.shape[0] // 3
    rows = step_ref.shape[0] // stride - 1
    for c in range(0, cells, PART):
        v = jnp.zeros((PART, LANES), F32)
        flux = v
        for j in range(rows):
            at = slice(j * stride + c, j * stride + c + PART)
            flux = flux + (jnp.broadcast_to(cos_ref[j : j + 1, :], (PART, LANES)) * v - y_ref[at, :])
            v = v + step_ref[at, :] * flux
        of_value, of_flux = sum_weights(weight_ref, coef_ref, c)
        out_ref[c : c + PART, :] = of_value * v + of_flux * flux


def pick_small(acc, value, c, memb):
    row = lax.broadcasted_iota(jnp.int32, (PART, LANES), 0) + c
    chosen = jnp.where(row == lax.broadcasted_iota(jnp.int32, (PART, LANES), 1) * memb, value, 0.0)
    for r in range(0, PART, 8):
        acc = acc + chosen[r : r + 8]
    return acc


def lat_add_kernel(mine_ref, other_ref, small_ref, pay_ref):
    cells = mine_ref.shape[0]
    pay_ref[:cells, :] = mine_ref[...] + other_ref[...]
    pay_ref[cells:, :] = small_ref[...]


def finish_kernel(*refs, levels, memb):
    own_ref, coef_ref, mine_ref, other_ref, end_ref = refs[:5]
    backs = refs[5 : 5 + levels - 1]
    q_ref, phi_ref, psi_ref, out_hbm, out, middles, sem = refs[5 + levels - 1 :]
    cells = coef_ref.shape[0] // 3
    rows = q_ref.shape[0] // cells
    upper = on_right("lat", levels - 1)
    soft = 1.0 / (mine_ref[cells:, :] + other_ref[cells:, :])
    for c in range(0, cells, PART):
        middles[c : c + PART, :] = -(mine_ref[c : c + PART, :] + other_ref[c : c + PART, :]) * unpack_small(
            soft, 0, c, memb
        )

    def chunk_copy(k):
        at = pl.ds(pl.multiple_of(k * BLOCK, BLOCK), BLOCK)
        return pltpu.make_async_copy(out.at[:, at, :], out_hbm.at[:, at, :], sem.at[k])

    @pl.loop(0, cells // BLOCK)
    def _(k):
        c = pl.multiple_of(k * BLOCK, BLOCK)
        lo, mid, hi = (pl.ds(pl.multiple_of(p * cells + c, BLOCK), BLOCK) for p in range(3))
        middle = middles[lo, :]
        outer = end_ref[lo, :] * middle - end_ref[mid, :]
        u_in, u_out = jnp.where(upper, middle, outer), jnp.where(upper, outer, middle)
        for level in reversed(range(levels - 1)):
            back = backs[level]
            middle = back[mid, :] * u_in + back[hi, :] * u_out - back[lo, :]
            right = on_right("lat", level)
            u_in, u_out = jnp.where(right, middle, u_in), jnp.where(right, u_out, middle)
        flux = coef_ref[mid, :] * u_out - coef_ref[lo, :] * u_in - own_ref[lo, :]
        for j in range(rows):
            at = pl.ds(pl.multiple_of(j * cells + c, BLOCK), BLOCK)
            out[j, lo, :] = q_ref[at, :] + phi_ref[at, :] * u_in + psi_ref[at, :] * flux
        chunk_copy(k).start()

    for k in range(cells // BLOCK):
        chunk_copy(k).wait()


def swapped(value, axis, mask):
    return lax.ppermute(value, axis, [(s, s ^ mask) for s in range(lax.axis_size(axis))])


def shards(ensemble, grad_increment, normalization, lon_diffusion, lat_diffusion, vert_diag, vert_sub):
    rows, cols, memb, lev = ensemble.shape
    bands, blocks = lax.axis_size("lat"), lax.axis_size("lon")
    lat_levels, lon_levels = levels_of(bands), levels_of(blocks)
    assert lev == LANES and 8 < rows <= 16 and 8 % memb == 0 and cols <= LANES and cols % CHUNK == 0
    assert 2**lat_levels == bands and 2**lon_levels == blocks and lat_levels >= 2 and lon_levels >= 2
    rest, cells = rows - 8, cols * memb
    assert 8 % rest == 0 and memb * rest % 8 == 0 and cells % PART == 0
    stride = cells + 1
    spaced = -(-(rows + 1) * stride // 8) * 8
    half = memb * rows
    hbm_spec = pl.BlockSpec(memory_space=pltpu.HBM)

    part, phi_t, psi_t, pay = call(
        lon_sweep_kernel,
        (shape(cells, 16, LANES), shape(cols, 16, LANES), shape(cols, 16, LANES), shape(2 * half + 8, LANES)),
        scratch=[
            pltpu.VMEM((cells, 16, LANES), F32),
            pltpu.VMEM((cols, 16, LANES), F32),
            pltpu.VMEM((rows, cols), F32),
            pltpu.VMEM((rows, cols), F32),
            pltpu.VMEM((cols, 16, LANES), F32),
            pltpu.VMEM((cols, 16, LANES), F32),
            pltpu.SemaphoreType.DMA((2 * (cols // CHUNK) + 2,)),
        ],
        in_specs=[hbm_spec] * 4,
        cost=cost(2),
    )(*(in_hbm(x) for x in (ensemble.reshape(rows, cells, lev), grad_increment, normalization, lon_diffusion)))

    own, backs = pay, []
    paired = lat_levels == 2
    spans = lon_rounds(lon_levels)
    for index, span in enumerate(spans):
        others = []
        for k in range(1, 1 << len(span)):
            others.append(swapped(pay, "lon", k << span[0]))
        if index == 0:
            step, lat_phi, lat_psi, coef, small, cosine = call(
                functools.partial(lat_coef_kernel, memb=memb, stride=stride, bands=bands),
                (
                    shape(spaced, LANES),
                    shape(rows * cells, LANES),
                    shape(rows * cells, LANES),
                    shape(3 * cells, LANES),
                    shape(8, LANES),
                    shape(16, LANES),
                ),
                cost=cost(1),
            )(lat_diffusion)
            phi, psi = call(
                functools.partial(expand_kernel, memb=memb, stride=stride, rows=rows),
                (shape(spaced, LANES), shape(spaced, LANES)),
                cost=cost(1),
            )(phi_t, psi_t)
            other_small = swapped(small, "lat", 1)
            others, phi, psi, lat_phi, lat_psi, other_small = lax.optimization_barrier(
                (others, phi, psi, lat_phi, lat_psi, other_small)
            )
        elif index == 1:
            pay, part = lax.optimization_barrier((pay, part))
            y, weights = call(
                functools.partial(vertical_kernel, stride=stride, rows=rows),
                (shape(spaced, LANES), shape(2 * LANES, 2 * LANES, dtype=jnp.bfloat16)),
                scratch=[pltpu.VMEM((8, LANES), F32)] + [pltpu.VMEM((LANES, LANES), F32)] * 3,
                cost=cost(2),
            )(vert_diag.reshape(1, lev), vert_sub.reshape(1, lev - 1), part)
            if paired:
                pair_weight, pair_small = call(
                    functools.partial(lat_pair_kernel, memb=memb),
                    (shape(2 * cells, LANES), shape(8, LANES)),
                    cost=cost(1),
                )(coef, other_small)
                response = call(
                    functools.partial(lat_response_kernel, memb=memb, stride=stride),
                    shape(cells, 2 * LANES, dtype=jnp.bfloat16),
                    cost=cost(1),
                )(step, phi, psi, coef, cosine, pair_weight)
            else:
                response = small
            own_sum = ()
            if paired:
                own_sum = call(
                    functools.partial(lat_own_kernel, stride=stride), shape(cells, LANES), cost=cost(1)
                )(y, step, coef, cosine, pair_weight)
            others, y, weights, own_sum, response = lax.optimization_barrier((others, y, weights, own_sum, response))
        if index < len(spans) - 1:
            pay, *more = call(
                functools.partial(lon_merge_kernel, levels=span, memb=memb, rest=rest),
                (shape(2 * half + 8, LANES),) + (shape(half + 32, LANES),) * len(span),
                cost=cost(1),
            )(pay, *others)
            backs += more
    ends, *sums = call(
        functools.partial(lon_close_kernel, levels=spans[-1], memb=memb, rest=rest),
        (shape(LANES, LANES),) + (shape(cells, LANES),) * paired,
        cost=cost(1),
    )(own, pay, *others, *backs, weights, *(response, own_sum) * paired)

    def sweep(ends):
        return call(
            functools.partial(lat_sweep_kernel, memb=memb, stride=stride),
            (shape(rows * cells, LANES), shape(2 * cells + 8, LANES)),
            scratch=[pltpu.VMEM((16 * rows, LANES), F32)],
            cost=cost(1),
        )(ends, y, phi, psi, step, coef, small, cosine)

    if paired:
        pay = call(lat_add_kernel, shape(cells + 8, LANES), cost=cost(1))(
            sums[0], swapped(sums[0], "lat", 1), pair_small
        )
        final = swapped(pay, "lat", 3)
        behind, _ = lax.optimization_barrier((ends, pay))
        q, lat_pay = sweep(behind)
        inner = swapped(lat_pay, "lat", 1)
        back, group = call(
            functools.partial(lat_merge_kernel, level=0, levels=2, memb=memb, send=False),
            (shape(3 * cells, LANES), shape(2 * cells, LANES)),
            cost=cost(1),
        )(lat_pay, coef, inner)
        lat_backs = [back]
        final, group, back, q = lax.optimization_barrier((final, group, back, q))
    else:
        q, lat_pay = sweep(ends)
        pay, group, lat_backs = lat_pay, coef, []
        for level in range(lat_levels - 1):
            other = swapped(pay, "lat", 1 << level)
            ready = level == lat_levels - 2
            pay, back, group = call(
                functools.partial(lat_merge_kernel, level=level, levels=lat_levels, memb=memb),
                (
                    shape((1 if ready else 2) * cells + 8, LANES),
                    shape(3 * cells, LANES),
                    shape((2 if ready else 3) * cells, LANES),
                ),
                cost=cost(1),
            )(pay, group, other)
            lat_backs.append(back)
        final = swapped(pay, "lat", 1 << (lat_levels - 1) | 1)
    out = call(
        functools.partial(finish_kernel, levels=lat_levels, memb=memb),
        shape(rows, cells, LANES),
        scratch=[
            pltpu.VMEM((rows, cells, LANES), F32),
            pltpu.VMEM((cells, LANES), F32),
            pltpu.SemaphoreType.DMA((cells // BLOCK,)),
        ],
        out_specs=hbm_spec,
        cost=cost(1),
    )(lat_pay, coef, pay, final, group, *lat_backs, q, lat_phi, lat_psi)
    return out.reshape(rows, cols, memb, lev)


def levels_of(count):
    return int(math.log2(count))


def lon_rounds(levels):
    return [tuple(range(k, min(k + 2, levels))) for k in range(0, levels, 2)]


def in_hbm(value):
    return pltpu.with_memory_space_constraint(value, pltpu.HBM)


def cost(microseconds):
    return pl.CostEstimate(flops=0, bytes_accessed=int(microseconds * 3e6), transcendentals=0)


def solution(mesh):
    in_specs = (
        P("lat", "lon", None, None),
        P("lat", "lon", None),
        P("lat", "lon"),
        P("lat", "lon"),
        P("lat", "lon"),
        P(),
        P(),
    )
    out_specs = P("lat", "lon", None, None)
    return jax.shard_map(shards, mesh=mesh, in_specs=in_specs, out_specs=out_specs, check_vma=False)
```

```python
import functools
import math

import jax
import jax.numpy as jnp
from jax import lax
from jax.experimental import pallas as pl
from jax.experimental.pallas import tpu as pltpu
from jax.sharding import PartitionSpec as P


F32 = jnp.float32
LANES = 128
CHUNK = 16
PART = 64
BLOCK = 64
VMEM_BYTES = 16 * 2**20


def call(kernel, outs, scratch=(), in_specs=None, out_specs=None, cost=None):
    specs = {k: v for k, v in (("in_specs", in_specs), ("out_specs", out_specs)) if v is not None}
    return pl.pallas_call(
        kernel,
        out_shape=outs,
        **specs,
        scratch_shapes=scratch,
        cost_estimate=cost,
        compiler_params=pltpu.CompilerParams(vmem_limit_bytes=VMEM_BYTES),
    )


def shape(*dims, dtype=F32):
    return jax.ShapeDtypeStruct(dims, dtype)


def lane_of(value, lane, rows):
    return jnp.broadcast_to(value[:, lane : lane + 1], (rows, LANES))


def split_rows(value):
    rest = value.shape[0] - 8
    fill = jnp.ones((8 - rest, value.shape[1]), F32)
    return value[:8], jnp.concatenate([value[8:], fill], axis=0)


def lon_sweep_kernel(
    ens_hbm,
    grad_hbm,
    norm_hbm,
    diff_hbm,
    part_ref,
    phi_ref,
    psi_ref,
    pay_ref,
    ens,
    grad,
    norm_ref,
    diff_ref,
    step_b,
    norm_b,
    sem,
):
    rows, cells, _ = ens_hbm.shape
    cols = grad_hbm.shape[1]
    memb = cells // cols
    rest = rows - 8
    half = memb * rows
    chunks = cols // CHUNK
    first = pltpu.make_async_copy(diff_hbm, diff_ref, sem.at[2 * chunks])
    second = pltpu.make_async_copy(norm_hbm, norm_ref, sem.at[2 * chunks + 1])
    first.start()
    second.start()
    arrivals = []
    for c in range(chunks):
        g_rows, e_rows = pl.ds(c * CHUNK, CHUNK), pl.ds(c * CHUNK * memb, CHUNK * memb)
        for j in range(rows):
            pltpu.make_async_copy(grad_hbm.at[j, g_rows], grad.at[g_rows, j, :], sem.at[2 * c]).start()
            pltpu.make_async_copy(ens_hbm.at[j, e_rows], ens.at[e_rows, j, :], sem.at[2 * c + 1]).start()
        arrivals.append(
            (
                pltpu.make_async_copy(grad_hbm.at[:, g_rows], grad_hbm.at[:, g_rows], sem.at[2 * c]),
                pltpu.make_async_copy(ens_hbm.at[:, e_rows], ens_hbm.at[:, e_rows], sem.at[2 * c + 1]),
            )
        )
    zero, one = jnp.zeros((8, LANES), F32), jnp.ones((8, LANES), F32)
    tiles = [slice(0, 8), slice(8, 16)]

    first.wait()
    second.wait()
    step = split_rows(1.0 / diff_ref[...])
    norm = split_rows(norm_ref[...])
    phi, phi_f, psi, psi_f = [one] * 2, [zero] * 2, [zero] * 2, [one] * 2
    for i in range(cols):
        for g in range(2):
            t = lane_of(step[g], i, 8)
            step_b[i, tiles[g], :] = t
            norm_b[i, tiles[g], :] = lane_of(norm[g], i, 8)
            phi_ref[i, tiles[g], :] = phi[g]
            psi_ref[i, tiles[g], :] = psi[g]
            phi_f[g] = phi_f[g] + phi[g]
            psi_f[g] = psi_f[g] + psi[g]
            phi[g] = phi[g] + t * phi_f[g]
            psi[g] = psi[g] + t * psi_f[g]
    ends, coefs = [], []
    for g in range(2):
        b = 1.0 / psi[g]
        a, d = phi[g] * b, psi_f[g] * b
        ends.append((b, d))
        coefs.append((a, b, d))
    pay_ref[2 * half :, :] = lon_coef_tile(coefs, rest)

    u = [[zero] * memb for _ in range(2)]
    flux = [[zero] * memb for _ in range(2)]
    for i in range(cols):
        if i % CHUNK == 0:
            for copy in arrivals[i // CHUNK]:
                copy.wait()
        for g in range(2):
            t = step_b[i, tiles[g], :]
            w = norm_b[i, tiles[g], :] * grad[i, tiles[g], :]
            for m in range(memb):
                part_ref[i * memb + m, tiles[g], :] = u[g][m]
                f = w * ens[i * memb + m, tiles[g], :]
                flux[g][m] = flux[g][m] + (u[g][m] - f)
                u[g][m] = u[g][m] + t * flux[g][m]
    for g in range(2):
        b, d = ends[g]
        start = 0 if g == 0 else 8 * memb
        size = 8 if g == 0 else rest
        for m in range(memb):
            at = start + m * size
            pay_ref[at : at + size, :] = (u[g][m] * b)[:size]
            pay_ref[half + at : half + at + size, :] = (flux[g][m] - d * u[g][m])[:size]


def lon_expand(tiles, memb, rest):
    return jnp.concatenate([tiles[:8]] * memb + [tiles[8:]] * (memb * rest // 8), axis=0)


def lon_coef_tile(groups, rest):
    lane = lax.broadcasted_iota(jnp.int32, (8, LANES), 1)
    tile = jnp.zeros((8, LANES), F32)
    for g, group in enumerate(groups):
        for k, value in enumerate(group):
            if g == 1:
                value = jnp.concatenate([value[:rest]] * (8 // rest), axis=0)
            tile = jnp.where(lane == 3 * g + k, value, tile)
    return tile


def lon_parts(pay, half):
    coef = pay[2 * half :]
    coefs = tuple(jnp.concatenate([lane_of(coef, k, 8), lane_of(coef, 3 + k, 8)], axis=0) for k in range(3))
    return (pay[:half], pay[half : 2 * half]) + coefs


def lon_join(mine, other, right, memb, rest):
    lh1, lh2, la, lb, ld = (jnp.where(right, o, m) for m, o in zip(mine, other))
    rh1, rh2, ra, rb, rd = (jnp.where(right, m, o) for m, o in zip(mine, other))
    inv = 1.0 / (ld + ra)
    ca, cb = lb * inv, rb * inv
    grow = functools.partial(lon_expand, memb=memb, rest=rest)
    total = lh2 + rh1
    joined = (lh1 + grow(ca) * total, rh2 + grow(cb) * total, la - lb * ca, lb * cb, rd - rb * cb)
    return joined, (total * grow(inv), ca, cb)


def lon_join_round(pays, levels, memb, rest):
    half = memb * (8 + rest)
    groups = [lon_parts(p[...], half) for p in pays]
    backs = []
    for level in levels:
        right = on_right("lon", level)
        pairs = [lon_join(groups[k], groups[k + 1], right, memb, rest) for k in range(0, len(groups), 2)]
        groups = [joined for joined, _ in pairs]
        backs.append(pairs[0][1])
    return groups[0], backs


def on_right(axis, level):
    return ((lax.axis_index(axis) >> level) & 1) == 1


def lon_merge_kernel(*refs, levels, memb, rest):
    pays, (pay_ref, *back_refs) = refs[: 1 << len(levels)], refs[1 << len(levels) :]
    (h1, h2, a, b, d), backs = lon_join_round(pays, levels, memb, rest)
    half = h1.shape[0]
    pay_ref[:half, :] = h1
    pay_ref[half : 2 * half, :] = h2
    pay_ref[2 * half :, :] = lon_coef_tile([(a[:8], b[:8], d[:8]), (a[8:], b[8:], d[8:])], rest)
    for back_ref, (s, ca, cb) in zip(back_refs, backs):
        back_ref[:half, :] = s
        back_ref[half : half + 16, :] = ca
        back_ref[half + 16 :, :] = cb


def times_inverse(rows, weights):
    high = rows.astype(jnp.bfloat16)
    low = (rows - high.astype(F32)).astype(jnp.bfloat16)
    out = jnp.dot(jnp.concatenate([high, low], axis=1), weights, preferred_element_type=F32)
    return out[:, :LANES] + out[:, LANES:]


def vertical_kernel(diag_ref, sub_ref, part_ref, y_ref, weights_ref, line, ratio, inverse, factor, *, stride, rows):
    levels = diag_ref.shape[1]
    line[...] = jnp.zeros_like(line)
    line[0:1, 0 : levels - 1] = sub_ref[...]
    row_ids = lax.broadcasted_iota(jnp.int32, (levels, levels), 0)
    col_ids = lax.broadcasted_iota(jnp.int32, (levels, levels), 1)
    diag = jnp.sum(jnp.where(row_ids == col_ids, diag_ref[...], 0.0), axis=1, keepdims=True)
    below = jnp.sum(jnp.where(row_ids == col_ids + 1, line[0:1, :], 0.0), axis=1, keepdims=True)
    inv = 1.0 / jnp.broadcast_to(diag, (levels, levels))
    inverse[...] = inv
    ratio[...] = -jnp.broadcast_to(below, (levels, levels)) * inv
    lane = lax.broadcasted_iota(jnp.int32, (1, levels), 1)
    row = jnp.zeros((1, levels), F32)
    for i in range(levels):
        row = jnp.where(lane == i, inverse[i : i + 1, :], row * ratio[i : i + 1, :])
        factor[i : i + 1, :] = row
    low_inv = factor[...]
    full = jnp.dot(low_inv.T, low_inv, preferred_element_type=F32, precision=lax.Precision.HIGHEST)
    high = full.astype(jnp.bfloat16)
    low = (full - high.astype(F32)).astype(jnp.bfloat16)
    weights_ref[0:levels, 0:levels] = high
    weights_ref[0:levels, levels:] = low
    weights_ref[levels:, 0:levels] = high
    weights_ref[levels:, levels:] = jnp.zeros_like(low)
    weights = weights_ref[...]
    cells = part_ref.shape[0]
    for c in range(0, cells, 16):
        y = times_inverse(part_ref[c : c + 16].reshape(256, LANES), weights)
        for k in range(16):
            y_ref[pl.ds(c + k, 8, stride=stride), :] = y[16 * k : 16 * k + 8]
            y_ref[pl.ds(8 * stride + c + k, rows - 8, stride=stride), :] = y[16 * k + 8 : 16 * k + rows]


def spread(out_ref, tiles, i, memb, stride, rows):
    for m in range(memb):
        out_ref[pl.ds(i * memb + m, 8, stride=stride), :] = tiles[0]
        out_ref[pl.ds(8 * stride + i * memb + m, rows - 8, stride=stride), :] = tiles[1][: rows - 8]


def expand_kernel(phi_ref, psi_ref, phi_out, psi_out, *, memb, stride, rows):
    for i in range(phi_ref.shape[0]):
        for src, dst in ((phi_ref, phi_out), (psi_ref, psi_out)):
            spread(dst, (src[i, 0:8, :], src[i, 8:16, :]), i, memb, stride, rows)


def lat_coef_kernel(diff_ref, step_out, phi_out, psi_out, coef_out, small_out, cos_out, *, memb, stride, bands):
    rows, cols = diff_ref.shape
    cells = cols * memb
    band = lax.axis_index("lat")
    row_ids = lax.broadcasted_iota(jnp.int32, (rows, cols), 0)
    last = jnp.logical_and(row_ids == rows - 1, band == bands - 1)
    step = split_rows(jnp.where(last, 0.0, 1.0 / diff_ref[...]))
    for i in range(cols):
        spread(step_out, [lane_of(s, i, 8) for s in step], i, memb, stride, rows)
    tile_ids = lax.broadcasted_iota(jnp.int32, (16, LANES), 0) + band * rows
    cosine = jnp.cos(-jnp.pi / 2 + (tile_ids.astype(F32) + 0.5) * jnp.pi / (bands * rows))
    cos_out[...] = cosine
    acc = [jnp.zeros((8, LANES), F32) for _ in range(3)]
    lane = lax.broadcasted_iota(jnp.int32, (PART, LANES), 1)
    for c in range(0, cells, PART):
        phi = jnp.ones((PART, LANES), F32)
        psi = jnp.zeros((PART, LANES), F32)
        phi_f, psi_f = psi, phi
        for j in range(rows):
            cos_j = jnp.broadcast_to(cosine[j : j + 1, :], (PART, LANES))
            t = step_out[j * stride + c : j * stride + c + PART, :]
            now_phi, now_psi = cos_j * phi, cos_j * psi
            phi_out[j * cells + c : j * cells + c + PART, :] = now_phi
            psi_out[j * cells + c : j * cells + c + PART, :] = now_psi
            phi_f = phi_f + now_phi
            psi_f = psi_f + now_psi
            phi = phi + t * phi_f
            psi = psi + t * psi_f
        b = 1.0 / psi
        picked = lax.broadcasted_iota(jnp.int32, (PART, LANES), 0) + c == lane * memb
        for k, value in enumerate((phi * b, b, psi_f * b)):
            coef_out[k * cells + c : k * cells + c + PART, :] = value
            chosen = jnp.where(picked, value, 0.0)
            for r in range(0, PART, 8):
                acc[k] = acc[k] + chosen[r : r + 8]
    small_out[...] = pack_small([jnp.sum(a, axis=0, keepdims=True) for a in acc])


def pack_small(lines):
    tile = lax.broadcasted_iota(jnp.int32, (8, LANES), 0)
    out = jnp.zeros((8, LANES), F32)
    for k, line in enumerate(lines):
        out = jnp.where(tile == k, jnp.broadcast_to(line, (8, LANES)), out)
    return out


def lon_close_kernel(*refs, levels, memb, rest):
    count = 1 << len(levels)
    own_ref, pays, backs = refs[0], refs[1 : 1 + count], refs[1 + count : 1 + count + levels[0]]
    weights_ref, *refs = refs[1 + count + levels[0] :]
    rows = 8 + rest
    half = memb * rows
    grow = functools.partial(lon_expand, memb=memb, rest=rest)
    (h1, h2, a, b, d), last = lon_join_round(pays, levels, memb, rest)
    u_in = -(h1 + h2) * grow(1.0 / (a + d - 2.0 * b))
    u_out = u_in
    stored = [(back[:half, :], back[half : half + 16, :], back[half + 16 :, :]) for back in backs]
    for level, (s, ca, cb) in reversed(list(enumerate(stored + last))):
        middle = grow(ca) * u_in + grow(cb) * u_out - s
        right = on_right("lon", level)
        u_in, u_out = jnp.where(right, middle, u_in), jnp.where(right, u_out, middle)
    oh1, _, oa, ob, _ = lon_parts(own_ref[...], half)
    f_in = grow(ob) * u_out - grow(oa) * u_in - oh1
    ends = times_inverse(jnp.concatenate([u_in, f_in], axis=0), weights_ref[...])
    full = jnp.concatenate([ends, jnp.zeros((LANES - 2 * half, LANES), F32)], axis=0)
    if len(refs) == 1:
        refs[0][...] = full
        return
    response_ref, part_ref, ends_ref, sum_ref = refs
    ends_ref[...] = full
    high = full.astype(jnp.bfloat16)
    low = (full - high.astype(F32)).astype(jnp.bfloat16)
    table = jnp.concatenate(
        [jnp.concatenate([high, low], axis=1), jnp.concatenate([high, jnp.zeros_like(low)], axis=1)], axis=0
    )
    out = jnp.dot(response_ref[...], table, preferred_element_type=F32)
    sum_ref[...] = part_ref[...] + (out[:, :LANES] + out[:, LANES:])


def lat_sweep_kernel(
    ends, y_ref, phi_ref, psi_ref, step_ref, coef_ref, small_ref, cos_ref, q_ref, pay_ref, tiles, *, memb, stride
):
    rows = step_ref.shape[0] // stride - 1
    rest, half = rows - 8, memb * rows
    for k in range(2):
        for j in range(rows):
            if j < 8:
                value = ends[pl.ds(k * half + j, memb, stride=8), :]
            else:
                value = ends[pl.ds(k * half + 8 * memb + j - 8, memb, stride=rest), :]
            tiles[8 * (k * rows + j) : 8 * (k * rows + j) + 8, :] = jnp.concatenate([value] * (8 // memb), axis=0)
    cells = coef_ref.shape[0] // 3
    for c in range(0, cells, PART):
        v = jnp.zeros((PART, LANES), F32)
        flux = v
        for j in range(rows):
            at = slice(j * stride + c, j * stride + c + PART)
            u_tile = jnp.concatenate([tiles[8 * j : 8 * j + 8, :]] * (PART // 8), axis=0)
            f_tile = jnp.concatenate([tiles[8 * (rows + j) : 8 * (rows + j) + 8, :]] * (PART // 8), axis=0)
            u = y_ref[at, :] + phi_ref[at, :] * u_tile + psi_ref[at, :] * f_tile
            now = jnp.broadcast_to(cos_ref[j : j + 1, :], (PART, LANES)) * v
            q_ref[j * cells + c : j * cells + c + PART, :] = now
            flux = flux + (now - u)
            v = v + step_ref[at, :] * flux
        b = coef_ref[cells + c : cells + c + PART, :]
        d = coef_ref[2 * cells + c : 2 * cells + c + PART, :]
        pay_ref[c : c + PART, :] = v * b
        pay_ref[cells + c : cells + c + PART, :] = flux - d * v
    pay_ref[2 * cells :, :] = small_ref[...]


def unpack_small(tile, k, c, memb):
    row = lax.broadcasted_iota(jnp.int32, (PART, LANES), 0) + c
    lane = lax.broadcasted_iota(jnp.int32, (PART, LANES), 1) * memb
    mask = jnp.logical_and(row >= lane, row < lane + memb)
    line = jnp.broadcast_to(tile[k : k + 1, :], (PART, LANES))
    return jnp.broadcast_to(jnp.sum(jnp.where(mask, line, 0.0), axis=1, keepdims=True), (PART, LANES))


def lat_merge_kernel(mine_ref, coef_ref, other_ref, *outs, level, levels, memb, send=True):
    ready = level == levels - 2
    if not send:
        back_ref, end_ref = outs
    elif ready:
        pay_ref, back_ref, end_ref = outs
    else:
        pay_ref, back_ref, next_ref = outs
    cells = coef_ref.shape[0] // 3
    right = on_right("lat", level)
    upper = on_right("lat", level + 1)
    small = other_ref[2 * cells :, :]
    acc = [jnp.zeros((8, LANES), F32) for _ in range(3)]
    for c in range(0, cells, PART):
        at = slice(c, c + PART)
        lo, mid, hi = (slice(k * cells + c, k * cells + c + PART) for k in range(3))
        mine = [mine_ref[lo, :], mine_ref[mid, :], coef_ref[lo, :], coef_ref[mid, :], coef_ref[hi, :]]
        other = [other_ref[lo, :], other_ref[mid, :]] + [unpack_small(small, k, c, memb) for k in range(3)]
        lh1, lh2, la, lb, ld = (jnp.where(right, o, m) for m, o in zip(mine, other))
        rh1, rh2, ra, rb, rd = (jnp.where(right, m, o) for m, o in zip(mine, other))
        inv = 1.0 / (ld + ra)
        ca, cb = lb * inv, rb * inv
        total = lh2 + rh1
        back_ref[lo, :] = total * inv
        back_ref[mid, :] = ca
        back_ref[hi, :] = cb
        h1, h2 = lh1 + ca * total, rh2 + cb * total
        a, b, d = la - lb * ca, lb * cb, rd - rb * cb
        picked = lax.broadcasted_iota(jnp.int32, (PART, LANES), 0) + c == lax.broadcasted_iota(
            jnp.int32, (PART, LANES), 1
        ) * memb
        if ready:
            free, tied = jnp.where(upper, d, a), jnp.where(upper, a, d)
            h_free, h_tied = jnp.where(upper, h2, h1), jnp.where(upper, h1, h2)
            free_inv = 1.0 / free
            lean = b * free_inv
            end_ref[lo, :] = lean
            end_ref[mid, :] = h_free * free_inv
            if not send:
                continue
            pay_ref[at, :] = h_tied + lean * h_free
            values = (tied - b * lean,)
        else:
            pay_ref[lo, :] = h1
            pay_ref[mid, :] = h2
            values = (a, b, d)
            for k, value in enumerate(values):
                next_ref[k * cells + c : k * cells + c + PART, :] = value
        for k, value in enumerate(values):
            chosen = jnp.where(picked, value, 0.0)
            for r in range(0, PART, 8):
                acc[k] = acc[k] + chosen[r : r + 8]
    if not send:
        return
    lines = [jnp.sum(x, axis=0, keepdims=True) for x in acc[: 1 if ready else 3]]
    pay_ref[cells * (1 if ready else 2) :, :] = pack_small(lines)


def lat_pair_kernel(coef_ref, other_ref, weight_ref, small_ref, *, memb):
    cells = coef_ref.shape[0] // 3
    right, upper = on_right("lat", 0), on_right("lat", 1)
    small = other_ref[...]
    acc = jnp.zeros((8, LANES), F32)
    one = jnp.ones((PART, LANES), F32)
    for c in range(0, cells, PART):
        lo, mid, hi = (slice(k * cells + c, k * cells + c + PART) for k in range(3))
        mine = [coef_ref[lo, :], coef_ref[mid, :], coef_ref[hi, :]]
        other = [unpack_small(small, k, c, memb) for k in range(3)]
        la, lb, ld = (jnp.where(right, o, m) for m, o in zip(mine, other))
        ra, rb, rd = (jnp.where(right, m, o) for m, o in zip(mine, other))
        inv = 1.0 / (ld + ra)
        ca, cb = lb * inv, rb * inv
        a, b, d = la - lb * ca, lb * cb, rd - rb * cb
        free, tied = jnp.where(upper, d, a), jnp.where(upper, a, d)
        lean = b / free
        shared = jnp.where(upper, ca + lean * cb, cb + lean * ca)
        own = jnp.where(right == upper, lean, one)
        weight_ref[lo, :] = jnp.where(right, shared, own)
        weight_ref[mid, :] = jnp.where(right, own, shared)
        acc = pick_small(acc, tied - b * lean, c, memb)
    small_ref[...] = pack_small([jnp.sum(acc, axis=0, keepdims=True)])


def sum_weights(weight_ref, coef_ref, c):
    cells = coef_ref.shape[0] // 3
    e1, e2 = (weight_ref[k * cells + c : k * cells + c + PART, :] for k in range(2))
    b, d = (coef_ref[k * cells + c : k * cells + c + PART, :] for k in (1, 2))
    return e1 * b - e2 * d, e2


def lat_response_kernel(step_ref, phi_ref, psi_ref, coef_ref, cos_ref, weight_ref, out_ref, *, memb, stride):
    cells = coef_ref.shape[0] // 3
    rows = step_ref.shape[0] // stride - 1
    rest, half = rows - 8, memb * rows
    lane = lax.broadcasted_iota(jnp.int32, (8, LANES), 1)
    member = lax.broadcasted_iota(jnp.int32, (8, LANES), 0) % memb
    for c in range(0, cells, PART):
        value, flux = sum_weights(weight_ref, coef_ref, c)
        tiles = [jnp.zeros((8, LANES), F32)] * (PART // 8)
        for j in reversed(range(rows)):
            at = slice(j * stride + c, j * stride + c + PART)
            flux = flux + step_ref[at, :] * value
            value = value + jnp.broadcast_to(cos_ref[j : j + 1, :], (PART, LANES)) * flux
            for end, source in enumerate((phi_ref, psi_ref)):
                first = end * half + (j if j < 8 else 8 * memb + j - 8)
                mask = lane == first + member * (8 if j < 8 else rest)
                entry = flux * source[at, :]
                tiles = [jnp.where(mask, entry[8 * r : 8 * r + 8], tile) for r, tile in enumerate(tiles)]
        full = -jnp.concatenate(tiles, axis=0)
        high = full.astype(jnp.bfloat16)
        out_ref[c : c + PART, :LANES] = high
        out_ref[c : c + PART, LANES:] = (full - high.astype(F32)).astype(jnp.bfloat16)


def lat_own_kernel(y_ref, step_ref, coef_ref, cos_ref, weight_ref, out_ref, *, stride):
    cells = coef_ref.shape[0] // 3
    rows = step_ref.shape[0] // stride - 1
    for c in range(0, cells, PART):
        v = jnp.zeros((PART, LANES), F32)
        flux = v
        for j in range(rows):
            at = slice(j * stride + c, j * stride + c + PART)
            flux = flux + (jnp.broadcast_to(cos_ref[j : j + 1, :], (PART, LANES)) * v - y_ref[at, :])
            v = v + step_ref[at, :] * flux
        of_value, of_flux = sum_weights(weight_ref, coef_ref, c)
        out_ref[c : c + PART, :] = of_value * v + of_flux * flux


def pick_small(acc, value, c, memb):
    row = lax.broadcasted_iota(jnp.int32, (PART, LANES), 0) + c
    chosen = jnp.where(row == lax.broadcasted_iota(jnp.int32, (PART, LANES), 1) * memb, value, 0.0)
    for r in range(0, PART, 8):
        acc = acc + chosen[r : r + 8]
    return acc


def lat_add_kernel(mine_ref, other_ref, small_ref, pay_ref):
    cells = mine_ref.shape[0]
    pay_ref[:cells, :] = mine_ref[...] + other_ref[...]
    pay_ref[cells:, :] = small_ref[...]


def finish_kernel(*refs, levels, memb):
    own_ref, coef_ref, mine_ref, other_ref, end_ref = refs[:5]
    backs = refs[5 : 5 + levels - 1]
    q_ref, phi_ref, psi_ref, out_hbm, out, middles, sem = refs[5 + levels - 1 :]
    cells = coef_ref.shape[0] // 3
    rows = q_ref.shape[0] // cells
    upper = on_right("lat", levels - 1)
    soft = 1.0 / (mine_ref[cells:, :] + other_ref[cells:, :])
    for c in range(0, cells, PART):
        middles[c : c + PART, :] = -(mine_ref[c : c + PART, :] + other_ref[c : c + PART, :]) * unpack_small(
            soft, 0, c, memb
        )

    def chunk_copy(k):
        at = pl.ds(pl.multiple_of(k * BLOCK, BLOCK), BLOCK)
        return pltpu.make_async_copy(out.at[:, at, :], out_hbm.at[:, at, :], sem.at[k])

    @pl.loop(0, cells // BLOCK)
    def _(k):
        c = pl.multiple_of(k * BLOCK, BLOCK)
        lo, mid, hi = (pl.ds(pl.multiple_of(p * cells + c, BLOCK), BLOCK) for p in range(3))
        middle = middles[lo, :]
        outer = end_ref[lo, :] * middle - end_ref[mid, :]
        u_in, u_out = jnp.where(upper, middle, outer), jnp.where(upper, outer, middle)
        for level in reversed(range(levels - 1)):
            back = backs[level]
            middle = back[mid, :] * u_in + back[hi, :] * u_out - back[lo, :]
            right = on_right("lat", level)
            u_in, u_out = jnp.where(right, middle, u_in), jnp.where(right, u_out, middle)
        flux = coef_ref[mid, :] * u_out - coef_ref[lo, :] * u_in - own_ref[lo, :]
        for j in range(rows):
            at = pl.ds(pl.multiple_of(j * cells + c, BLOCK), BLOCK)
            out[j, lo, :] = q_ref[at, :] + phi_ref[at, :] * u_in + psi_ref[at, :] * flux
        chunk_copy(k).start()

    for k in range(cells // BLOCK):
        chunk_copy(k).wait()


def lat_fold_kernel(own_ref, coef_ref, end_ref, back_ref, q_ref, phi_ref, psi_ref, base_ref, gain_ref):
    cells = coef_ref.shape[0] // 3
    rows = q_ref.shape[0] // cells
    right, upper = on_right("lat", 0), on_right("lat", 1)
    for c in range(0, cells, PART):
        lo, mid, hi = (slice(k * cells + c, k * cells + c + PART) for k in range(3))
        one, zero = jnp.ones((PART, LANES), F32), jnp.zeros((PART, LANES), F32)
        inner, outer = (one, zero), (end_ref[lo, :], -end_ref[mid, :])
        u_in = [jnp.where(upper, i, o) for i, o in zip(inner, outer)]
        u_out = [jnp.where(upper, o, i) for i, o in zip(inner, outer)]
        between = [back_ref[mid, :] * i + back_ref[hi, :] * o for i, o in zip(u_in, u_out)]
        between[1] = between[1] - back_ref[lo, :]
        u_in, u_out = (
            [jnp.where(right, b, i) for b, i in zip(between, u_in)],
            [jnp.where(right, o, b) for b, o in zip(between, u_out)],
        )
        flux = [coef_ref[mid, :] * o - coef_ref[lo, :] * i for i, o in zip(u_in, u_out)]
        flux[1] = flux[1] - own_ref[lo, :]
        for j in range(rows):
            at = slice(j * cells + c, j * cells + c + PART)
            gain_ref[at, :] = phi_ref[at, :] * u_in[0] + psi_ref[at, :] * flux[0]
            base_ref[at, :] = q_ref[at, :] + phi_ref[at, :] * u_in[1] + psi_ref[at, :] * flux[1]


def finish_pair_kernel(mine_ref, other_ref, base_ref, gain_ref, out_hbm, out, sem, *, memb):
    cells = mine_ref.shape[0] - 8
    rows = base_ref.shape[0] // cells
    soft = 1.0 / (mine_ref[cells:, :] + other_ref[cells:, :])
    copies = []
    for k, c in enumerate(range(0, cells, PART)):
        lo = slice(c, c + PART)
        middle = -(mine_ref[lo, :] + other_ref[lo, :]) * unpack_small(soft, 0, c, memb)
        for j in range(rows):
            at = slice(j * cells + c, j * cells + c + PART)
            out[j, lo, :] = base_ref[at, :] + gain_ref[at, :] * middle
        block = pl.ds(c, PART)
        copies.append(pltpu.make_async_copy(out.at[:, block, :], out_hbm.at[:, block, :], sem.at[k]))
        copies[-1].start()
    for copy in copies:
        copy.wait()


def swapped(value, axis, mask):
    return lax.ppermute(value, axis, [(s, s ^ mask) for s in range(lax.axis_size(axis))])


def shards(ensemble, grad_increment, normalization, lon_diffusion, lat_diffusion, vert_diag, vert_sub):
    rows, cols, memb, lev = ensemble.shape
    bands, blocks = lax.axis_size("lat"), lax.axis_size("lon")
    lat_levels, lon_levels = levels_of(bands), levels_of(blocks)
    assert lev == LANES and 8 < rows <= 16 and 8 % memb == 0 and cols <= LANES and cols % CHUNK == 0
    assert 2**lat_levels == bands and 2**lon_levels == blocks and lat_levels >= 2 and lon_levels >= 2
    rest, cells = rows - 8, cols * memb
    assert 8 % rest == 0 and memb * rest % 8 == 0 and cells % PART == 0
    stride = cells + 1
    spaced = -(-(rows + 1) * stride // 8) * 8
    half = memb * rows
    hbm_spec = pl.BlockSpec(memory_space=pltpu.HBM)

    part, phi_t, psi_t, pay = call(
        lon_sweep_kernel,
        (shape(cells, 16, LANES), shape(cols, 16, LANES), shape(cols, 16, LANES), shape(2 * half + 8, LANES)),
        scratch=[
            pltpu.VMEM((cells, 16, LANES), F32),
            pltpu.VMEM((cols, 16, LANES), F32),
            pltpu.VMEM((rows, cols), F32),
            pltpu.VMEM((rows, cols), F32),
            pltpu.VMEM((cols, 16, LANES), F32),
            pltpu.VMEM((cols, 16, LANES), F32),
            pltpu.SemaphoreType.DMA((2 * (cols // CHUNK) + 2,)),
        ],
        in_specs=[hbm_spec] * 4,
        cost=cost(2),
    )(*(in_hbm(x) for x in (ensemble.reshape(rows, cells, lev), grad_increment, normalization, lon_diffusion)))

    own, backs = pay, []
    paired = lat_levels == 2
    spans = lon_rounds(lon_levels)
    for index, span in enumerate(spans):
        others = []
        for k in range(1, 1 << len(span)):
            others.append(swapped(pay, "lon", k << span[0]))
        if index == 0:
            step, lat_phi, lat_psi, coef, small, cosine = call(
                functools.partial(lat_coef_kernel, memb=memb, stride=stride, bands=bands),
                (
                    shape(spaced, LANES),
                    shape(rows * cells, LANES),
                    shape(rows * cells, LANES),
                    shape(3 * cells, LANES),
                    shape(8, LANES),
                    shape(16, LANES),
                ),
                cost=cost(1),
            )(lat_diffusion)
            phi, psi = call(
                functools.partial(expand_kernel, memb=memb, stride=stride, rows=rows),
                (shape(spaced, LANES), shape(spaced, LANES)),
                cost=cost(1),
            )(phi_t, psi_t)
            other_small = swapped(small, "lat", 1)
            others, phi, psi, lat_phi, lat_psi, other_small = lax.optimization_barrier(
                (others, phi, psi, lat_phi, lat_psi, other_small)
            )
        elif index == 1:
            pay, part = lax.optimization_barrier((pay, part))
            y, weights = call(
                functools.partial(vertical_kernel, stride=stride, rows=rows),
                (shape(spaced, LANES), shape(2 * LANES, 2 * LANES, dtype=jnp.bfloat16)),
                scratch=[pltpu.VMEM((8, LANES), F32)] + [pltpu.VMEM((LANES, LANES), F32)] * 3,
                cost=cost(2),
            )(vert_diag.reshape(1, lev), vert_sub.reshape(1, lev - 1), part)
            if paired:
                pair_weight, pair_small = call(
                    functools.partial(lat_pair_kernel, memb=memb),
                    (shape(2 * cells, LANES), shape(8, LANES)),
                    cost=cost(1),
                )(coef, other_small)
                response = call(
                    functools.partial(lat_response_kernel, memb=memb, stride=stride),
                    shape(cells, 2 * LANES, dtype=jnp.bfloat16),
                    cost=cost(1),
                )(step, phi, psi, coef, cosine, pair_weight)
            else:
                response = small
            own_sum = ()
            if paired:
                own_sum = call(
                    functools.partial(lat_own_kernel, stride=stride), shape(cells, LANES), cost=cost(1)
                )(y, step, coef, cosine, pair_weight)
            others, y, weights, own_sum, response = lax.optimization_barrier((others, y, weights, own_sum, response))
        if index < len(spans) - 1:
            pay, *more = call(
                functools.partial(lon_merge_kernel, levels=span, memb=memb, rest=rest),
                (shape(2 * half + 8, LANES),) + (shape(half + 32, LANES),) * len(span),
                cost=cost(1),
            )(pay, *others)
            backs += more
    ends, *sums = call(
        functools.partial(lon_close_kernel, levels=spans[-1], memb=memb, rest=rest),
        (shape(LANES, LANES),) + (shape(cells, LANES),) * paired,
        cost=cost(1),
    )(own, pay, *others, *backs, weights, *(response, own_sum) * paired)

    def sweep(ends):
        return call(
            functools.partial(lat_sweep_kernel, memb=memb, stride=stride),
            (shape(rows * cells, LANES), shape(2 * cells + 8, LANES)),
            scratch=[pltpu.VMEM((16 * rows, LANES), F32)],
            cost=cost(1),
        )(ends, y, phi, psi, step, coef, small, cosine)

    if paired:
        pay = call(lat_add_kernel, shape(cells + 8, LANES), cost=cost(1))(
            sums[0], swapped(sums[0], "lat", 1), pair_small
        )
        final = swapped(pay, "lat", 3)
        behind, _ = lax.optimization_barrier((ends, pay))
        q, lat_pay = sweep(behind)
        inner = swapped(lat_pay, "lat", 1)
        back, group = call(
            functools.partial(lat_merge_kernel, level=0, levels=2, memb=memb, send=False),
            (shape(3 * cells, LANES), shape(2 * cells, LANES)),
            cost=cost(1),
        )(lat_pay, coef, inner)
        base, gain = call(
            lat_fold_kernel, (shape(rows * cells, LANES), shape(rows * cells, LANES)), cost=cost(1)
        )(lat_pay, coef, group, back, q, lat_phi, lat_psi)
        final, base, gain = lax.optimization_barrier((final, base, gain))
        out = call(
            functools.partial(finish_pair_kernel, memb=memb),
            shape(rows, cells, LANES),
            scratch=[pltpu.VMEM((rows, cells, LANES), F32), pltpu.SemaphoreType.DMA((cells // PART,))],
            out_specs=hbm_spec,
            cost=cost(1),
        )(pay, final, base, gain)
        return out.reshape(rows, cols, memb, lev)
    else:
        q, lat_pay = sweep(ends)
        pay, group, lat_backs = lat_pay, coef, []
        for level in range(lat_levels - 1):
            other = swapped(pay, "lat", 1 << level)
            ready = level == lat_levels - 2
            pay, back, group = call(
                functools.partial(lat_merge_kernel, level=level, levels=lat_levels, memb=memb),
                (
                    shape((1 if ready else 2) * cells + 8, LANES),
                    shape(3 * cells, LANES),
                    shape((2 if ready else 3) * cells, LANES),
                ),
                cost=cost(1),
            )(pay, group, other)
            lat_backs.append(back)
        final = swapped(pay, "lat", 1 << (lat_levels - 1) | 1)
    out = call(
        functools.partial(finish_kernel, levels=lat_levels, memb=memb),
        shape(rows, cells, LANES),
        scratch=[
            pltpu.VMEM((rows, cells, LANES), F32),
            pltpu.VMEM((cells, LANES), F32),
            pltpu.SemaphoreType.DMA((cells // BLOCK,)),
        ],
        out_specs=hbm_spec,
        cost=cost(1),
    )(lat_pay, coef, pay, final, group, *lat_backs, q, lat_phi, lat_psi)
    return out.reshape(rows, cols, memb, lev)


def levels_of(count):
    return int(math.log2(count))


def lon_rounds(levels):
    return [tuple(range(k, min(k + 2, levels))) for k in range(0, levels, 2)]


def in_hbm(value):
    return pltpu.with_memory_space_constraint(value, pltpu.HBM)


def cost(microseconds):
    return pl.CostEstimate(flops=0, bytes_accessed=int(microseconds * 3e6), transcendentals=0)


def solution(mesh):
    in_specs = (
        P("lat", "lon", None, None),
        P("lat", "lon", None),
        P("lat", "lon"),
        P("lat", "lon"),
        P("lat", "lon"),
        P(),
        P(),
    )
    out_specs = P("lat", "lon", None, None)
    return jax.shard_map(shards, mesh=mesh, in_specs=in_specs, out_specs=out_specs, check_vma=False)
```
